32 devices in a mesh: dp: 8 (over z, y), tensor: 4 (over x, core).
Axes of the slice: x: 2, y: 2, z: 4, core: 2. Of those that a mesh axis runs over, the one named last changes fastest.
Arguments:
- tokens: bfloat16 [32768, 768], P(('dp', 'tensor')), may hold values from -6 to 6
- segment_ids: int32 [16, 2048], P('dp'), may hold values from 0 to 15, never falling along the last dimension, each value on 1 to 1024 neighbouring positions
- qkv_weight: bfloat16 [768, 3, 768], P('dp', None, 'tensor'), may hold values from -0.21875 to 0.21875
- qv_bias: bfloat16 [2, 768], P(None, 'tensor'), may hold values from -2 to 2
- out_weight: bfloat16 [768, 768], P('dp', 'tensor'), may hold values from -0.4375 to 0.4375
- out_bias: bfloat16 [768], replicated, may hold values from -2 to 2
- first_gain: bfloat16 [768], replicated, may hold values from 0.25 to 1.75
- first_shift: bfloat16 [768], replicated, may hold values from -2 to 2
- up_weight: bfloat16 [768, 3072], P('dp', 'tensor'), may hold values from -0.21875 to 0.21875
- up_bias: bfloat16 [3072], P('tensor'), may hold values from -3 to 3
- down_weight: bfloat16 [768, 3072], P('dp', 'tensor'), may hold values from -0.109375 to 0.109375
- down_bias: bfloat16 [768], replicated, may hold values from -2 to 2
- second_gain: bfloat16 [768], replicated, may hold values from 0.25 to 1.75
- second_shift: bfloat16 [768], replicated, may hold values from -2 to 2
- output_grad: bfloat16 [32768, 768], P(('dp', 'tensor')), may hold values from -6 to 6
Outputs:
- output: bfloat16 [32768, 768], P(('dp', 'tensor'))
- input_grad: float32 [32768, 768], P(('dp', 'tensor'))
- qkv_grad: float32 [768, 3, 768], P('dp', None, 'tensor')
- qv_bias_grad: float32 [2, 768], P(None, 'tensor')
- out_weight_grad: float32 [768, 768], P('dp', 'tensor')
- up_weight_grad: float32 [768, 3072], P('dp', 'tensor')
- up_bias_grad: float32 [3072], P('tensor')
- down_weight_grad: float32 [768, 3072], P('dp', 'tensor')
- vector_grads: float32 [6, 768], replicated
The draws below stay inside these ranges and needn't reach their ends.
Inputs may be any that keep to these rules, and one draw needn't show every extreme that they name: `segment_ids`: document ids never fall along a sequence; each document has at most 1024 tokens.
All inputs are finite; a program needn't handle non-finite values.
Results may differ from the reference program's by a relative error of at most 0.015.
Values may be sent and summed in bfloat16 or wider, within the bound.
No kernel may reach another device: no remote copies, remote signals or barrier semaphores. Data moves between devices by JAX's collectives and lax.ppermute only.
A program may use at most 192 MiB of HBM per device.

```python
import math
import jax
import jax.numpy as jnp
import numpy as np
from jax import lax

D = 768
HEADS = 12
HEAD_DIM = 64
FF = 3072
SEQ_LEN = 2048
DOCS = 16
TOK_DEV = 1024
SEQS = 2
TOKENS = 32768
N_DP = 8
N_TENSOR = 4


def block_levels(own_key, shape, cuts, smallest, top_value):
    def one(dim, blocks):
        heights = jax.random.uniform(jax.random.fold_in(jax.random.fold_in(own_key, 6), dim), (blocks,), jnp.float32, smallest / len(cuts), top_value / len(cuts))
        return jnp.repeat(jnp.exp(heights), shape[dim] // blocks).reshape((-1,) + (1,) * (len(shape) - dim - 1))

    level = one(*cuts[0])
    for cut in cuts[1:]:
        level = level * one(*cut)
    return level


def length_profile(count, total, reach, skew):
    weights = [(1 << 20) // math.isqrt(rank ** skew) + 1 for rank in range(2, count + 1)]
    spare, counts = total - reach - (count - 1), [1] * (count - 1)
    while spare > 0:
        candidates = [i for i in range(count - 1) if counts[i] < reach]
        pool, left = sum([weights[i] for i in candidates]), spare
        for i in candidates:
            more = min(reach - counts[i], max(1, left * weights[i] // pool), spare)
            counts[i] = counts[i] + more
            spare = spare - more
    return np.array([reach] + counts)


def uneven_parts(stream_key, number_of, total, most, slope):
    if number_of == 2:
        one = jax.random.randint(stream_key, (), max(1, total - most), min(most, total - 1) + 1)
        return jnp.stack([one, total - one])
    tallies = jnp.asarray(length_profile(number_of, total, most, slope), jnp.int32)
    pairs = (number_of - 1) // 2
    donor, sink = tallies[1:1 + 2 * pairs:2], tallies[2:2 + 2 * pairs:2]
    margin = jnp.minimum(donor - 1, most - sink)
    moved = jax.random.randint(jax.random.fold_in(stream_key, 1), (pairs,), 0, 1 << 20) % (margin + 1)
    tallies = tallies.at[1:1 + 2 * pairs:2].set(donor - moved).at[2:2 + 2 * pairs:2].set(sink + moved)
    return tallies[jax.random.permutation(jax.random.fold_in(stream_key, 2), number_of)]


def centred(stream_key, dims, width, limit, pieces=(), dtype=jnp.bfloat16):
    array = width * jax.random.normal(stream_key, dims, jnp.float32)
    if pieces:
        array = array * block_levels(stream_key, dims, pieces, -0.22, 0.18)
    return jnp.clip(array, -limit, limit).astype(dtype)


def setup_inputs(seed: int = 0) -> dict:
    streams_of = jax.random.split(jax.random.key(seed), 16)
    tokens = centred(streams_of[0], (TOKENS, D), 1.0, 6.0, ((0, 32),))
    segment_ids = jax.vmap(lambda own: jnp.searchsorted(jnp.cumsum(uneven_parts(own, DOCS, SEQ_LEN, SEQ_LEN // 2, 3)), jnp.arange(SEQ_LEN), side="right"))(jax.random.split(streams_of[1], (N_DP * SEQS))).reshape((N_DP * SEQS, SEQ_LEN)).astype(jnp.int32)
    qkv_weight = centred(streams_of[2], (D, 3, D), D ** -0.5, 0.21875, ((0, 8), (2, 4)))
    qv_bias = centred(streams_of[3], (2, D), 0.3, 2.0, ((1, 4),))
    out_weight = centred(streams_of[4], (D, D), (D // 4) ** -0.5, 0.4375, ((0, 8), (1, 4)))
    out_bias = centred(streams_of[5], (D,), 0.3, 2.0)
    first_gain = jnp.clip(1.0 + 0.15 * jax.random.normal(streams_of[6], (D,), jnp.float32), 0.25, 1.75).astype(jnp.bfloat16)
    first_shift = centred(streams_of[7], (D,), 0.3, 2.0)
    up_weight = centred(streams_of[8], (D, FF), D ** -0.5, 0.21875, ((0, 8), (1, 4)))
    up_bias = centred(streams_of[9], (FF,), 0.5, 3.0, ((0, 4),))
    down_weight = centred(streams_of[10], (D, FF), FF ** -0.5, 0.109375, ((0, 8), (1, 4)))
    down_bias = centred(streams_of[11], (D,), 0.3, 2.0)
    second_gain = jnp.clip(1.0 + 0.15 * jax.random.normal(streams_of[12], (D,), jnp.float32), 0.25, 1.75).astype(jnp.bfloat16)
    second_shift = centred(streams_of[13], (D,), 0.3, 2.0)
    output_grad = centred(streams_of[14], (TOKENS, D), 1.0, 6.0, ((0, 32),))
    return dict(tokens=tokens, segment_ids=segment_ids, qkv_weight=qkv_weight, qv_bias=qv_bias, out_weight=out_weight, out_bias=out_bias, first_gain=first_gain, first_shift=first_shift, up_weight=up_weight, up_bias=up_bias, down_weight=down_weight, down_bias=down_bias, second_gain=second_gain, second_shift=second_shift, output_grad=output_grad)


@jax.custom_vjp
def low(v):
    return lax.optimization_barrier(v.astype(jnp.bfloat16)).astype(jnp.float32)

@jax.custom_vjp
def low_back(v):
    return v

def low_keep(v):
    return (low(v), None)

def low_pass(kept, grad):
    return (grad,)

def back_keep(v):
    return (v, None)

def back_low(kept, grad):
    return (low(grad),)
low.defvjp(low_keep, low_pass)
low_back.defvjp(back_keep, back_low)
EPSILON = 1e-12
MASKED = -1e+30
HIGHEST = lax.Precision.HIGHEST

def matmul_full(left, right):
    return jnp.dot(left, right, precision=HIGHEST, preferred_element_type=jnp.float32)

def layer_norm(values, gain, shift):
    center = lax.optimization_barrier(jnp.mean(values, axis=-1, keepdims=True))
    offset = values - center
    spread = lax.optimization_barrier(jnp.mean(offset * offset, axis=-1, keepdims=True))
    return offset * lax.rsqrt(spread + EPSILON) * gain + shift

def attend_rows(query_rows, seg_rows, key_seq, value_seq, seg_seq):
    scores = jnp.einsum('qhd,khd->hqk', query_rows, key_seq, precision=HIGHEST) * HEAD_DIM ** (-0.5)
    scores = low_back(scores)
    same_doc = (seg_rows[:, None] == seg_seq[None, :])[None]
    scores = jnp.where(same_doc, scores, MASKED)
    row_max = lax.optimization_barrier(jnp.max(scores, axis=-1, keepdims=True))
    powers = jnp.exp(scores - row_max)
    probs = low(powers / lax.optimization_barrier(jnp.sum(powers, axis=-1, keepdims=True)))
    return jnp.einsum('hqk,khd->qhd', probs, value_seq, precision=HIGHEST)

def attend_sequence(query_seq, key_seq, value_seq, seg_seq):
    block_rows = min(512, SEQ_LEN)
    block_count = SEQ_LEN // block_rows
    query_blocks = query_seq.reshape(block_count, block_rows, HEADS, HEAD_DIM)
    seg_blocks = seg_seq.reshape(block_count, block_rows)

    def one_block(packed):
        return attend_rows(packed[0], packed[1], key_seq, value_seq, seg_seq)
    context = lax.map(jax.checkpoint(one_block), (query_blocks, seg_blocks))
    return context.reshape(SEQ_LEN, HEADS * HEAD_DIM)

def layer_group(inputs, seg_group, params):
    qkv_weight, qv_bias, out_weight, out_bias, first_gain, first_shift, up_weight, up_bias, down_weight, down_bias, second_gain, second_shift = params
    group_rows = inputs.shape[0]
    sequences = group_rows // SEQ_LEN
    shape_four = (sequences, SEQ_LEN, HEADS, HEAD_DIM)
    queries = low(low_back(matmul_full(inputs, qkv_weight[:, 0, :]) + qv_bias[0])).reshape(shape_four)
    keys_all = low(low_back(matmul_full(inputs, qkv_weight[:, 1, :]))).reshape(shape_four)
    values_all = low(low_back(matmul_full(inputs, qkv_weight[:, 2, :]) + qv_bias[1])).reshape(shape_four)

    def one_sequence(packed):
        return attend_sequence(packed[0], packed[1], packed[2], packed[3])
    context = lax.map(one_sequence, (queries, keys_all, values_all, seg_group))
    context = low(low_back(context.reshape(group_rows, D)))
    attended = low_back(matmul_full(context, out_weight.T) + out_bias)
    first = layer_norm(inputs + attended, first_gain, first_shift)
    hidden_pre = low_back(matmul_full(low(first), up_weight) + up_bias)
    activated = low(jax.nn.gelu(hidden_pre, approximate=False))
    fed = low_back(matmul_full(activated, down_weight.T) + down_bias)
    return layer_norm(first + fed, second_gain, second_shift)

def reference(tokens, segment_ids, qkv_weight, qv_bias, out_weight, out_bias, first_gain, first_shift, up_weight, up_bias, down_weight, down_bias, second_gain, second_shift, output_grad):
    params = tuple((member.astype(jnp.float32) for member in (qkv_weight, qv_bias, out_weight, out_bias, first_gain, first_shift, up_weight, up_bias, down_weight, down_bias, second_gain, second_shift)))
    group_rows = TOK_DEV * N_TENSOR

    def forward(inputs, weights):
        grouped = inputs.reshape(N_DP, group_rows, D)
        seg_groups = segment_ids.reshape(N_DP, group_rows // SEQ_LEN, SEQ_LEN)

        def one_group(packed):
            return layer_group(packed[0], packed[1], weights)
        return lax.map(jax.checkpoint(one_group), (grouped, seg_groups)).reshape(TOKENS, D)
    result, pullback = jax.vjp(forward, tokens.astype(jnp.float32), params)
    input_grad, weight_grads = pullback(output_grad.astype(jnp.float32))
    qkv_grad, qv_grad, out_grad_w, out_bias_g, gain_one_g, shift_one_g, up_grad, up_bias_g, down_grad, down_bias_g, gain_two_g, shift_two_g = weight_grads
    vectors = jnp.stack([out_bias_g, gain_one_g, shift_one_g, down_bias_g, gain_two_g, shift_two_g])
    return (result.astype(jnp.bfloat16), input_grad, qkv_grad, qv_grad, out_grad_w, up_grad, up_bias_g, down_grad, vectors)
```

```python
from functools import partial

import jax
import jax.numpy as jnp
from jax import lax
from jax.experimental import pallas as pl
from jax.experimental.pallas import tpu as pltpu
from jax.sharding import Mesh
from jax.sharding import PartitionSpec as P

HEAD_DIM = 64
PAIR = 2 * HEAD_DIM
EPSILON = 1e-12
MASKED = -1e30
BLOCK = 256
F32 = jnp.float32
BF16 = jnp.bfloat16
VMEM_BYTES = 60 << 20


def dot_nn(left, right):
    return jnp.dot(left, right, preferred_element_type=F32)


def dot_nt(left, right):
    return lax.dot_general(left, right, (((1,), (1,)), ((), ())), preferred_element_type=F32)


def call(body, outs, ins, in_specs=None, out_specs=None, scratch=(), grid=(), flops=0, name=None, alias=None):
    whole = pl.BlockSpec(memory_space=pltpu.VMEM)
    moved = sum(a.size * a.dtype.itemsize for a in ins) + sum(o.size * o.dtype.itemsize for o in outs)
    return pl.pallas_call(
        body,
        grid=grid,
        out_shape=outs,
        in_specs=in_specs or [whole] * len(ins),
        out_specs=out_specs or [whole] * len(outs),
        scratch_shapes=list(scratch),
        compiler_params=pltpu.CompilerParams(vmem_limit_bytes=VMEM_BYTES),
        cost_estimate=pl.CostEstimate(flops=int(flops), bytes_accessed=int(moved), transcendentals=0),
        input_output_aliases=alias or {},
        name=name,
    )(*ins)


ANY = pl.BlockSpec(memory_space=pl.ANY)
SMEM = pl.BlockSpec(memory_space=pltpu.SMEM)
VMEM = pl.BlockSpec(memory_space=pltpu.VMEM)


def shape_of(shape, dtype):
    return jax.ShapeDtypeStruct(shape, dtype)


class Grid:
    def __init__(self, mesh):
        n_dp, n_tensor = mesh.devices.shape
        assert n_tensor == 4 and n_dp % 2 == 0
        self.ny = 2
        self.nz = n_dp // 2
        self.n_dp = n_dp
        self.mesh = Mesh(mesh.devices.reshape(self.nz, 2, 2, 2), ("z", "y", "x", "c"))

    def swap(self, array, axis, r=1):
        size = self.nz if axis == "z" else 2
        return lax.ppermute(array, axis, [(i, i ^ r) for i in range(size)])

    def regular(self, rows):
        return rows % 32 == 0 and self.nz & (self.nz - 1) == 0


class Pieces:
    def __init__(self, arrays, entries):
        self.arrays = arrays
        self.entries = entries


def gather(g, shard, both_ends, order):
    rows = shard.shape[0]
    if not g.regular(rows):
        full = lax.all_gather(shard, ("z", "y"), axis=0, tiled=True)[None, None]
        return Pieces([full, g.swap(full, "x")], [(0, 0, 0, 0, 0, 0, full.shape[2]), (1, 0, 0, 1, 0, 0, full.shape[2])])
    near = [shard] + [g.swap(shard, "z", r) for r in range(1, g.nz)]
    arrays, entries = [], []
    parts = [(0, rows // 2, "x"), (rows // 2, rows // 2, "y")] if both_ends else [(0, rows, order)]
    for first, size, axis in parts:
        line = jnp.stack([part[first : first + size] for part in near])
        other = "y" if axis == "x" else "x"
        two = jnp.stack([line, g.swap(line, axis)])
        four = g.swap(two, other)
        for index, array in ((0, two), (1, four)):
            for i in range(2):
                rx, ry = (i, index) if axis == "x" else (index, i)
                for k in range(g.nz):
                    entries.append((len(arrays), i, k, rx, k * 2 + ry, first, size))
            arrays.append(array)
    return Pieces(arrays, entries)


def across_cores(g, pieces):
    count = len(pieces.arrays)
    return Pieces(
        pieces.arrays + [g.swap(a, "c") for a in pieces.arrays],
        [(a, i, k, r * 2, s, f, n) for a, i, k, r, s, f, n in pieces.entries]
        + [(a + count, i, k, r * 2 + 1, s, f, n) for a, i, k, r, s, f, n in pieces.entries],
    )


def load_pieces(entries, refs, offsets, target, sems):
    slots = 1 + max(entry[4] for entry in entries)
    copies = []
    for number, (a, i, k, place, slot, first, size) in enumerate(entries):
        row = pl.multiple_of((slot ^ offsets) * (target.shape[1] // slots) + first, 16)
        copies.append(
            pltpu.make_async_copy(refs[a].at[i, k], target.at[place, pl.ds(row, size)], sems.at[number])
        )
    for copy in copies:
        copy.start()
    for copy in copies:
        copy.wait()


def scatter_layout(g, rows, lanes, order):
    if not g.regular(rows):
        return shape_of((1, 1, rows * g.n_dp, lanes), BF16)
    return shape_of((2, g.nz, rows, lanes), BF16)


def scatter_sum(g, kept, sent, rows, order):
    if not g.regular(rows):
        both = kept[0, 0].astype(F32) + g.swap(sent, "x")[0, 0].astype(F32)
        return lax.psum_scatter(both, ("z", "y"), scatter_dimension=0, tiled=True)
    other = "y" if order == "x" else "x"
    first = g.swap(sent, order)
    away = (kept[1].astype(F32) + first[1].astype(F32)).astype(BF16)
    second = g.swap(away, other)
    line = kept[0].astype(F32) + first[0].astype(F32) + second.astype(F32)
    total = line[0]
    for r in range(1, g.nz):
        total = total + g.swap(line[r].astype(BF16), "z", r).astype(F32)
    return total


def attention_forward(entries, count, meta, lows, highs, *refs):
    pieces = refs[:count]
    own, other, bias, seg_col, seg_row = refs[count : count + 5]
    (q_out, k_out, v_out, ctx_own, ctx_other, lse, w_out, o_out) = refs[count + 5 : count + 13]
    weights, scores, q_masked, sems = refs[count + 13 :]
    rows = own.shape[0]
    core = meta[0]
    load_pieces(entries, pieces, meta[1], weights, sems)
    d = HEAD_DIM
    first, second = weights[0], weights[1]
    pairs = [
        jnp.concatenate([first[:, n * d : (n + 1) * d], second[:, n * d : (n + 1) * d]], axis=1)
        for n in range(4)
    ]
    joined = jnp.concatenate(pairs[:3], axis=1)
    w_out[...] = joined
    o_out[...] = pairs[3]
    lane = lax.broadcasted_iota(jnp.int32, (BLOCK, PAIR), 1)
    left = lane < d
    for source, base in ((own, core * rows), (other, (1 - core) * rows)):
        for r in range(0, rows, BLOCK):
            acc = dot_nn(source[r : r + BLOCK, :], joined)
            at = pl.ds(pl.multiple_of(base + r, BLOCK), BLOCK)
            q = ((acc[:, :PAIR] + bias[0:1, :]).astype(BF16).astype(F32)) * d**-0.5
            q_out[at, :] = q.astype(BF16)
            q_masked[0, at, :] = jnp.where(left, q, 0.0).astype(BF16)
            q_masked[1, at, :] = jnp.where(left, 0.0, q).astype(BF16)
            k_out[at, :] = acc[:, PAIR : 2 * PAIR].astype(BF16)
            v_out[at, :] = (acc[:, 2 * PAIR :] + bias[1:2, :]).astype(BF16)

    def query_block(i, carry):
        at = pl.ds(pl.multiple_of(i * BLOCK, BLOCK), BLOCK)
        seg_q = seg_col[at, :]
        low, high = lows[i], highs[i]
        queries = [q_masked[h, at, :] for h in range(2)]

        def score_block(b, tops):
            keys = k_out[pl.ds(pl.multiple_of(b * BLOCK, BLOCK), BLOCK), :]
            same = seg_q == seg_row[b]
            new = []
            for h in range(2):
                s = jnp.where(same, dot_nt(queries[h], keys), MASKED)
                scores[h, b] = s
                new.append(jnp.maximum(tops[h], jnp.maximum(s[:, :128], s[:, 128:])))
            return tuple(new)

        low_value = jnp.full((BLOCK, 128), MASKED, F32)
        tops = lax.fori_loop(low, high, score_block, (low_value, low_value))
        tops = [jnp.max(t, axis=1, keepdims=True) for t in tops]

        def value_block(b, carry):
            values = v_out[pl.ds(pl.multiple_of(b * BLOCK, BLOCK), BLOCK), :]
            new = []
            for h in range(2):
                total, acc = carry[2 * h], carry[2 * h + 1]
                p = jnp.exp(scores[h, b] - tops[h])
                new.append(total + (p[:, :128] + p[:, 128:]))
                new.append(acc + dot_nn(p.astype(BF16), values))
            return tuple(new)

        zero = jnp.zeros((BLOCK, 128), F32)
        sums = lax.fori_loop(low, high, value_block, (zero,) * 4)
        totals = [jnp.sum(sums[2 * h], axis=1, keepdims=True) for h in range(2)]
        ctx = jnp.where(left, sums[1] / totals[0], sums[3] / totals[1]).astype(BF16)
        for h in range(2):
            column = jnp.broadcast_to(tops[h] + jnp.log(totals[h]), (BLOCK, 128))
            lse[i, h : h + 1, :] = column.T[0:1, :]
        half = i // (rows // BLOCK)
        place = pl.ds(pl.multiple_of((i - half * (rows // BLOCK)) * BLOCK, BLOCK), BLOCK)

        @pl.when(half == core)
        def _():
            ctx_own[place, :] = ctx

        @pl.when(half != core)
        def _():
            ctx_other[place, :] = ctx

        return carry

    lax.fori_loop(0, 2 * rows // BLOCK, query_block, 0)


def attention_backward(
    meta, lows, highs, own, other, da_own, da_other, q, k, v, ctx_own, ctx_other, lse, w, wo, seg_col, seg_row, ig_own,
    ig_other, keep_out, send_out, ig_own_out, ig_other_out, bias_out, q_masked, d_masked, dq_t, k_t, dqkv, delta, token_t,
    da_t, context,
):
    rows = own.shape[0]
    seq = 2 * rows
    core = meta[0]
    d = HEAD_DIM
    lane = lax.broadcasted_iota(jnp.int32, (BLOCK, PAIR), 1)
    left = lane < d
    weights_o = wo[...]
    for source, values, base in ((da_own, ctx_own, core * rows), (da_other, ctx_other, (1 - core) * rows)):
        for r in range(0, rows, BLOCK):
            at = pl.ds(pl.multiple_of(base + r, BLOCK), BLOCK)
            grad = dot_nn(source[r : r + BLOCK, :], weights_o).astype(BF16).astype(F32)
            d_masked[0, at, :] = jnp.where(left, grad, 0.0).astype(BF16)
            d_masked[1, at, :] = jnp.where(left, 0.0, grad).astype(BF16)
            prod = (grad * values[r : r + BLOCK, :].astype(F32)).T
            block = (base + r) // BLOCK
            delta[block, 0:1, :] = jnp.sum(prod[:d], axis=0, keepdims=True)
            delta[block, 1:2, :] = jnp.sum(prod[d:], axis=0, keepdims=True)
            query = q[at, :].astype(F32)
            q_masked[0, at, :] = jnp.where(left, query, 0.0).astype(BF16)
            q_masked[1, at, :] = jnp.where(left, 0.0, query).astype(BF16)
    for r in range(0, seq, BLOCK):
        k_t[:, r : r + BLOCK] = k[r : r + BLOCK, :].T
    dq_t[...] = jnp.zeros_like(dq_t)

    def key_block(b, carry):
        at = pl.ds(pl.multiple_of(b * BLOCK, BLOCK), BLOCK)
        keys, values = k[at, :], v[at, :]
        keys_t = k_t[:, at]
        seg_k = seg_col[at, :]

        def query_block(i, grads):
            dk, dv = grads
            rows_q = pl.ds(pl.multiple_of(i * BLOCK, BLOCK), BLOCK)
            same = seg_k == seg_row[i]
            for h in range(2):
                queries, grad = q_masked[h, rows_q, :], d_masked[h, rows_q, :]
                s = jnp.where(same, dot_nt(keys, queries), MASKED)
                p = jnp.exp(s - lse[i, h : h + 1, :])
                dp = dot_nt(values, grad)
                ds = (p * (dp - delta[i, h : h + 1, :])).astype(BF16)
                dv = dv + dot_nn(p.astype(BF16), grad)
                dk = dk + dot_nn(ds, queries)
                dq_t[h * d : (h + 1) * d, rows_q] += dot_nn(keys_t[h * d : (h + 1) * d, :], ds)
            return dk, dv

        zero = jnp.zeros((BLOCK, PAIR), F32)
        dk, dv = lax.fori_loop(lows[b], highs[b], query_block, (zero, zero))
        dqkv[at, PAIR : 2 * PAIR] = dk.astype(BF16)
        dqkv[at, 2 * PAIR :] = dv.astype(BF16)
        return carry

    lax.fori_loop(0, seq // BLOCK, key_block, 0)
    for r in range(0, seq, BLOCK):
        dqkv[r : r + BLOCK, :PAIR] = (dq_t[:, r : r + BLOCK].T * d**-0.5).astype(BF16)
    total = jnp.zeros((1, 3 * PAIR), F32)
    for r in range(0, seq, BLOCK):
        total = total + jnp.sum(dqkv[r : r + BLOCK, :].astype(F32), axis=0, keepdims=True)
    bias_out[0:1, :] = total
    weights = w[...]
    for base, before, after in ((core * rows, ig_own, ig_own_out), ((1 - core) * rows, ig_other, ig_other_out)):
        for r in range(0, rows, BLOCK):
            at = pl.ds(pl.multiple_of(base + r, BLOCK), BLOCK)
            grad = dot_nt(dqkv[at, :], weights)
            if before is not None:
                grad = grad + before[r : r + BLOCK, :].astype(F32)
            after[r : r + BLOCK, :] = grad.astype(after.dtype)
    for base, source, grads in ((core * rows, own, da_own), ((1 - core) * rows, other, da_other)):
        for r in range(0, rows, BLOCK):
            at = pl.ds(pl.multiple_of(base + r, BLOCK), BLOCK)
            token_t[:, at] = source[r : r + BLOCK, :].T
            da_t[:, at] = grads[r : r + BLOCK, :].T
    context[pl.ds(pl.multiple_of(core * rows, BLOCK), rows), :] = ctx_own[...]
    context[pl.ds(pl.multiple_of((1 - core) * rows, BLOCK), rows), :] = ctx_other[...]
    part = dot_nn(token_t[...], dqkv[...])
    part_o = dot_nn(da_t[...], context[...])
    kinds = [part[:, n * PAIR : (n + 1) * PAIR] for n in range(3)] + [part_o]
    store_blocks(jnp.concatenate([kind[:, :d] for kind in kinds], axis=1), keep_out, meta[1])
    store_blocks(jnp.concatenate([kind[:, d:] for kind in kinds], axis=1), send_out, meta[1])


def store_blocks(value, target, index, lanes=slice(None)):
    ny, nz, size = target.shape[:3]
    for block in range(value.shape[0] // size):
        slot = block ^ index
        target[lax.rem(slot, ny), lax.div(slot, ny), :, lanes] = value[block * size : (block + 1) * size].astype(BF16)


def normalize(values):
    center = jnp.mean(values, axis=-1, keepdims=True)
    offset = values - center
    inverse = lax.rsqrt(jnp.mean(offset * offset, axis=-1, keepdims=True) + EPSILON)
    return offset * inverse, inverse


def normalize_back(incoming, normed, inverse, gain):
    weighted = incoming * gain
    centered = weighted - jnp.mean(weighted, axis=-1, keepdims=True)
    centered = centered - normed * jnp.mean(weighted * normed, axis=-1, keepdims=True)
    return centered * inverse


def column_sum(values):
    return jnp.sum(values, axis=0, keepdims=True)


def accumulate(target, row, value):
    @pl.when(pl.program_id(0) == 0)
    def _():
        target[row : row + 1, :] = value

    @pl.when(pl.program_id(0) != 0)
    def _():
        target[row : row + 1, :] += value


def project_and_norm(tokens, vectors, *refs):
    contexts, weights = refs[:6], refs[6:12]
    normed_out, inverse_out, low_out, weight, context = refs[12:]

    @pl.when(pl.program_id(0) == 0)
    def _():
        for n in range(6):
            weight[:, n * PAIR : (n + 1) * PAIR] = weights[n][...]

    for n in range(6):
        context[:, n * PAIR : (n + 1) * PAIR] = contexts[n][...]
    mixed = dot_nt(context[...], weight[...])
    normed, inverse = normalize(tokens[...].astype(F32) + mixed + vectors[0:1, :])
    normed_out[...] = normed
    inverse_out[...] = inverse
    low_out[...] = (normed * vectors[1:2, :] + vectors[2:3, :]).astype(BF16)


def hidden_forward(entries, count, meta, *refs):
    pieces = refs[:count]
    low, bias, act_out, slope_out, weight, sems = refs[count:]

    @pl.when(pl.program_id(0) == 0)
    def _():
        load_pieces(entries, pieces, meta[1], weight, sems)

    width = weight.shape[2]
    for t in range(4):
        for n in range(0, width, BLOCK):
            at = slice(t * width + n, t * width + n + BLOCK)
            u = dot_nn(low[...], weight[t, :, n : n + BLOCK]) + bias[:, at]
            share = 0.5 + 0.5 * lax.erf(u * 0.5**0.5)
            act_out[:, at] = (u * share).astype(BF16)
            slope_out[:, at] = (share + u * (jnp.exp(-0.5 * u * u) * 0.3989422804014327)).astype(BF16)


def finish_forward(entries, count, meta, *refs):
    pieces = refs[:count]
    act, slope, normed_one, out_grad, vectors = refs[count : count + 5]
    output, dr2_out, df_out, du_out, sums, bias_sums, weight, sems = refs[count + 5 :]

    @pl.when(pl.program_id(0) == 0)
    def _():
        load_pieces(entries, pieces, meta[1], weight, sems)

    width = weight.shape[2]
    fed = vectors[3:4, :]
    for t in range(4):
        fed = fed + dot_nt(act[:, t * width : (t + 1) * width], weight[t])
    first = normed_one[...] * vectors[1:2, :] + vectors[2:3, :]
    normed, inverse = normalize(first + fed)
    output[...] = (normed * vectors[4:5, :] + vectors[5:6, :]).astype(BF16)
    incoming = out_grad[...].astype(F32)
    dr2 = normalize_back(incoming, normed, inverse, vectors[4:5, :])
    dr2_out[...] = dr2
    df = dr2.astype(BF16)
    df_out[...] = df
    accumulate(sums, 0, column_sum(df.astype(F32)))
    accumulate(sums, 1, column_sum(incoming * normed))
    accumulate(sums, 2, column_sum(incoming))
    parts = []
    for t in range(4):
        for n in range(0, width, BLOCK):
            at = slice(t * width + n, t * width + n + BLOCK)
            du = (dot_nn(df, weight[t, :, n : n + BLOCK]) * slope[:, at].astype(F32)).astype(BF16)
            du_out[:, at] = du
            parts.append(column_sum(du.astype(F32)))
    accumulate(bias_sums, 0, jnp.concatenate(parts, axis=1))


def grad_for_partner(left, right, out, left_t):
    @pl.when(pl.program_id(0) == 0)
    def _():
        left_t[...] = left[...].T

    for n in range(0, right.shape[1], BLOCK):
        out[0, :, n : n + BLOCK] = dot_nn(left_t[...], right[:, n : n + BLOCK]).astype(BF16)


def grad_for_chip(order, meta, left, right, received, keep, send, left_t):
    @pl.when(pl.program_id(0) == 0)
    def _():
        left_t[...] = left[...].T

    for place in range(2):
        @pl.when(pl.program_id(0) == place)
        def _():
            for n in range(0, right.shape[1], BLOCK):
                at = slice(n, n + BLOCK)
                value = dot_nn(left_t[...], right[:, at]) + received[0, :, at].astype(F32)
                if order == "x":
                    store_blocks(value, send if place else keep, meta[1], at)
                else:
                    ny, nz, size = keep.shape[:3]
                    for block in range(value.shape[0] // size):
                        rows = value[block * size : (block + 1) * size].astype(BF16)
                        slot = block ^ meta[1]

                        @pl.when(lax.rem(slot, 2) == 0)
                        def _():
                            keep[place, lax.div(slot, 2), :, at] = rows

                        @pl.when(lax.rem(slot, 2) == 1)
                        def _():
                            send[place, lax.div(slot, 2), :, at] = rows


def first_norm_back(entries, count, meta, *refs):
    pieces = refs[:count]
    du, dr2, normed, inverse, vectors, dr1_out, da_out, sums, weight, sems = refs[count:]

    @pl.when(pl.program_id(0) == 0)
    def _():
        load_pieces(entries, pieces, meta[1], weight, sems)

    width = weight.shape[2]
    incoming = dr2[...]
    for t in range(4):
        incoming = incoming + dot_nt(du[:, t * width : (t + 1) * width], weight[t])
    dr1 = normalize_back(incoming, normed[...], inverse[...], vectors[1:2, :])
    dr1_out[...] = dr1
    da = dr1.astype(BF16)
    da_out[...] = da
    accumulate(sums, 0, column_sum(da.astype(F32)))
    accumulate(sums, 1, column_sum(incoming * normed[...]))
    accumulate(sums, 2, column_sum(incoming))


def local(
    g,
    tokens,
    segment_ids,
    qkv_weight,
    qv_bias,
    out_weight,
    out_bias,
    first_gain,
    first_shift,
    up_weight,
    up_bias,
    down_weight,
    down_bias,
    second_gain,
    second_shift,
    output_grad,
):
    rows, width = tokens.shape
    seq = segment_ids.shape[1]
    heads = qkv_weight.shape[2] // HEAD_DIM
    hidden = up_weight.shape[1]
    shard = qkv_weight.shape[0]
    assert seq == 2 * rows and rows % BLOCK == 0
    d = HEAD_DIM
    z, y, x, c = (lax.axis_index(name) for name in ("z", "y", "x", "c"))
    regular = g.regular(shard)
    meta = jnp.stack([c, (z * 2 + y) if regular else c * 0]).astype(jnp.int32)

    segments = lax.dynamic_index_in_dim(segment_ids, x, 0, keepdims=False)
    blocks = seq // BLOCK
    by_block = segments.reshape(blocks, BLOCK)
    lows = jnp.sum((segments[None, :] < by_block[:, :1]).astype(jnp.int32), axis=1) // BLOCK
    highs = (jnp.sum((segments[None, :] <= by_block[:, -1:]).astype(jnp.int32), axis=1) + BLOCK - 1) // BLOCK
    seg_col = segments.reshape(seq, 1)
    seg_row = segments.reshape(blocks, 1, BLOCK)

    small = jnp.concatenate([up_bias, qv_bias.reshape(-1)]).reshape(1, -1)
    small = jnp.concatenate([small, g.swap(small, "c")], axis=0)
    small = jnp.concatenate([small, g.swap(small, "x")], axis=0).astype(F32)
    hidden_bias = small[:, :hidden].reshape(1, 4 * hidden)
    pair_bias = small[:, hidden:].reshape(2, 2, 2, heads, d)[:, 0]
    vectors = jnp.stack(
        [out_bias, first_gain, first_shift, down_bias, second_gain, second_shift, out_bias, out_bias]
    ).astype(F32)

    other_tokens = g.swap(tokens, "c")
    head_pieces = []
    for j in range(heads):
        at = slice(j * d, (j + 1) * d)
        chunk = jnp.concatenate(
            [qkv_weight[:, 0, at], qkv_weight[:, 1, at], qkv_weight[:, 2, at], out_weight[:, at]], axis=1
        )
        head_pieces.append(gather(g, chunk, True, "x"))
    up_pieces = across_cores(g, gather(g, up_weight, True, "x"))
    down_pieces = across_cores(g, gather(g, down_weight, True, "x"))

    saved = []
    for j in range(heads):
        pieces = head_pieces[j]
        count = len(pieces.arrays)
        bias = jnp.concatenate([pair_bias[0, :, j], pair_bias[1, :, j]], axis=1)
        ins = [meta, lows, highs, *pieces.arrays, tokens, other_tokens, bias, seg_col, seg_row]
        outs = [shape_of((seq, PAIR), BF16)] * 3 + [shape_of((rows, PAIR), BF16)] * 2
        outs += [shape_of((blocks, 8, BLOCK), F32), shape_of((width, 3 * PAIR), BF16), shape_of((width, PAIR), BF16)]
        saved.append(
            call(
                partial(attention_forward, pieces.entries, count),
                outs,
                ins,
                in_specs=[SMEM] * 3 + [ANY] * count + [VMEM] * 5,
                scratch=[
                    pltpu.VMEM((2, width, 4 * d), BF16),
                    pltpu.VMEM((2, blocks, BLOCK, BLOCK), F32),
                    pltpu.VMEM((2, seq, PAIR), BF16),
                    pltpu.SemaphoreType.DMA((len(pieces.entries),)),
                ],
                flops=2 * seq * width * 3 * PAIR + 8 * seq * seq * PAIR,
                name="attention_forward",
            )
        )
    contexts = [s[3] for s in saved] + [g.swap(s[4], "c") for s in saved]
    out_weights = [s[7] for s in saved] + [g.swap(s[7], "c") for s in saved]

    steps = (rows // BLOCK,)

    def by_rows(lanes):
        return pl.BlockSpec((BLOCK, lanes), lambda i: (i, 0))

    def fixed(array):
        return pl.BlockSpec(array.shape, lambda i: (0,) * len(array.shape))

    normed_one, inverse_one, first_low = call(
        project_and_norm,
        [shape_of((rows, width), F32), shape_of((rows, 1), F32), shape_of((rows, width), BF16)],
        [tokens, vectors, *contexts, *out_weights],
        in_specs=[by_rows(width), fixed(vectors)] + [by_rows(PAIR)] * 6 + [fixed(out_weights[0])] * 6,
        out_specs=[by_rows(width), by_rows(1), by_rows(width)],
        scratch=[pltpu.VMEM((width, width), BF16), pltpu.VMEM((BLOCK, width), BF16)],
        grid=steps,
        flops=2 * rows * width * width,
        name="project_and_norm",
    )
    ffn = 2 * rows * width * 4 * hidden
    weight_scratch = pltpu.VMEM((4, width, hidden), BF16)

    count = len(up_pieces.arrays)
    activated, slope = call(
        partial(hidden_forward, up_pieces.entries, count),
        [shape_of((rows, 4 * hidden), BF16)] * 2,
        [meta, *up_pieces.arrays, first_low, hidden_bias],
        in_specs=[SMEM] + [ANY] * count + [by_rows(width), fixed(hidden_bias)],
        out_specs=[by_rows(4 * hidden)] * 2,
        scratch=[weight_scratch, pltpu.SemaphoreType.DMA((len(up_pieces.entries),))],
        grid=steps,
        flops=ffn,
        name="hidden_forward",
    )
    sums_shape = shape_of((8, width), F32)
    bias_shape = shape_of((8, 4 * hidden), F32)
    output, dr2, df, du, sums_two, hidden_sums = call(
        partial(finish_forward, down_pieces.entries, len(down_pieces.arrays)),
        [
            shape_of((rows, width), BF16),
            shape_of((rows, width), F32),
            shape_of((rows, width), BF16),
            shape_of((rows, 4 * hidden), BF16),
            sums_shape,
            bias_shape,
        ],
        [meta, *down_pieces.arrays, activated, slope, normed_one, output_grad, vectors],
        in_specs=[SMEM]
        + [ANY] * len(down_pieces.arrays)
        + [by_rows(4 * hidden)] * 2
        + [by_rows(width)] * 2
        + [fixed(vectors)],
        out_specs=[by_rows(width)] * 3 + [by_rows(4 * hidden), fixed(sums_shape), fixed(bias_shape)],
        scratch=[weight_scratch, pltpu.SemaphoreType.DMA((len(down_pieces.entries),))],
        grid=steps,
        flops=2 * ffn,
        name="finish_forward",
    )

    def weight_grad(left, right, order):
        outs = [shape_of((2, width, hidden), BF16)]
        whole_left = pl.BlockSpec((rows, width), lambda i: (0, 0))
        by_place = pl.BlockSpec((1, width, hidden), lambda i: (i, 0, 0))
        (for_partner,) = call(
            grad_for_partner,
            outs,
            [left, right],
            in_specs=[whole_left, pl.BlockSpec((rows, hidden), lambda i: (0, 2 * i + 1))],
            out_specs=[by_place],
            scratch=[pltpu.VMEM((width, rows), BF16)],
            grid=(2,),
            flops=ffn // 2,
            name="grad_for_partner",
        )
        received = g.swap(for_partner, "c")
        leaving = scatter_layout(g, shard, hidden, order)
        keep, send = call(
            partial(grad_for_chip, order),
            [leaving] * 2,
            [meta, left, right, received],
            in_specs=[SMEM, whole_left, pl.BlockSpec((rows, hidden), lambda i: (0, 2 * i)), by_place],
            out_specs=[fixed(leaving)] * 2,
            scratch=[pltpu.VMEM((width, rows), BF16)],
            grid=(2,),
            flops=ffn // 2,
            name="grad_for_chip",
        )
        return scatter_sum(g, keep, send, shard, order)

    down_order, up_order = ("x", "y") if regular else ("x", "x")
    down_share = weight_grad(df, activated, down_order)
    up_share = weight_grad(first_low, du, up_order)

    dr1, da, sums_one = call(
        partial(first_norm_back, up_pieces.entries, count),
        [shape_of((rows, width), F32), shape_of((rows, width), BF16), sums_shape],
        [meta, *up_pieces.arrays, du, dr2, normed_one, inverse_one, vectors],
        in_specs=[SMEM] + [ANY] * count + [by_rows(4 * hidden), by_rows(width), by_rows(width), by_rows(1), fixed(vectors)],
        out_specs=[by_rows(width)] * 2 + [fixed(sums_shape)],
        scratch=[weight_scratch, pltpu.SemaphoreType.DMA((len(up_pieces.entries),))],
        grid=steps,
        flops=ffn,
        name="first_norm_back",
    )
    other_da = g.swap(da, "c")

    head_shares, bias_sums = [], []
    ig_own = ig_other = None
    for j in range(heads):
        q, k, v, ctx_own, ctx_other, lse, w, wo = saved[j]
        last = j == heads - 1
        leaving = scatter_layout(g, shard, 4 * d, "x")
        ins = [meta, lows, highs, tokens, other_tokens, da, other_da, q, k, v, ctx_own, ctx_other, lse, w, wo, seg_col, seg_row]
        body = partial(first_pair, attention_backward) if ig_own is None else attention_backward
        if ig_own is not None:
            ins += [ig_own, ig_other]
        keep, send, ig_own, ig_other, sums = call(
            body,
            [
                leaving,
                leaving,
                shape_of((rows, width), F32),
                shape_of((rows, width), BF16 if last else F32),
                shape_of((8, 3 * PAIR), F32),
            ],
            ins,
            in_specs=[SMEM] * 3 + [VMEM] * (len(ins) - 3),
            scratch=[
                pltpu.VMEM((2, seq, PAIR), BF16),
                pltpu.VMEM((2, seq, PAIR), BF16),
                pltpu.VMEM((PAIR, seq), F32),
                pltpu.VMEM((PAIR, seq), BF16),
                pltpu.VMEM((seq, 3 * PAIR), BF16),
                pltpu.VMEM((blocks, 8, BLOCK), F32),
                pltpu.VMEM((width, seq), BF16),
                pltpu.VMEM((width, seq), BF16),
                pltpu.VMEM((seq, PAIR), BF16),
            ],
            flops=2 * seq * width * 9 * PAIR + 20 * seq * seq * PAIR,
            name="attention_backward",
        )
        head_shares.append(scatter_sum(g, keep, send, shard, "x"))
        bias_sums.append(sums[0].reshape(3, 2, d))
    input_grad = dr1 + ig_own + g.swap(ig_other, "c").astype(F32)

    me = x * 2 + c
    places = jnp.arange(4, dtype=jnp.int32) ^ me
    hidden_abs = hidden_sums[0].reshape(4, hidden)[places]
    pair_sums = jnp.stack(bias_sums)
    kinds = jnp.stack([pair_sums[:, 0], pair_sums[:, 2]])
    kinds = kinds.transpose(2, 0, 1, 3).reshape(2, 2 * heads * d)
    owned = jnp.zeros((4, 2 * heads * d), F32)
    owned = lax.dynamic_update_slice(owned, kinds[0:1], (me, 0))
    owned = lax.dynamic_update_slice(owned, kinds[1:2], (me ^ 2, 0))
    six = jnp.stack([sums_one[0], sums_one[1], sums_one[2], sums_two[0], sums_two[1], sums_two[2]])
    summed = lax.psum(jnp.concatenate([six.reshape(-1), hidden_abs.reshape(-1), owned.reshape(-1)]), ("z", "y", "x", "c"))
    vectors_grad = summed[: 6 * width].reshape(6, width)
    hidden_all = summed[6 * width : 6 * width + 4 * hidden].reshape(4, hidden)
    owned_all = summed[6 * width + 4 * hidden :].reshape(4, 2, heads * d)
    up_bias_share = lax.dynamic_index_in_dim(hidden_all, me, 0, keepdims=False)
    qv_share = lax.dynamic_index_in_dim(owned_all, me, 0, keepdims=False)

    qkv_share = jnp.stack(
        [jnp.concatenate([h[:, n * d : (n + 1) * d] for h in head_shares], axis=1) for n in range(3)], axis=1
    )
    out_share = jnp.concatenate([h[:, 3 * d :] for h in head_shares], axis=1)
    return (output, input_grad, qkv_share, qv_share, out_share, up_share, up_bias_share, down_share, vectors_grad)


def first_pair(body, *refs):
    body(*refs[:17], None, None, *refs[17:])


def solution(mesh):
    g = Grid(mesh)
    dp, tensor = ("z", "y"), ("x", "c")
    rows = P(dp + tensor, None)
    in_specs = (
        rows,
        P(dp, None),
        P(dp, None, tensor),
        P(None, tensor),
        P(dp, tensor),
        P(),
        P(),
        P(),
        P(dp, tensor),
        P(tensor),
        P(dp, tensor),
        P(),
        P(),
        P(),
        rows,
    )
    out_specs = (
        rows,
        rows,
        P(dp, None, tensor),
        P(None, tensor),
        P(dp, tensor),
        P(dp, tensor),
        P(tensor),
        P(dp, tensor),
        P(),
    )
    return jax.shard_map(partial(local, g), mesh=g.mesh, in_specs=in_specs, out_specs=out_specs, check_vma=False)
```

```python
from functools import partial

import jax
import jax.numpy as jnp
from jax import lax
from jax.experimental import pallas as pl
from jax.experimental.pallas import tpu as pltpu
from jax.sharding import Mesh
from jax.sharding import PartitionSpec as P

HEAD_DIM = 64
PAIR = 2 * HEAD_DIM
EPSILON = 1e-12
MASKED = -1e30
BLOCK = 256
F32 = jnp.float32
BF16 = jnp.bfloat16
MIB = 1 << 20


def dot_nn(left, right):
    return jnp.dot(left, right, preferred_element_type=F32)


def dot_nt(left, right):
    return lax.dot_general(left, right, (((1,), (1,)), ((), ())), preferred_element_type=F32)


def call(body, outs, ins, in_specs=None, out_specs=None, scratch=(), grid=(), flops=0, name=None, vmem=60, alias=None):
    moved = sum(a.size * a.dtype.itemsize for a in ins) + sum(o.size * o.dtype.itemsize for o in outs)
    return pl.pallas_call(
        body,
        grid=grid,
        out_shape=outs,
        in_specs=in_specs or [VMEM] * len(ins),
        out_specs=out_specs or [VMEM] * len(outs),
        scratch_shapes=list(scratch),
        compiler_params=pltpu.CompilerParams(vmem_limit_bytes=vmem * MIB),
        cost_estimate=pl.CostEstimate(flops=int(flops), bytes_accessed=int(moved), transcendentals=0),
        input_output_aliases=alias or {},
        name=name,
    )(*ins)


ANY = pl.BlockSpec(memory_space=pl.ANY)
SMEM = pl.BlockSpec(memory_space=pltpu.SMEM)
VMEM = pl.BlockSpec(memory_space=pltpu.VMEM)


def shape_of(shape, dtype):
    return jax.ShapeDtypeStruct(shape, dtype)


def after(values, done):
    return lax.optimization_barrier((values, done))[0]


class Grid:
    def __init__(self, mesh):
        n_dp, n_tensor = mesh.devices.shape
        assert n_tensor == 4 and n_dp % 2 == 0
        self.nz = n_dp // 2
        self.n_dp = n_dp
        self.mesh = Mesh(mesh.devices.reshape(self.nz, 2, 2, 2), ("z", "y", "x", "c"))

    def swap(self, array, axis, r=1):
        size = self.nz if axis == "z" else 2
        return lax.ppermute(array, axis, [(i, i ^ r) for i in range(size)])

    def regular(self, rows):
        return rows % 32 == 0 and self.nz & (self.nz - 1) == 0

    def total_dp(self, array):
        if self.nz & (self.nz - 1):
            return lax.psum(array, ("z", "y"))
        array = array + self.swap(array, "y")
        r = 1
        while r < self.nz:
            array = array + self.swap(array, "z", r)
            r *= 2
        return array


class Gather:
    def __init__(self, g, shard):
        self.g, self.shard, self.rows = g, shard, shard.shape[0]
        self.regular = g.regular(self.rows)

    def line(self):
        g, half = self.g, self.rows // 2
        if not self.regular:
            full = lax.all_gather(self.shard, ("z", "y"), axis=0, tiled=True)[None, None]
            self.arrays = [full, g.swap(full, "x")]
            self.entries = [(n, 0, 0, n, 0, 0, full.shape[2]) for n in range(2)]
            return self.arrays
        near = [self.shard] + [g.swap(self.shard, "z", r) for r in range(1, g.nz)]
        self.lines = [jnp.stack([part[:half] for part in near]), jnp.stack([part[half:] for part in near])]
        return self.lines

    def wait(self, step, done):
        if self.regular:
            setattr(self, step, after(getattr(self, step), done))

    def first(self, done=()):
        if not self.regular:
            return self.arrays
        arrived = after([self.g.swap(line, axis) for line, axis in zip(self.lines, "xy")], done)
        self.twos = [jnp.stack([line, other]) for line, other in zip(self.lines, arrived)]
        return arrived

    def second(self):
        if not self.regular:
            return self.arrays
        half = self.rows // 2
        self.arrays, self.entries = [], []
        for number, axis in enumerate("xy"):
            two = self.twos[number]
            four = self.g.swap(two, "yx"[number])
            for index, array in ((0, two), (1, four)):
                for i in range(2):
                    rx, ry = (i, index) if axis == "x" else (index, i)
                    for k in range(self.g.nz):
                        self.entries.append((len(self.arrays), i, k, rx, k * 2 + ry, number * half, half))
                self.arrays.append(array)
        return self.arrays


def load_pieces(entries, refs, index, target, sems, lanes):
    slots = 1 + max(entry[4] for entry in entries)
    copies = []
    for number, (a, i, k, place, slot, first, size) in enumerate(entries):
        row = pl.multiple_of((slot ^ index) * (target.shape[1] // slots) + first, 16)
        copies.append(
            pltpu.make_async_copy(refs[a].at[i, k, :, lanes], target.at[place, pl.ds(row, size)], sems.at[number])
        )
    for copy in copies:
        copy.start()
    for copy in copies:
        copy.wait()


def gather_everywhere(g, shard):
    if g.regular(shard.shape[0]):
        full = lax.all_gather(shard, ("z", "y", "x", "c"), axis=0)
        return full.reshape(g.n_dp, 4, *shard.shape)
    full = lax.all_gather(shard, ("z", "y"), axis=0, tiled=True)
    return lax.all_gather(full, ("x", "c"), axis=0)[None]


def everywhere_copies(source, me, target, sems, lanes):
    blocks, places, rows = source.shape[:3]
    return [
        pltpu.make_async_copy(
            source.at[block, t, :, lanes],
            target.at[t ^ me, pl.ds(block * rows, rows)],
            sems.at[block * places + t],
        )
        for block in range(blocks)
        for t in range(places)
    ]


class Scatter:
    def __init__(self, g, rows, arrays):
        self.g, self.rows = g, rows
        self.regular = g.regular(rows)
        self.arrays = arrays

    @staticmethod
    def shapes(g, rows, lanes):
        if not g.regular(rows):
            return [shape_of((2, rows * g.n_dp, lanes), BF16)]
        return [shape_of((2, g.nz, rows // 2, lanes), BF16)] * 4

    def first(self, done=()):
        g = self.g
        if not self.regular:
            (whole,) = self.arrays
            both = whole[0].astype(F32) + g.swap(whole[1], "x").astype(F32)
            self.sum = lax.psum_scatter(both, ("z", "y"), scatter_dimension=0, tiled=True)
            return [self.sum]
        keep_x, send_x, keep_y, send_y = self.arrays
        self.got = after([g.swap(send_x, "x"), g.swap(send_y, "y")], done)
        shape = shape_of(keep_x.shape[1:], BF16)
        self.away = call(
            sum_away, [shape] * 2, [keep_x, self.got[0], keep_y, self.got[1]], name="sum_away", vmem=SUM_VMEM
        )
        return self.away

    def wait(self, step, done):
        if self.regular:
            setattr(self, step, after(getattr(self, step), done))

    def second(self, done=()):
        if not self.regular:
            return [self.sum]
        g = self.g
        seconds = after([g.swap(self.away[0], "y"), g.swap(self.away[1], "x")], done)
        half, lanes = self.away[0].shape[1:]
        self.near, *self.far = call(
            sum_line,
            [shape_of((2, half, lanes), F32)] + [shape_of((2, half, lanes), BF16)] * (g.nz - 1),
            [self.arrays[0], self.got[0], seconds[0], self.arrays[2], self.got[1], seconds[1]],
            name="sum_line",
            vmem=SUM_VMEM,
        )
        return [self.near, *self.far]

    def third(self, done=()):
        if not self.regular:
            return self.sum
        total = self.near
        for arrived in after([self.g.swap(far, "z", r + 1) for r, far in enumerate(self.far)], done):
            total = total + arrived.astype(F32)
        return total.reshape(self.rows, total.shape[-1])


SUM_VMEM = 12
VM_HEADS = 40
VM_ROWS = 48
VM_GRAD = 24
VM_BACK = 50
VM_PROJ = 36


def sum_away(keep_x, got_x, keep_y, got_y, out_x, out_y):
    for keep, got, out in ((keep_x, got_x, out_x), (keep_y, got_y, out_y)):
        out[...] = (keep[1].astype(F32) + got[1].astype(F32)).astype(BF16)


def sum_line(keep_x, got_x, last_x, keep_y, got_y, last_y, near, *far):
    for n, (keep, got, last) in enumerate(((keep_x, got_x, last_x), (keep_y, got_y, last_y))):
        for r in range(1 + len(far)):
            total = keep[0, r].astype(F32) + got[0, r].astype(F32) + last[r].astype(F32)
            if r:
                far[r - 1][n] = total.astype(BF16)
            else:
                near[n] = total


def store_blocks(value, outs, place, index, lanes=slice(None)):
    value = value.astype(BF16)
    if len(outs) == 1:
        outs[0][place, :, lanes] = value
        return
    by_x, by_y = outs[place], outs[2:]
    half = by_x.shape[2]
    blocks = value.shape[0] // (2 * half)
    for block in range(blocks):
        slot = block ^ index
        by_x[lax.rem(slot, 2), lax.div(slot, 2), :, lanes] = value[2 * block * half : (2 * block + 1) * half]
    for odd in range(2):

        @pl.when(lax.rem(index, 2) == odd)
        def _():
            for block in range(blocks):
                rows = value[(2 * block + 1) * half : (2 * block + 2) * half]
                by_y[(block + odd) % 2][place, lax.div(block ^ index, 2), :, lanes] = rows


SUMMED = HEAD_DIM + 16


def heads_forward(entries, count, meta, lows, highs, *refs):
    pieces = refs[:count]
    own, other, bias, seg_col, seg_row = refs[count : count + 5]
    q, k, v, w_out, wo_out, ctx_own, ctx_other, lse = refs[count + 5 : count + 13]
    weights, v_t, q_masked, powers, sems = refs[count + 13 :]
    rows = own.shape[0]
    core = meta[0]
    load_pieces(entries, pieces, meta[1], weights, sems, slice(None))
    d = HEAD_DIM
    width = q.shape[1]
    pairs = width // PAIR
    for j in range(pairs):
        for kind in range(4):
            at = slice((4 * j + kind) * d, (4 * j + kind + 1) * d)
            pair = jnp.concatenate([weights[0][:, at], weights[1][:, at]], axis=1)
            lanes = slice(j * PAIR, (j + 1) * PAIR)
            if kind == 3:
                wo_out[:, lanes] = pair
            else:
                w_out[:, kind * width + j * PAIR : kind * width + (j + 1) * PAIR] = pair
    ones = jnp.ones((SUMMED - d, BLOCK), BF16)
    for source, base in ((own, core * rows), (other, (1 - core) * rows)):

        def project(n, carry):
            at = pl.ds(pl.multiple_of(base + n * BLOCK, BLOCK), BLOCK)
            block = source[pl.ds(pl.multiple_of(n * BLOCK, BLOCK), BLOCK), :]
            all_three = dot_nn(block, w_out[...])
            query = (all_three[:, :width] + bias[0:1, :]).astype(BF16)
            q[at, :] = (query.astype(F32) * d**-0.5).astype(BF16)
            k[at, :] = all_three[:, width : 2 * width].astype(BF16)
            values = (all_three[:, 2 * width :] + bias[1:2, :]).astype(BF16)
            v[at, :] = values
            for p in range(pairs):
                columns = values[:, p * PAIR : (p + 1) * PAIR].T
                for h in range(2):
                    v_t[2 * p + h, :d, at] = columns[h * d : (h + 1) * d]
                    v_t[2 * p + h, d:, at] = ones
            return carry

        lax.fori_loop(0, rows // BLOCK, project, 0)
    left = lax.broadcasted_iota(jnp.int32, (BLOCK, PAIR), 1) < d
    half = rows // BLOCK

    def query_block(i, carry):
        at = pl.ds(pl.multiple_of(i * BLOCK, BLOCK), BLOCK)
        seg_q = seg_row[i]
        for p in range(pairs):
            query = q[at, p * PAIR : (p + 1) * PAIR].astype(F32)
            q_masked[2 * p] = jnp.where(left, query, 0.0).astype(BF16)
            q_masked[2 * p + 1] = jnp.where(left, 0.0, query).astype(BF16)

        def key_block(b, carry):
            tops, sums = carry
            rows = pl.ds(pl.multiple_of(b * BLOCK, BLOCK), BLOCK)
            same = seg_col[rows, :] == seg_q
            new_tops, new_sums = [], []
            for h in range(2 * pairs):
                s = dot_nt(k[rows, (h // 2) * PAIR : (h // 2 + 1) * PAIR], q_masked[h])
                s = jnp.where(same, s, MASKED)
                top = jnp.maximum(tops[h], jnp.max(s, axis=0, keepdims=True))
                powers[h] = jnp.exp(s - top).astype(BF16)
                new_tops.append(top)
            for h in range(2 * pairs):
                scale = jnp.exp(tops[h] - new_tops[h])
                new_sums.append(sums[h] * scale + dot_nn(v_t[h, :, rows], powers[h]))
            return tuple(new_tops), tuple(new_sums)

        first_top = jnp.full((1, BLOCK), MASKED, F32)
        first_sum = jnp.zeros((SUMMED, BLOCK), F32)
        tops, sums = lax.fori_loop(
            lows[i], highs[i], key_block, ((first_top,) * (2 * pairs), (first_sum,) * (2 * pairs))
        )
        for p in range(pairs):
            parts = []
            for h in (2 * p, 2 * p + 1):
                total = sums[h][d : d + 1, :]
                lse[i, h : h + 1, :] = tops[h] + jnp.log(total)
                parts.append(sums[h][:d, :] / total)
            ctx = jnp.concatenate(parts, axis=0).T.astype(BF16)
            lanes = slice(p * PAIR, (p + 1) * PAIR)
            own_half = lax.div(i, half) == core
            within = pl.ds(pl.multiple_of(lax.rem(i, half) * BLOCK, BLOCK), BLOCK)

            @pl.when(own_half)
            def _():
                ctx_own[within, lanes] = ctx

            @pl.when(jnp.logical_not(own_half))
            def _():
                ctx_other[within, lanes] = ctx

        return carry

    lax.fori_loop(0, 2 * half, query_block, 0)


def attention_backward(
    meta, lows, highs, da_own, da_other, q, k, v, ctx_own, ctx_other, lse, wo, seg_col, seg_row,
    dqkv, sums, q_masked, d_masked, dq_t, k_t, delta, dk_sum, dv_sum, powers, slopes,
):
    rows = da_own.shape[0]
    seq = 2 * rows
    core = meta[0]
    d = HEAD_DIM
    width = q.shape[1]
    pairs = width // PAIR
    left = lax.broadcasted_iota(jnp.int32, (BLOCK, PAIR), 1) < d
    for source, values, base in ((da_own, ctx_own, core * rows), (da_other, ctx_other, (1 - core) * rows)):
        for r in range(0, rows, BLOCK):
            at = pl.ds(pl.multiple_of(base + r, BLOCK), BLOCK)
            block = (base + r) // BLOCK
            grads = dot_nn(source[r : r + BLOCK, :], wo[...]).astype(BF16).astype(F32)
            for p in range(pairs):
                lanes = slice(p * PAIR, (p + 1) * PAIR)
                grad = grads[:, lanes]
                d_masked[2 * p, at, :] = jnp.where(left, grad, 0.0).astype(BF16)
                d_masked[2 * p + 1, at, :] = jnp.where(left, 0.0, grad).astype(BF16)
                prod = (grad * values[r : r + BLOCK, lanes].astype(F32)).T
                delta[block, 2 * p : 2 * p + 1, :] = jnp.sum(prod[:d], axis=0, keepdims=True)
                delta[block, 2 * p + 1 : 2 * p + 2, :] = jnp.sum(prod[d:], axis=0, keepdims=True)
    for r in range(0, seq, BLOCK):
        for p in range(pairs):
            lanes = slice(p * PAIR, (p + 1) * PAIR)
            query = q[r : r + BLOCK, lanes].astype(F32)
            q_masked[2 * p, r : r + BLOCK, :] = jnp.where(left, query, 0.0).astype(BF16)
            q_masked[2 * p + 1, r : r + BLOCK, :] = jnp.where(left, 0.0, query).astype(BF16)
            k_t[p, :, r : r + BLOCK] = k[r : r + BLOCK, lanes].T
    dq_t[...] = jnp.zeros_like(dq_t)

    def key_block(b, carry):
        at = pl.ds(pl.multiple_of(b * BLOCK, BLOCK), BLOCK)
        seg_k = seg_col[at, :]
        dk_sum[...] = jnp.zeros_like(dk_sum)
        dv_sum[...] = jnp.zeros_like(dv_sum)

        def query_block(i, carry):
            rows_q = pl.ds(pl.multiple_of(i * BLOCK, BLOCK), BLOCK)
            same = seg_k == seg_row[i]
            for h in range(2 * pairs):
                lanes = slice((h // 2) * PAIR, (h // 2 + 1) * PAIR)
                s = jnp.where(same, dot_nt(k[at, lanes], q_masked[h, rows_q, :]), MASKED)
                p = jnp.exp(s - lse[i, h : h + 1, :])
                dp = dot_nt(v[at, lanes], d_masked[h, rows_q, :])
                powers[h] = p.astype(BF16)
                slopes[h] = (p * (dp - delta[i, h : h + 1, :])).astype(BF16)
            for h in range(2 * pairs):
                p, lanes = h // 2, slice((h % 2) * d, (h % 2 + 1) * d)
                dv_sum[p] += dot_nn(powers[h], d_masked[h, rows_q, :])
                dk_sum[p] += dot_nn(slopes[h], q_masked[h, rows_q, :])
                dq_t[p, lanes, rows_q] += dot_nn(k_t[p, lanes, at], slopes[h])
            return carry

        lax.fori_loop(lows[b], highs[b], query_block, 0)
        for p in range(pairs):
            dqkv[at, width + p * PAIR : width + (p + 1) * PAIR] = dk_sum[p].astype(BF16)
            dqkv[at, 2 * width + p * PAIR : 2 * width + (p + 1) * PAIR] = dv_sum[p].astype(BF16)
        return carry

    lax.fori_loop(0, seq // BLOCK, key_block, 0)
    total = jnp.zeros((1, 3 * width), F32)
    for r in range(0, seq, BLOCK):
        for p in range(pairs):
            dqkv[r : r + BLOCK, p * PAIR : (p + 1) * PAIR] = (dq_t[p, :, r : r + BLOCK].T * d**-0.5).astype(BF16)
        total = total + column_sum(dqkv[r : r + BLOCK, :].astype(F32))
    sums[0:1, :] = total


def transpose_tokens(meta, own, other, out):
    rows = own.shape[0]
    for base, source in ((meta[0] * rows, own), ((1 - meta[0]) * rows, other)):
        for r in range(0, rows, BLOCK):
            out[:, pl.ds(pl.multiple_of(base + r, BLOCK), BLOCK)] = source[r : r + BLOCK, :].T


def projection_grad(meta, token_t, da_own, da_other, ctx_own, ctx_other, dqkv, *refs):
    outs, da_t = refs[:-1], refs[-1]
    d = HEAD_DIM
    width = ctx_own.shape[1]
    da_t[...] = da_own[...].T
    part = dot_nn(da_t[...], ctx_own[...])
    da_t[...] = da_other[...].T
    part = part + dot_nn(da_t[...], ctx_other[...])
    full = dot_nn(token_t[...], dqkv[...])
    for place in range(2):
        lanes = []
        for j in range(width // PAIR):
            at = j * PAIR + place * d
            lanes += [full[:, n * width + at : n * width + at + d] for n in range(3)] + [part[:, at : at + d]]
        store_blocks(jnp.concatenate(lanes, axis=1), outs, place, meta[1])


def input_grad_part(groups, other, meta, *refs):
    out = refs[2 * groups]
    rows = out.shape[0]
    base = (1 - meta[0] if other else meta[0]) * rows
    for r in range(0, rows, BLOCK):
        at = pl.ds(pl.multiple_of(base + r, BLOCK), BLOCK)
        total = dot_nt(refs[0][at, :], refs[groups][...])
        for n in range(1, groups):
            total = total + dot_nt(refs[n][at, :], refs[groups + n][...])
        out[r : r + BLOCK, :] = total.astype(out.dtype)


def normalize(values):
    center = jnp.mean(values, axis=-1, keepdims=True)
    offset = values - center
    inverse = lax.rsqrt(jnp.mean(offset * offset, axis=-1, keepdims=True) + EPSILON)
    return offset * inverse, inverse


def normalize_back(incoming, normed, inverse, gain):
    weighted = incoming * gain
    centered = weighted - jnp.mean(weighted, axis=-1, keepdims=True)
    centered = centered - normed * jnp.mean(weighted * normed, axis=-1, keepdims=True)
    return centered * inverse


def column_sum(values):
    return jnp.sum(values, axis=0, keepdims=True)


def accumulate(target, row, value, lanes=slice(None)):
    @pl.when(pl.program_id(0) == 0)
    def _():
        target[row : row + 1, lanes] = value

    @pl.when(pl.program_id(0) != 0)
    def _():
        target[row : row + 1, lanes] += value


def rows_step(
    meta, everywhere, tokens, vectors, ctx_own, ctx_other, wo_own, wo_other, bias, out_grad,
    output, dr1_out, da_out, act_out, du_out, df_t, low_t, sums, bias_sums,
    w_out, w_up, w_down, slope, sems_up, sems_down,
):
    hidden = w_up.shape[2]
    half = ctx_own.shape[1]
    copies_up = everywhere_copies(everywhere, meta[2], w_up, sems_up, slice(0, hidden))
    copies_down = everywhere_copies(everywhere, meta[2], w_down, sems_down, slice(hidden, 2 * hidden))
    start = pl.program_id(0) == 0

    @pl.when(start)
    def _():
        for copy in copies_up + copies_down:
            copy.start()
        w_out[:, :half] = wo_own[...]
        w_out[:, half:] = wo_other[...]

    out_bias, gain_one, shift_one, down_bias, gain_two, shift_two = (vectors[n : n + 1, :] for n in range(6))
    mixed = dot_nt(jnp.concatenate([ctx_own[...], ctx_other[...]], axis=1), w_out[...])
    normed_one, inverse_one = normalize(tokens[...].astype(F32) + mixed + out_bias)
    first = normed_one * gain_one + shift_one
    low = first.astype(BF16)
    low_t[...] = low.T

    @pl.when(start)
    def _():
        for copy in copies_up:
            copy.wait()

    for t in range(4):
        for n in range(0, hidden, BLOCK):
            at = slice(t * hidden + n, t * hidden + n + BLOCK)
            u = dot_nn(low, w_up[t, :, n : n + BLOCK]) + bias[:, at]
            share = 0.5 + 0.5 * lax.erf(u * 0.5**0.5)
            act_out[:, at] = (u * share).astype(BF16)
            slope[:, at] = share + u * (jnp.exp(-0.5 * u * u) * 0.3989422804014327)

    @pl.when(start)
    def _():
        for copy in copies_down:
            copy.wait()

    fed = first + down_bias
    for t in range(4):
        fed = fed + dot_nt(act_out[:, t * hidden : (t + 1) * hidden], w_down[t])
    normed, inverse = normalize(fed)
    output[...] = (normed * gain_two + shift_two).astype(BF16)
    incoming = out_grad[...].astype(F32)
    dr2 = normalize_back(incoming, normed, inverse, gain_two)
    df = dr2.astype(BF16)
    df_t[...] = df.T
    accumulate(sums, 3, column_sum(df.astype(F32)))
    accumulate(sums, 4, column_sum(incoming * normed))
    accumulate(sums, 5, column_sum(incoming))
    for t in range(4):
        for n in range(0, hidden, BLOCK):
            at = slice(t * hidden + n, t * hidden + n + BLOCK)
            du = (dot_nn(df, w_down[t, :, n : n + BLOCK]) * slope[:, at]).astype(BF16)
            du_out[:, at] = du
            accumulate(bias_sums, 0, column_sum(du.astype(F32)), at)
    incoming = dr2
    for t in range(4):
        incoming = incoming + dot_nt(du_out[:, t * hidden : (t + 1) * hidden], w_up[t])
    dr1 = normalize_back(incoming, normed_one, inverse_one, gain_one)
    dr1_out[...] = dr1
    da = dr1.astype(BF16)
    da_out[...] = da
    accumulate(sums, 0, column_sum(da.astype(F32)))
    accumulate(sums, 1, column_sum(incoming * normed_one))
    accumulate(sums, 2, column_sum(incoming))


def grad_for_partner(left_t, *refs):
    count = len(refs) // 2
    for n in range(count):
        refs[count + n][...] = dot_nn(left_t[...], refs[n][...]).astype(BF16)


def grad_for_chip(meta, left_t, right_one, right_two, received_one, received_two, *outs):
    for place, right, received in ((0, right_one, received_one), (1, right_two, received_two)):
        store_blocks(dot_nn(left_t[...], right[...]) + received[...].astype(F32), outs, place, meta[1])


def local(
    g,
    tokens,
    segment_ids,
    qkv_weight,
    qv_bias,
    out_weight,
    out_bias,
    first_gain,
    first_shift,
    up_weight,
    up_bias,
    down_weight,
    down_bias,
    second_gain,
    second_shift,
    output_grad,
):
    rows, width = tokens.shape
    seq = segment_ids.shape[1]
    heads = qkv_weight.shape[2] // HEAD_DIM
    hidden = up_weight.shape[1]
    shard = qkv_weight.shape[0]
    assert seq == 2 * rows and rows % BLOCK == 0
    d = HEAD_DIM
    local_width = heads * d
    z, y, x, c = (lax.axis_index(name) for name in ("z", "y", "x", "c"))
    regular = g.regular(shard)
    meta = jnp.stack([c, (z * 2 + y) if regular else c * 0, x * 2 + c]).astype(jnp.int32)

    segments = lax.dynamic_index_in_dim(segment_ids, x, 0, keepdims=False)
    blocks = seq // BLOCK
    by_block = segments.reshape(blocks, BLOCK)
    lows = jnp.sum((segments[None, :] < by_block[:, :1]).astype(jnp.int32), axis=1) // BLOCK
    highs = (jnp.sum((segments[None, :] <= by_block[:, -1:]).astype(jnp.int32), axis=1) + BLOCK - 1) // BLOCK
    seg_col = segments.reshape(seq, 1)
    seg_row = segments.reshape(blocks, 1, BLOCK)

    small = jnp.concatenate([up_bias, qv_bias.reshape(-1)]).reshape(1, -1)
    small = jnp.concatenate([small, g.swap(small, "c")], axis=0)
    small = jnp.concatenate([small, g.swap(small, "x")], axis=0).astype(F32)
    hidden_bias = small[:, :hidden].reshape(1, 4 * hidden)
    pair_bias = small[:, hidden:].reshape(2, 2, 2, heads, d)[:, 0].transpose(1, 2, 0, 3)
    pair_bias = pair_bias.reshape(2, heads * PAIR)
    vectors = jnp.stack(
        [out_bias, first_gain, first_shift, down_bias, second_gain, second_shift, out_bias, out_bias]
    ).astype(F32)

    parts = []
    for j in range(heads):
        at = slice(j * d, (j + 1) * d)
        parts += [qkv_weight[:, n, at] for n in range(3)] + [out_weight[:, at]]
    head_weights = Gather(g, jnp.concatenate(parts, axis=1))
    both = gather_everywhere(g, jnp.concatenate([up_weight, down_weight], axis=1))
    other_tokens = g.swap(tokens, "c")
    head_weights.line()
    (token_t,) = call(
        transpose_tokens,
        [shape_of((width, seq), BF16)],
        [meta, tokens, other_tokens],
        in_specs=[SMEM, VMEM, VMEM],
        name="transpose_tokens",
        vmem=16,
    )
    head_weights.first(token_t)
    head_weights.second()

    lanes = heads * PAIR
    blocks = seq // BLOCK
    count = len(head_weights.arrays)
    q, k, v, w, wo, ctx_own, ctx_send, lse = call(
        partial(heads_forward, head_weights.entries, count),
        [shape_of((seq, lanes), BF16)] * 3
        + [shape_of((width, 3 * lanes), BF16), shape_of((width, lanes), BF16)]
        + [shape_of((rows, lanes), BF16)] * 2
        + [shape_of((blocks, 8, BLOCK), F32)],
        [meta, lows, highs, *head_weights.arrays, tokens, other_tokens, pair_bias, seg_col, seg_row],
        in_specs=[SMEM] * 3 + [ANY] * count + [VMEM] * 5,
        scratch=[
            pltpu.VMEM((2, width, 2 * lanes), BF16),
            pltpu.VMEM((2 * heads, SUMMED, seq), BF16),
            pltpu.VMEM((2 * heads, BLOCK, PAIR), BF16),
            pltpu.VMEM((2 * heads, BLOCK, BLOCK), BF16),
            pltpu.SemaphoreType.DMA((len(head_weights.entries),)),
        ],
        flops=2 * seq * width * 3 * lanes + 4 * seq * seq * lanes,
        name="heads_forward",
        vmem=VM_HEADS,
    )
    ctx_other = g.swap(ctx_send, "c")
    other_wo = g.swap(wo, "c")

    def by_rows(lanes):
        return pl.BlockSpec((BLOCK, lanes), lambda i: (i, 0))

    def by_columns(array_rows):
        return pl.BlockSpec((array_rows, BLOCK), lambda i: (0, i))

    def fixed(array):
        return pl.BlockSpec(array.shape, lambda i: (0,) * len(array.shape))

    ffn = 2 * rows * width * 4 * hidden
    sums_shape = shape_of((8, width), F32)
    bias_shape = shape_of((8, 4 * hidden), F32)
    weight_sems = pltpu.SemaphoreType.DMA((both.shape[0] * both.shape[1],))
    output, dr1, da, act, du, df_t, low_t, sums_rows, hidden_sums = call(
        rows_step,
        [
            shape_of((rows, width), BF16),
            shape_of((rows, width), F32),
            shape_of((rows, width), BF16),
            shape_of((rows, 4 * hidden), BF16),
            shape_of((rows, 4 * hidden), BF16),
            shape_of((width, rows), BF16),
            shape_of((width, rows), BF16),
            sums_shape,
            bias_shape,
        ],
        [meta, both, tokens, vectors, ctx_own, ctx_other, wo, other_wo, hidden_bias, output_grad],
        in_specs=[SMEM, ANY, by_rows(width), fixed(vectors), by_rows(lanes), by_rows(lanes), fixed(wo), fixed(wo)]
        + [fixed(hidden_bias), by_rows(width)],
        out_specs=[by_rows(width)] * 3
        + [by_rows(4 * hidden)] * 2
        + [by_columns(width)] * 2
        + [fixed(sums_shape), fixed(bias_shape)],
        scratch=[
            pltpu.VMEM((width, width), BF16),
            pltpu.VMEM((4, width, hidden), BF16),
            pltpu.VMEM((4, width, hidden), BF16),
            pltpu.VMEM((BLOCK, 4 * hidden), F32),
            weight_sems,
            weight_sems,
        ],
        grid=(rows // BLOCK,),
        flops=4 * ffn + 2 * rows * width * width,
        name="rows_step",
        vmem=VM_ROWS,
    )
    other_da = g.swap(da, "c")
    tiles = hidden // BLOCK
    left_spec = pl.BlockSpec((width, rows), lambda i: (0, 0))

    def partner_grad(left_t, right):
        return call(
            grad_for_partner,
            [shape_of((width, hidden), BF16)] * 2,
            [left_t, right, right],
            in_specs=[left_spec] + [pl.BlockSpec((rows, BLOCK), lambda i, t=t: (0, t * tiles + i)) for t in (1, 3)],
            out_specs=[by_columns(width)] * 2,
            grid=(tiles,),
            flops=ffn // 2,
            name="grad_for_partner",
            vmem=VM_GRAD,
        )

    def chip_grad(left_t, right, received):
        leaving = Scatter.shapes(g, shard, hidden)
        arrays = call(
            grad_for_chip,
            leaving,
            [meta, left_t, right, right, *received],
            in_specs=[SMEM, left_spec]
            + [pl.BlockSpec((rows, BLOCK), lambda i, t=t: (0, t * tiles + i)) for t in (0, 2)]
            + [by_columns(width)] * 2,
            out_specs=[
                pl.BlockSpec((*a.shape[:-1], BLOCK), lambda i, n=len(a.shape) - 1: (0,) * n + (i,)) for a in leaving
            ],
            grid=(tiles,),
            flops=ffn // 2,
            name="grad_for_chip",
            vmem=VM_GRAD,
        )
        return Scatter(g, shard, arrays)

    down_other = partner_grad(df_t, act)
    down_received = [g.swap(a, "c") for a in down_other]
    up_other = partner_grad(after(low_t, down_other), du)
    up_received = [g.swap(a, "c") for a in up_other]
    down_grad = chip_grad(after(df_t, up_other), act, down_received)
    up_grad = chip_grad(after(low_t, down_grad.arrays), du, up_received)
    down_away = down_grad.first(up_grad.arrays)

    dqkv, head_sums = call(
        attention_backward,
        [shape_of((seq, 3 * lanes), BF16), shape_of((8, 3 * lanes), F32)],
        [meta, lows, highs, after(da, down_away), other_da, q, k, v, ctx_own, ctx_send, lse, wo, seg_col, seg_row],
        in_specs=[SMEM] * 3 + [VMEM] * 11,
        scratch=[
            pltpu.VMEM((2 * heads, seq, PAIR), BF16),
            pltpu.VMEM((2 * heads, seq, PAIR), BF16),
            pltpu.VMEM((heads, PAIR, seq), F32),
            pltpu.VMEM((heads, PAIR, seq), BF16),
            pltpu.VMEM((blocks, 8, BLOCK), F32),
            pltpu.VMEM((heads, BLOCK, PAIR), F32),
            pltpu.VMEM((heads, BLOCK, PAIR), F32),
            pltpu.VMEM((2 * heads, BLOCK, BLOCK), BF16),
            pltpu.VMEM((2 * heads, BLOCK, BLOCK), BF16),
        ],
        flops=2 * seq * width * lanes + 10 * seq * seq * lanes,
        name="attention_backward",
        vmem=VM_BACK,
    )
    up_away = up_grad.first(dqkv)
    down_second = down_grad.second(dqkv)
    arrays = call(
        projection_grad,
        Scatter.shapes(g, shard, 2 * lanes),
        [meta, token_t, da, other_da, ctx_own, ctx_send, after(dqkv, (up_away, down_second))],
        in_specs=[SMEM] + [VMEM] * 6,
        scratch=[pltpu.VMEM((width, rows), BF16)],
        flops=2 * seq * width * 4 * lanes,
        name="projection_grad",
        vmem=VM_PROJ,
    )
    head_grad = Scatter(g, shard, arrays)

    six = sums_rows[:6]
    six = (six + g.swap(six, "c")).reshape(-1)
    hidden_sums = hidden_sums[0].reshape(2, 2, hidden)
    hidden_sums = hidden_sums[:, 0] + g.swap(hidden_sums[:, 1], "c")
    kinds = head_sums[0].reshape(3, heads, 2, d).transpose(2, 0, 1, 3).reshape(2, 3, local_width)
    keep, send = (jnp.concatenate([six, hidden_sums[r], kinds[r, 0], kinds[r, 2]]) for r in range(2))

    def input_part(first, dtype, dqkv):
        return call(
            partial(input_grad_part, 1, first),
            [shape_of((rows, width), dtype)],
            [meta, dqkv, w],
            in_specs=[SMEM] + [VMEM] * 2,
            flops=seq * width * 3 * lanes,
            name="input_grad_part",
            vmem=VM_PROJ,
        )[0]

    up_second = up_grad.second(arrays)
    down_share = down_grad.third(arrays)
    ig_other = input_part(1, BF16, after(dqkv, (up_second, down_share)))
    head_away = head_grad.first(ig_other)
    summed = keep + after(g.swap(send, "x"), ig_other)
    ig_own = input_part(0, F32, after(dqkv, head_away))
    head_grad.second(ig_own)
    up_share = up_grad.third(ig_own)
    shares = head_grad.third().reshape(shard, heads, 4, d)
    summed = g.total_dp(summed)
    vectors_grad = summed[: 6 * width].reshape(6, width)
    up_bias_share = summed[6 * width : 6 * width + hidden]
    qv_share = summed[6 * width + hidden :].reshape(2, local_width)
    input_grad = dr1 + ig_own + g.swap(ig_other, "c").astype(F32)
    qkv_share = shares[:, :, :3].transpose(0, 2, 1, 3).reshape(shard, 3, local_width)
    out_share = shares[:, :, 3].reshape(shard, local_width)
    return (output, input_grad, qkv_share, qv_share, out_share, up_share, up_bias_share, down_share, vectors_grad)


def solution(mesh):
    g = Grid(mesh)
    dp, tensor = ("z", "y"), ("x", "c")
    rows = P(dp + tensor, None)
    in_specs = (
        rows,
        P(dp, None),
        P(dp, None, tensor),
        P(None, tensor),
        P(dp, tensor),
        P(),
        P(),
        P(),
        P(dp, tensor),
        P(tensor),
        P(dp, tensor),
        P(),
        P(),
        P(),
        rows,
    )
    out_specs = (
        rows,
        rows,
        P(dp, None, tensor),
        P(None, tensor),
        P(dp, tensor),
        P(dp, tensor),
        P(tensor),
        P(dp, tensor),
        P(),
    )
    return jax.shard_map(partial(local, g), mesh=g.mesh, in_specs=in_specs, out_specs=out_specs, check_vma=False)
```

```python
from functools import partial

import jax
import jax.numpy as jnp
from jax import lax
from jax.experimental import pallas as pl
from jax.experimental.pallas import tpu as pltpu
from jax.sharding import Mesh
from jax.sharding import PartitionSpec as P

HEAD_DIM = 64
PAIR = 2 * HEAD_DIM
EPSILON = 1e-12
MASKED = -1e30
BLOCK = 256
ROW_BLOCK = 256
F32 = jnp.float32
BF16 = jnp.bfloat16
MIB = 1 << 20
COST = 1


def dot_nn(left, right):
    return jnp.dot(left, right, preferred_element_type=F32)


def dot_nt(left, right):
    return lax.dot_general(left, right, (((1,), (1,)), ((), ())), preferred_element_type=F32)


def call(body, outs, ins, in_specs=None, out_specs=None, scratch=(), grid=(), flops=0, name=None, vmem=60, alias=None):
    moved = sum(a.size * a.dtype.itemsize for a in ins) + sum(o.size * o.dtype.itemsize for o in outs)
    return pl.pallas_call(
        body,
        grid=grid,
        out_shape=outs,
        in_specs=in_specs or [VMEM] * len(ins),
        out_specs=out_specs or [VMEM] * len(outs),
        scratch_shapes=list(scratch),
        compiler_params=pltpu.CompilerParams(vmem_limit_bytes=vmem * MIB),
        cost_estimate=pl.CostEstimate(flops=int(flops) // COST, bytes_accessed=int(moved) // COST, transcendentals=0),
        input_output_aliases=alias or {},
        name=name,
    )(*ins)


ANY = pl.BlockSpec(memory_space=pl.ANY)
SMEM = pl.BlockSpec(memory_space=pltpu.SMEM)
VMEM = pl.BlockSpec(memory_space=pltpu.VMEM)


def shape_of(shape, dtype):
    return jax.ShapeDtypeStruct(shape, dtype)


def after(values, done):
    return lax.optimization_barrier((values, done))[0]


class Grid:
    def __init__(self, mesh):
        n_dp, n_tensor = mesh.devices.shape
        assert n_tensor == 4 and n_dp % 2 == 0
        self.nz = n_dp // 2
        self.n_dp = n_dp
        self.mesh = Mesh(mesh.devices.reshape(self.nz, 2, 2, 2), ("z", "y", "x", "c"))

    def swap(self, array, axis, r=1):
        size = self.nz if axis == "z" else 2
        return lax.ppermute(array, axis, [(i, i ^ r) for i in range(size)])

    def regular(self, rows):
        return rows % 32 == 0 and self.nz & (self.nz - 1) == 0

    def total_dp(self, array):
        if self.nz & (self.nz - 1):
            return lax.psum(array, ("z", "y"))
        array = array + self.swap(array, "y")
        r = 1
        while r < self.nz:
            array = array + self.swap(array, "z", r)
            r *= 2
        return array


class Gather:
    def __init__(self, g, shard):
        self.g, self.shard, self.rows = g, shard, shard.shape[0]
        self.regular = g.regular(self.rows)

    def line(self):
        g, half = self.g, self.rows // 2
        if not self.regular:
            full = lax.all_gather(self.shard, ("z", "y"), axis=0, tiled=True)[None, None]
            self.arrays = [full, g.swap(full, "x")]
            self.entries = [(n, 0, 0, n, 0, 0, full.shape[2]) for n in range(2)]
            return self.arrays
        near = [self.shard] + [g.swap(self.shard, "z", r) for r in range(1, g.nz)]
        self.lines = [jnp.stack([part[:half] for part in near]), jnp.stack([part[half:] for part in near])]
        return self.lines

    def wait(self, step, done):
        if self.regular:
            setattr(self, step, after(getattr(self, step), done))

    def first(self, done=()):
        if not self.regular:
            return self.arrays
        arrived = after([self.g.swap(line, axis) for line, axis in zip(self.lines, "xy")], done)
        self.twos = [jnp.stack([line, other]) for line, other in zip(self.lines, arrived)]
        return arrived

    def second(self):
        if not self.regular:
            return self.arrays
        half = self.rows // 2
        self.arrays, self.entries = [], []
        for number, axis in enumerate("xy"):
            two = self.twos[number]
            four = self.g.swap(two, "yx"[number])
            for index, array in ((0, two), (1, four)):
                for i in range(2):
                    rx, ry = (i, index) if axis == "x" else (index, i)
                    for k in range(self.g.nz):
                        self.entries.append((len(self.arrays), i, k, rx, k * 2 + ry, number * half, half))
                self.arrays.append(array)
        return self.arrays


def load_pieces(entries, refs, index, target, sems, lanes):
    slots = 1 + max(entry[4] for entry in entries)
    copies = []
    for number, (a, i, k, place, slot, first, size) in enumerate(entries):
        row = pl.multiple_of((slot ^ index) * (target.shape[1] // slots) + first, 16)
        copies.append(
            pltpu.make_async_copy(refs[a].at[i, k, :, lanes], target.at[place, pl.ds(row, size)], sems.at[number])
        )
    for copy in copies:
        copy.start()
    for copy in copies:
        copy.wait()


def gather_everywhere(g, shard):
    if g.regular(shard.shape[0]):
        full = lax.all_gather(shard, ("z", "y", "x", "c"), axis=0)
        return full.reshape(g.n_dp, 4, *shard.shape)
    full = lax.all_gather(shard, ("z", "y"), axis=0, tiled=True)
    return lax.all_gather(full, ("x", "c"), axis=0)[None]


def everywhere_copies(source, me, target, sems, lanes):
    blocks, places, rows = source.shape[:3]
    return [
        pltpu.make_async_copy(
            source.at[block, t, :, lanes],
            target.at[t ^ me, pl.ds(block * rows, rows)],
            sems.at[block * places + t],
        )
        for block in range(blocks)
        for t in range(places)
    ]


SPARE = 16


class Scatter:
    def __init__(self, g, rows, arrays, vector=None):
        self.g, self.rows = g, rows
        self.regular = g.regular(rows)
        self.arrays = arrays
        self.vector = vector

    @staticmethod
    def shapes(g, rows, lanes, spare=0, weights=None):
        lead = () if weights is None else (weights,)
        if not g.regular(rows):
            return [shape_of((*lead, 2, rows * g.n_dp, lanes), BF16)]
        size = 2 * g.nz * rows // 2
        block = shape_of((*lead, size, lanes), BF16)
        return [block, shape_of((*lead, size + spare, lanes), BF16), block, block]

    def first(self, done=()):
        g = self.g
        if not self.regular:
            (whole,) = self.arrays
            both = whole[..., 0, :, :].astype(F32) + g.swap(whole[..., 1, :, :], "x").astype(F32)
            self.sum = lax.psum_scatter(both, ("z", "y"), scatter_dimension=both.ndim - 2, tiled=True)
            if self.vector is not None:
                self.vector = lax.psum(self.vector[0] + g.swap(self.vector[1], "x"), ("z", "y"))
            return [self.sum]
        keep_x, send_x, keep_y, send_y = self.arrays
        self.got = after([g.swap(send_x, "x"), g.swap(send_y, "y")], done)
        lead, half, lanes = keep_x.shape[:-2], keep_x.shape[-2] // 2, keep_x.shape[-1]
        outs, ins = [shape_of((*lead, half, lanes), BF16)] * 2, [keep_x, self.got[0], keep_y, self.got[1]]
        if self.vector is not None:
            outs = [shape_of((half + SPARE, lanes), BF16), outs[1], shape_of((SPARE // 2, lanes), F32)]
            ins.append(self.vector[0])
        self.away = call(sum_away, outs, ins, name="sum_away", vmem=SUM_VMEM)
        return self.away

    def second(self, done=()):
        if not self.regular:
            return [self.sum]
        g = self.g
        seconds = after([g.swap(self.away[0], "y"), g.swap(self.away[1], "x")], done)
        lead, lanes = self.away[1].shape[:-2], self.away[1].shape[-1]
        outs = [shape_of((*lead, self.rows, lanes), F32)]
        ins = [self.arrays[0], self.got[0], seconds[0], self.arrays[2], self.got[1], seconds[1]]
        far_rows = self.rows
        if self.vector is not None:
            outs.append(shape_of((SPARE // 2, lanes), F32))
            ins.append(self.away[2])
            far_rows += SPARE
        outs += [shape_of((*lead, far_rows, lanes), BF16)] * (g.nz - 1)
        self.line = call(partial(sum_line, g.nz), outs, ins, name="sum_line", vmem=SUM_VMEM)
        return self.line

    def third(self, done=()):
        if not self.regular:
            return [self.sum] if self.vector is None else [self.sum, self.vector]
        count = 1 if self.vector is None else 2
        arrived = [self.g.swap(far, "z", r + 1) for r, far in enumerate(self.line[count:])]
        return [*self.line[:count], *after(arrived, done)]


SUM_VMEM = 12
VM_HEADS = 60
VM_ROWS = 60
VM_GRAD = 40
VM_BACK = 36
VM_PROJ = 36


def split_in_two(value):
    high = value.astype(BF16)
    return jnp.concatenate([high, (value - high.astype(F32)).astype(BF16)], axis=0)


def join_two(ref):
    spare = ref[ref.shape[0] - SPARE :, :].astype(F32)
    return spare[: SPARE // 2] + spare[SPARE // 2 :]


def sum_away(keep_x, got_x, keep_y, got_y, *refs):
    half = keep_x.shape[-2] // 2
    if len(refs) == 4:
        vector, out_x, out_y, vector_out = refs
        total = vector[...] + join_two(got_x)
        vector_out[...] = total
        out_x[half:, :] = split_in_two(total)
    else:
        out_x, out_y = refs
    for keep, got, out in ((keep_x, got_x, out_x), (keep_y, got_y, out_y)):
        away = keep[..., half:, :].astype(F32) + got[..., half : 2 * half, :].astype(F32)
        out[..., :half, :] = away.astype(BF16)


def sum_line(nz, keep_x, got_x, last_x, keep_y, got_y, last_y, *refs):
    size = keep_x.shape[-2] // (2 * nz)
    if len(refs) > nz:
        vector, near, vector_out, *far = refs
        total = vector[...] + join_two(last_x)
        vector_out[...] = total
        parts = split_in_two(total)
        for out in far:
            out[2 * size :, :] = parts
    else:
        near, *far = refs
    for n, (keep, got, last) in enumerate(((keep_x, got_x, last_x), (keep_y, got_y, last_y))):
        for r in range(nz):
            at = slice(r * size, (r + 1) * size)
            total = keep[..., at, :].astype(F32) + got[..., at, :].astype(F32) + last[..., at, :].astype(F32)
            out = far[r - 1] if r else near
            out[..., n * size : (n + 1) * size, :] = total.astype(out.dtype)


def store_blocks(value, outs, stage, place, index, nz):
    value = value.astype(BF16)
    if len(outs) == 1:
        outs[0][place] = value
        return
    by_x = outs[place]
    half = stage.shape[1] // (2 * nz)
    for block in range(value.shape[0] // (2 * half)):
        slot = block ^ index
        ry, rz = lax.rem(slot, 2), lax.div(slot, 2)
        row = pl.multiple_of((ry * nz + rz) * half, 16)
        by_x[pl.ds(row, half), :] = value[2 * block * half : (2 * block + 1) * half]
        row = pl.multiple_of((place * nz + rz) * half, 16)
        stage[ry, pl.ds(row, half), :] = value[(2 * block + 1) * half : (2 * block + 2) * half]
    if place == 1:
        outs[2][...] = stage[0]
        outs[3][...] = stage[1]


SUMMED = HEAD_DIM + 16


def heads_forward(entries, count, meta, lows, highs, *refs):
    pieces = refs[:count]
    own, other, bias, seg_row = refs[count : count + 4]
    q, k, v, w_out, ctx_own, ctx_other, lse = refs[count + 4 : count + 11]
    weights, v_t, q_masked, powers, seg_col, sems = refs[count + 11 :]
    rows = own.shape[0]
    core = meta[0]
    load_pieces(entries, pieces, meta[1], weights, sems, slice(None))
    d = HEAD_DIM
    width = q.shape[1]
    pairs = width // PAIR
    for j in range(pairs):
        for kind in range(3):
            at = slice((3 * j + kind) * d, (3 * j + kind + 1) * d)
            pair = jnp.concatenate([weights[0][:, at], weights[1][:, at]], axis=1)
            w_out[:, kind * width + j * PAIR : kind * width + (j + 1) * PAIR] = pair
    ones = jnp.ones((SUMMED - d, BLOCK), BF16)
    for source, base in ((own, core * rows), (other, (1 - core) * rows)):

        def project(n, carry):
            at = pl.ds(pl.multiple_of(base + n * BLOCK, BLOCK), BLOCK)
            block = source[pl.ds(pl.multiple_of(n * BLOCK, BLOCK), BLOCK), :]
            all_three = dot_nn(block, w_out[...])
            query = (all_three[:, :width] + bias[0:1, :]).astype(BF16)
            q[at, :] = (query.astype(F32) * d**-0.5).astype(BF16)
            k[at, :] = all_three[:, width : 2 * width].astype(BF16)
            values = (all_three[:, 2 * width :] + bias[1:2, :]).astype(BF16)
            v[at, :] = values
            for p in range(pairs):
                columns = values[:, p * PAIR : (p + 1) * PAIR].T
                for h in range(2):
                    v_t[2 * p + h, :d, at] = columns[h * d : (h + 1) * d]
                    v_t[2 * p + h, d:, at] = ones
            return carry

        lax.fori_loop(0, rows // BLOCK, project, 0)
    left = lax.broadcasted_iota(jnp.int32, (BLOCK, PAIR), 1) < d
    half = rows // BLOCK
    for b in range(2 * half):
        seg_col[b * BLOCK : (b + 1) * BLOCK, :] = column_of(seg_row[b])

    def query_block(i, carry):
        at = pl.ds(pl.multiple_of(i * BLOCK, BLOCK), BLOCK)
        seg_q = seg_row[i]
        for p in range(pairs):
            query = q[at, p * PAIR : (p + 1) * PAIR].astype(F32)
            q_masked[2 * p] = jnp.where(left, query, 0.0).astype(BF16)
            q_masked[2 * p + 1] = jnp.where(left, 0.0, query).astype(BF16)

        def key_block(b, carry):
            tops, sums = carry
            rows = pl.ds(pl.multiple_of(b * BLOCK, BLOCK), BLOCK)
            same = seg_col[rows, :] == seg_q
            new_tops, new_sums = [], []
            for h in range(2 * pairs):
                s = dot_nt(k[rows, (h // 2) * PAIR : (h // 2 + 1) * PAIR], q_masked[h])
                s = jnp.where(same, s, MASKED)
                top = jnp.maximum(tops[h], jnp.max(s, axis=0, keepdims=True))
                powers[h] = jnp.exp(s - top).astype(BF16)
                new_tops.append(top)
            for h in range(2 * pairs):
                scale = jnp.exp(tops[h] - new_tops[h])
                new_sums.append(sums[h] * scale + dot_nn(v_t[h, :, rows], powers[h]))
            return tuple(new_tops), tuple(new_sums)

        first_top = jnp.full((1, BLOCK), MASKED, F32)
        first_sum = jnp.zeros((SUMMED, BLOCK), F32)
        tops, sums = lax.fori_loop(
            lows[i], highs[i], key_block, ((first_top,) * (2 * pairs), (first_sum,) * (2 * pairs))
        )
        for p in range(pairs):
            parts = []
            for h in (2 * p, 2 * p + 1):
                total = sums[h][d : d + 1, :]
                lse[i, h : h + 1, :] = tops[h] + jnp.log(total)
                parts.append(sums[h][:d, :] / total)
            ctx = jnp.concatenate(parts, axis=0).T.astype(BF16)
            lanes = slice(p * PAIR, (p + 1) * PAIR)
            own_half = lax.div(i, half) == core
            within = pl.ds(pl.multiple_of(lax.rem(i, half) * BLOCK, BLOCK), BLOCK)

            @pl.when(own_half)
            def _():
                ctx_own[within, lanes] = ctx

            @pl.when(jnp.logical_not(own_half))
            def _():
                ctx_other[within, lanes] = ctx

        return carry

    lax.fori_loop(0, 2 * half, query_block, 0)


def heads_back_start(meta, da_own, da_other, ctx_own, ctx_other, wo, dctx, delta, out_grad, left_t):
    rows = da_own.shape[0]
    core = meta[0]
    d = HEAD_DIM
    pairs = ctx_own.shape[1] // PAIR
    for source, values, base in ((da_own, ctx_own, core * rows), (da_other, ctx_other, (1 - core) * rows)):

        def context_grad(n, carry):
            here = pl.ds(pl.multiple_of(n * BLOCK, BLOCK), BLOCK)
            at = pl.ds(pl.multiple_of(base + n * BLOCK, BLOCK), BLOCK)
            block = base // BLOCK + n
            left_t[:, here] = source[here, :].T
            grads = dot_nn(source[here, :], wo[...]).astype(BF16)
            dctx[at, :] = grads
            for p in range(pairs):
                lanes = slice(p * PAIR, (p + 1) * PAIR)
                prod = (grads[:, lanes].astype(F32) * values[here, lanes].astype(F32)).T
                delta[block, 2 * p : 2 * p + 1, :] = jnp.sum(prod[:d], axis=0, keepdims=True)
                delta[block, 2 * p + 1 : 2 * p + 2, :] = jnp.sum(prod[d:], axis=0, keepdims=True)
            return carry

        lax.fori_loop(0, rows // BLOCK, context_grad, 0)
        part = dot_nn(left_t[...], values[...])
        if source is da_own:
            out_grad[...] = part
        else:
            out_grad[...] += part


def attention_backward(first, last, given, meta, lows, highs, q, k, v, dctx, lse, delta, seg_row, *refs):
    dq_in, (dq_t, dkv, dk_sum, dv_sum, powers, slopes) = refs[:given], refs[given:]
    d = HEAD_DIM
    width = q.shape[1]
    pairs = width // PAIR
    left = lax.broadcasted_iota(jnp.int32, (BLOCK, PAIR), 1) < d
    dq_t[...] = dq_in[0][...] if given else jnp.zeros_like(dq_t)

    def key_block(b, carry):
        at = pl.ds(pl.multiple_of(b * BLOCK, BLOCK), BLOCK)
        seg_k = column_of(seg_row[b])
        dk_sum[...] = jnp.zeros_like(dk_sum)
        dv_sum[...] = jnp.zeros_like(dv_sum)
        keys, values, keys_t = [], [], []
        for p in range(pairs):
            lanes = slice(p * PAIR, (p + 1) * PAIR)
            key, value = k[at, lanes].astype(F32), v[at, lanes].astype(F32)
            keys += [jnp.where(left, key, 0.0).astype(BF16), jnp.where(left, 0.0, key).astype(BF16)]
            values += [jnp.where(left, value, 0.0).astype(BF16), jnp.where(left, 0.0, value).astype(BF16)]
            keys_t.append(k[at, lanes].T)

        def query_block(i, carry):
            rows_q = pl.ds(pl.multiple_of(i * BLOCK, BLOCK), BLOCK)
            same = seg_k == seg_row[i]
            for h in range(2 * pairs):
                lanes = slice((h // 2) * PAIR, (h // 2 + 1) * PAIR)
                s = jnp.where(same, dot_nt(keys[h], q[rows_q, lanes]), MASKED)
                p = jnp.exp(s - lse[i, h : h + 1, :])
                dp = dot_nt(values[h], dctx[rows_q, lanes])
                powers[h] = p.astype(BF16)
                slopes[h] = (p * (dp - delta[i, h : h + 1, :])).astype(BF16)
            for h in range(2 * pairs):
                p, half = h // 2, slice((h % 2) * d, (h % 2 + 1) * d)
                lanes = slice(p * PAIR, (p + 1) * PAIR)
                dv_sum[h] += dot_nn(powers[h], dctx[rows_q, lanes])
                dk_sum[h] += dot_nn(slopes[h], q[rows_q, lanes])
                dq_t[p, half, rows_q] += dot_nn(keys_t[p][half, :], slopes[h])
            return carry

        lax.fori_loop(lows[b], highs[b], query_block, 0)
        for p in range(pairs):
            for n, total in ((1, dk_sum), (2, dv_sum)):
                value = jnp.where(left, total[2 * p], total[2 * p + 1])
                here = pl.ds(pl.multiple_of((b - first) * BLOCK, BLOCK), BLOCK)
                dkv[here, (n - 1) * width + p * PAIR : (n - 1) * width + (p + 1) * PAIR] = value.astype(BF16)
        return carry

    lax.fori_loop(first, last, key_block, 0)


def column_of(row):
    return jnp.broadcast_to(row.astype(F32), (128, BLOCK)).T[:, 0:1].astype(jnp.int32)


def transpose_tokens(meta, own, other, out):
    rows = own.shape[0]
    for base, source in ((meta[0] * rows, own), ((1 - meta[0]) * rows, other)):
        for r in range(0, rows, BLOCK):
            out[:, pl.ds(pl.multiple_of(base + r, BLOCK), BLOCK)] = source[r : r + BLOCK, :].T


def projection_grad(nz, meta, token_t, out_grad, dq_t, dkv_one, dkv_two, vector, *refs):
    outs, dqkv, stage = refs[:-2], refs[-2], refs[-1]
    d = HEAD_DIM
    seq = token_t.shape[1]
    width = out_grad.shape[1]

    def join(n, total):
        at = pl.ds(pl.multiple_of(n * BLOCK, BLOCK), BLOCK)
        for p in range(width // PAIR):
            dqkv[at, p * PAIR : (p + 1) * PAIR] = (dq_t[p, :, at].T * d**-0.5).astype(BF16)
        return total + column_sum(dqkv[at, :width].astype(F32))

    dqkv[: seq // 2, width:] = dkv_one[...]
    dqkv[seq // 2 :, width:] = dkv_two[...]
    q_sum = lax.fori_loop(0, seq // BLOCK, join, jnp.zeros((1, width), F32))
    v_sum = column_sum(dkv_one[:, width:].astype(F32)) + column_sum(dkv_two[:, width:].astype(F32))
    full = dot_nn(token_t[...], dqkv[...])
    vectors = []
    for place in range(2):
        lanes, biases = [], []
        for j in range(width // PAIR):
            at = j * PAIR + place * d
            lanes += [full[:, n * width + at : n * width + at + d] for n in range(3)] + [out_grad[:, at : at + d]]
        store_blocks(jnp.concatenate(lanes, axis=1), outs[:-1], stage, place, meta[1], nz)
        for total in (q_sum, v_sum):
            biases += [total[:, j * PAIR + place * d : j * PAIR + (place + 1) * d] for j in range(width // PAIR)]
        biases.append(jnp.zeros((1, vector.shape[2] - len(biases) * d), F32))
        vectors.append(jnp.concatenate([vector[place], jnp.concatenate(biases, axis=1)], axis=0))
    outs[-1][0] = vectors[0]
    outs[-1][1] = vectors[1]
    if len(outs) > 2:
        outs[1][outs[0].shape[0] :, :] = split_in_two(vectors[1])


def input_grad_other(meta, dqkv, w, out):
    rows = out.shape[0]
    base = (1 - meta[0]) * rows
    for r in range(0, rows, BLOCK):
        at = pl.ds(pl.multiple_of(base + r, BLOCK), BLOCK)
        out[r : r + BLOCK, :] = dot_nt(dqkv[at, :], w[...]).astype(BF16)


def input_grad_own(meta, dqkv, w, dr1, arrived, out):
    rows = out.shape[0]
    base = meta[0] * rows
    for r in range(0, rows, BLOCK):
        at = pl.ds(pl.multiple_of(base + r, BLOCK), BLOCK)
        here = slice(r, r + BLOCK)
        out[here, :] = dot_nt(dqkv[at, :], w[...]) + dr1[here, :] + arrived[here, :].astype(F32)


def finish_heads(count, near, vector, *refs):
    arrived, (qkv_out, out_out, vector_out) = refs[:count], refs[count:]
    total, sums = near[...], vector[...]
    rows = total.shape[0]
    for part in arrived:
        total = total + part[:rows, :].astype(F32)
        sums = sums + join_two(part)
    d = HEAD_DIM
    heads = total.shape[1] // (4 * d)
    for kind in range(4):
        value = jnp.concatenate([total[:, (4 * j + kind) * d : (4 * j + kind + 1) * d] for j in range(heads)], axis=1)
        if kind == 3:
            out_out[...] = value
        else:
            qkv_out[kind] = value
    vector_out[...] = sums


def normalize(values):
    center = jnp.mean(values, axis=-1, keepdims=True)
    offset = values - center
    inverse = lax.rsqrt(jnp.mean(offset * offset, axis=-1, keepdims=True) + EPSILON)
    return offset * inverse, inverse


def normalize_back(incoming, normed, inverse, gain):
    weighted = incoming * gain
    centered = weighted - jnp.mean(weighted, axis=-1, keepdims=True)
    centered = centered - normed * jnp.mean(weighted * normed, axis=-1, keepdims=True)
    return centered * inverse


def column_sum(values):
    return jnp.sum(values, axis=0, keepdims=True)


def rows_step(
    meta, everywhere, tokens, vectors, ctx_own, ctx_other, bias, out_grad,
    output, dr1_out, da_out, act_out, du_out, df_t, low_t, sums, bias_sums, wo_own,
    w_out, w_all, slope, sems,
):
    hidden = tokens.shape[1]
    half = ctx_own.shape[1]
    copies = everywhere_copies(everywhere, meta[2], w_all, sems, slice(None))
    w_up = w_all.at[:, :, :hidden]
    w_down = w_all.at[:, :, hidden : 2 * hidden]
    start = pl.program_id(0) == 0

    @pl.when(start)
    def _():
        for copy in copies:
            copy.start()
        for copy in copies:
            copy.wait()
        d = HEAD_DIM
        for core in range(2):
            for j in range(half // PAIR):
                first = 2 * hidden + j * d
                pair = [w_all[2 * place + core, :, first : first + d] for place in range(2)]
                at = core * half + j * PAIR
                w_out[:, at : at + PAIR] = jnp.concatenate(pair, axis=1)
        wo_own[...] = w_out[:, :half]
        sums[...] = jnp.zeros_like(sums)
        bias_sums[...] = jnp.zeros_like(bias_sums)

    out_bias, gain_one, shift_one, down_bias, gain_two, shift_two = (vectors[n : n + 1, :] for n in range(6))
    mixed = dot_nt(jnp.concatenate([ctx_own[...], ctx_other[...]], axis=1), w_out[...])
    normed_one, inverse_one = normalize(tokens[...].astype(F32) + mixed + out_bias)
    first = normed_one * gain_one + shift_one
    low = first.astype(BF16)
    low_t[...] = low.T

    for t in range(4):
        for n in range(0, hidden, BLOCK):
            at = slice(t * hidden + n, t * hidden + n + BLOCK)
            u = dot_nn(low, w_up[t, :, n : n + BLOCK]) + bias[:, at]
            share = 0.5 + 0.5 * lax.erf(u * 0.5**0.5)
            act_out[:, at] = (u * share).astype(BF16)
            slope[:, at] = share + u * (jnp.exp(-0.5 * u * u) * 0.3989422804014327)

    fed = first + down_bias
    for t in range(4):
        fed = fed + dot_nt(act_out[:, t * hidden : (t + 1) * hidden], w_down[t])
    normed, inverse = normalize(fed)
    output[...] = (normed * gain_two + shift_two).astype(BF16)
    incoming = out_grad[...].astype(F32)
    dr2 = normalize_back(incoming, normed, inverse, gain_two)
    df = dr2.astype(BF16)
    df_t[...] = df.T
    sums[3:4, :] += column_sum(df.astype(F32))
    sums[4:5, :] += column_sum(incoming * normed)
    sums[5:6, :] += column_sum(incoming)
    for t in range(4):
        for n in range(0, hidden, BLOCK):
            at = slice(t * hidden + n, t * hidden + n + BLOCK)
            du = (dot_nn(df, w_down[t, :, n : n + BLOCK]) * slope[:, at]).astype(BF16)
            du_out[:, at] = du
            bias_sums[0:1, at] += column_sum(du.astype(F32))
    incoming = dr2
    for t in range(4):
        incoming = incoming + dot_nt(du_out[:, t * hidden : (t + 1) * hidden], w_up[t])
    dr1 = normalize_back(incoming, normed_one, inverse_one, gain_one)
    dr1_out[...] = dr1
    da = dr1.astype(BF16)
    da_out[...] = da
    sums[0:1, :] += column_sum(da.astype(F32))
    sums[1:2, :] += column_sum(incoming * normed_one)
    sums[2:3, :] += column_sum(incoming)


def grad_for_partner(df_t, low_t, act_one, act_two, du_one, du_two, out_one, out_two):
    for out, act, du in ((out_one, act_one, du_one), (out_two, act_two, du_two)):
        out[0] = dot_nn(df_t[...], act[...]).astype(BF16)
        out[1] = dot_nn(low_t[...], du[...]).astype(BF16)


def grad_for_chip(nz, meta, df_t, low_t, act_one, act_two, du_one, du_two, received_one, received_two, *refs):
    outs, stage = refs[:-1], refs[-1]
    for n, left_t, rights in ((0, df_t, (act_one, act_two)), (1, low_t, (du_one, du_two))):
        for place, received in ((0, received_one), (1, received_two)):
            value = dot_nn(left_t[...], rights[place][...]) + received[n].astype(F32)
            store_blocks(value, [out.at[n] for out in outs], stage.at[n], place, meta[1], nz)


def local(
    g,
    tokens,
    segment_ids,
    qkv_weight,
    qv_bias,
    out_weight,
    out_bias,
    first_gain,
    first_shift,
    up_weight,
    up_bias,
    down_weight,
    down_bias,
    second_gain,
    second_shift,
    output_grad,
):
    rows, width = tokens.shape
    seq = segment_ids.shape[1]
    heads = qkv_weight.shape[2] // HEAD_DIM
    hidden = up_weight.shape[1]
    shard = qkv_weight.shape[0]
    assert seq == 2 * rows and rows % BLOCK == 0 and hidden == width
    d = HEAD_DIM
    local_width = heads * d
    z, y, x, c = (lax.axis_index(name) for name in ("z", "y", "x", "c"))
    regular = g.regular(shard)
    meta = jnp.stack([c, (z * 2 + y) if regular else c * 0, x * 2 + c]).astype(jnp.int32)

    segments = lax.dynamic_index_in_dim(segment_ids, x, 0, keepdims=False)
    blocks = seq // BLOCK
    by_block = segments.reshape(blocks, BLOCK)
    lows = jnp.sum((segments[None, :] < by_block[:, :1]).astype(jnp.int32), axis=1) // BLOCK
    highs = (jnp.sum((segments[None, :] <= by_block[:, -1:]).astype(jnp.int32), axis=1) + BLOCK - 1) // BLOCK
    seg_row = segments.reshape(blocks, 1, BLOCK)

    small = jnp.concatenate([up_bias, qv_bias.reshape(-1)]).reshape(1, -1)
    small = jnp.concatenate([small, g.swap(small, "x")], axis=0)
    small = jnp.stack([small, g.swap(small, "c")], axis=1).reshape(4, -1).astype(F32)
    hidden_bias = small[:, :hidden].reshape(1, 4 * hidden)
    pair_bias = small[:, hidden:].reshape(2, 2, 2, heads, d)[:, 0].transpose(1, 2, 0, 3)
    pair_bias = pair_bias.reshape(2, heads * PAIR)
    vectors = jnp.stack(
        [out_bias, first_gain, first_shift, down_bias, second_gain, second_shift, out_bias, out_bias]
    ).astype(F32)

    parts = []
    for j in range(heads):
        at = slice(j * d, (j + 1) * d)
        parts += [qkv_weight[:, n, at] for n in range(3)]
    parts.append(jnp.zeros((shard, -3 * local_width % 128), BF16))
    head_weights = Gather(g, jnp.concatenate(parts, axis=1))
    rest = jnp.zeros((shard, -local_width % 128), BF16)
    rest = jnp.concatenate([up_weight, after(down_weight, head_weights.shard), out_weight, rest], axis=1)
    both = gather_everywhere(g, rest)
    other_tokens = g.swap(tokens, "c")
    head_weights.line()
    head_weights.wait("lines", small)
    (token_t,) = call(
        transpose_tokens,
        [shape_of((width, seq), BF16)],
        [meta, tokens, other_tokens],
        in_specs=[SMEM, VMEM, VMEM],
        name="transpose_tokens",
        vmem=16,
    )
    head_weights.first(token_t)
    head_weights.second()

    lanes = heads * PAIR
    blocks = seq // BLOCK
    count = len(head_weights.arrays)
    q, k, v, w, ctx_own, ctx_send, lse = call(
        partial(heads_forward, head_weights.entries, count),
        [shape_of((seq, lanes), BF16)] * 3
        + [shape_of((width, 3 * lanes), BF16)]
        + [shape_of((rows, lanes), BF16)] * 2
        + [shape_of((blocks, 8, BLOCK), F32)],
        [meta, lows, highs, *head_weights.arrays, tokens, other_tokens, pair_bias, seg_row],
        in_specs=[SMEM] * 3 + [ANY] * count + [VMEM] * 4,
        scratch=[
            pltpu.VMEM((2, width, head_weights.shard.shape[1]), BF16),
            pltpu.VMEM((2 * heads, SUMMED, seq), BF16),
            pltpu.VMEM((2 * heads, BLOCK, PAIR), BF16),
            pltpu.VMEM((2 * heads, BLOCK, BLOCK), BF16),
            pltpu.VMEM((seq, 1), jnp.int32),
            pltpu.SemaphoreType.DMA((len(head_weights.entries),)),
        ],
        flops=2 * seq * width * 3 * lanes + 4 * seq * seq * lanes,
        name="heads_forward",
        vmem=VM_HEADS,
    )
    ctx_other = g.swap(ctx_send, "c")

    def by_rows(lanes):
        return pl.BlockSpec((ROW_BLOCK, lanes), lambda i: (i, 0))

    def by_columns(array_rows):
        return pl.BlockSpec((array_rows, ROW_BLOCK), lambda i: (0, i))

    def fixed(array):
        return pl.BlockSpec(array.shape, lambda i: (0,) * len(array.shape))

    ffn = 2 * rows * width * 4 * hidden
    sums_shape = shape_of((8, width), F32)
    bias_shape = shape_of((8, 4 * hidden), F32)
    weight_sems = pltpu.SemaphoreType.DMA((both.shape[0] * both.shape[1],))
    output, dr1, da, act, du, df_t, low_t, sums_rows, hidden_sums, wo = call(
        rows_step,
        [
            shape_of((rows, width), BF16),
            shape_of((rows, width), F32),
            shape_of((rows, width), BF16),
            shape_of((rows, 4 * hidden), BF16),
            shape_of((rows, 4 * hidden), BF16),
            shape_of((width, rows), BF16),
            shape_of((width, rows), BF16),
            sums_shape,
            bias_shape,
            shape_of((width, lanes), BF16),
        ],
        [meta, both, tokens, vectors, ctx_own, ctx_other, hidden_bias, output_grad],
        in_specs=[SMEM, ANY, by_rows(width), fixed(vectors), by_rows(lanes), by_rows(lanes)]
        + [fixed(hidden_bias), by_rows(width)],
        out_specs=[by_rows(width)] * 3
        + [by_rows(4 * hidden)] * 2
        + [by_columns(width)] * 2
        + [fixed(sums_shape), fixed(bias_shape), pl.BlockSpec((width, lanes), lambda i: (0, 0))],
        scratch=[
            pltpu.VMEM((width, width), BF16),
            pltpu.VMEM((4, width, both.shape[3]), BF16),
            pltpu.VMEM((ROW_BLOCK, 4 * hidden), F32),
            weight_sems,
        ],
        grid=(rows // ROW_BLOCK,),
        flops=4 * ffn + 2 * rows * width * width,
        name="rows_step",
        vmem=VM_ROWS,
    )
    other_da = g.swap(da, "c")
    tiles = hidden // BLOCK
    left_spec = pl.BlockSpec((width, rows), lambda i: (0, 0))

    def right_specs(places):
        return [pl.BlockSpec((rows, BLOCK), lambda i, t=t: (0, t * tiles + i)) for t in places] * 2

    partner_spec = pl.BlockSpec((2, width, BLOCK), lambda i: (0, 0, i))
    for_partner = call(
        grad_for_partner,
        [shape_of((2, width, hidden), BF16)] * 2,
        [df_t, low_t, act, act, du, du],
        in_specs=[left_spec] * 2 + right_specs((1, 3)),
        out_specs=[partner_spec] * 2,
        grid=(tiles,),
        flops=ffn,
        name="grad_for_partner",
        vmem=VM_GRAD,
    )
    dctx, delta, out_grad = call(
        heads_back_start,
        [shape_of((seq, lanes), BF16), shape_of((blocks, 8, BLOCK), F32), shape_of((width, lanes), F32)],
        [meta, da, other_da, ctx_own, ctx_send, wo],
        in_specs=[SMEM] + [VMEM] * 5,
        scratch=[pltpu.VMEM((width, rows), BF16)],
        flops=4 * seq * width * lanes,
        name="heads_back_start",
        vmem=VM_PROJ,
    )
    received = [g.swap(a, "c") for a in after(for_partner, other_da)]
    leaving = Scatter.shapes(g, shard, hidden, weights=2)
    ffn_grad = Scatter(
        g,
        shard,
        call(
            partial(grad_for_chip, g.nz),
            leaving,
            [meta, after(df_t, dctx), low_t, act, act, du, du, *received],
            in_specs=[SMEM] + [left_spec] * 2 + right_specs((0, 2)) + [partner_spec] * 2,
            out_specs=[
                pl.BlockSpec((*a.shape[:-1], BLOCK), lambda i, n=len(a.shape) - 1: (0,) * n + (i,)) for a in leaving
            ],
            scratch=[pltpu.VMEM((2, 2, leaving[0].shape[-2], BLOCK), BF16)],
            grid=(tiles,),
            flops=ffn,
            name="grad_for_chip",
            vmem=VM_GRAD,
        ),
    )

    def attend_back(first, last, dctx, *dq):
        return call(
            partial(attention_backward, first, last, len(dq)),
            [shape_of((heads, PAIR, seq), F32), shape_of(((last - first) * BLOCK, 2 * lanes), BF16)],
            [meta, lows, highs, q, k, v, dctx, lse, delta, seg_row, *dq],
            in_specs=[SMEM] * 3 + [VMEM] * (7 + len(dq)),
            scratch=[pltpu.VMEM((2 * heads, BLOCK, PAIR), F32)] * 2 + [pltpu.VMEM((2 * heads, BLOCK, BLOCK), BF16)] * 2,
            flops=5 * seq * seq * lanes,
            name="attention_backward",
            vmem=VM_BACK,
        )

    dq_t, dkv_one = attend_back(0, blocks // 2, after(dctx, ffn_grad.arrays))
    ffn_away = ffn_grad.first(dkv_one)
    dq_t, dkv_two = attend_back(blocks // 2, blocks, after(dctx, ffn_away), dq_t)
    ffn_second = ffn_grad.second(dkv_two)

    six = sums_rows[:6]
    six = six + g.swap(six, "c")
    hidden_sums = hidden_sums[0].reshape(2, 2, hidden)
    hidden_sums = hidden_sums[:, 0] + g.swap(hidden_sums[:, 1], "c")
    vector = jnp.concatenate([jnp.stack([six, six]), hidden_sums[:, None]], axis=1)
    *arrays, vector, dqkv = call(
        partial(projection_grad, g.nz),
        Scatter.shapes(g, shard, 2 * lanes, SPARE) + [shape_of((2, 8, width), F32), shape_of((seq, 3 * lanes), BF16)],
        [meta, token_t, out_grad, after(dq_t, ffn_second), dkv_one, dkv_two, vector],
        in_specs=[SMEM] + [VMEM] * 6,
        scratch=[pltpu.VMEM((2, width // 2, 2 * lanes), BF16)],
        flops=2 * seq * width * 3 * lanes,
        name="projection_grad",
        vmem=VM_PROJ,
    )
    head_grad = Scatter(g, shard, arrays, (vector[0], vector[1]))
    ffn_parts = ffn_grad.third(arrays)
    ffn_share = ffn_parts[0] + sum(part.astype(F32) for part in ffn_parts[1:])
    head_away = head_grad.first(ffn_share)
    (ig_other,) = call(
        input_grad_other,
        [shape_of((rows, width), BF16)],
        [meta, after(dqkv, head_away), w],
        in_specs=[SMEM] + [VMEM] * 2,
        flops=seq * width * 3 * lanes,
        name="input_grad_other",
        vmem=VM_PROJ,
    )
    ig_arrived = g.swap(ig_other, "c")
    (input_grad,) = call(
        input_grad_own,
        [shape_of((rows, width), F32)],
        [meta, dqkv, w, dr1, ig_arrived],
        in_specs=[SMEM] + [VMEM] * 4,
        flops=seq * width * 3 * lanes,
        name="input_grad_own",
        vmem=VM_PROJ,
    )
    head_grad.second(input_grad)
    down_share, up_share = ffn_share[0], ffn_share[1]
    parts = head_grad.third()
    if regular:
        qkv_share, out_share, summed = call(
            partial(finish_heads, len(parts) - 2),
            [shape_of((3, shard, local_width), F32), shape_of((shard, local_width), F32), shape_of((8, width), F32)],
            parts,
            name="finish_heads",
            vmem=SUM_VMEM,
        )
    else:
        shares, summed = parts
        shares = shares.reshape(shard, heads, 4, d).transpose(2, 0, 1, 3).reshape(4, shard, local_width)
        qkv_share, out_share = shares[:3], shares[3]
    qkv_share = qkv_share.transpose(1, 0, 2)
    vectors_grad, up_bias_share = summed[:6], summed[6]
    qv_share = summed[7, : 2 * local_width].reshape(2, local_width)
    return (output, input_grad, qkv_share, qv_share, out_share, up_share, up_bias_share, down_share, vectors_grad)


def solution(mesh):
    g = Grid(mesh)
    dp, tensor = ("z", "y"), ("x", "c")
    rows = P(dp + tensor, None)
    in_specs = (
        rows,
        P(dp, None),
        P(dp, None, tensor),
        P(None, tensor),
        P(dp, tensor),
        P(),
        P(),
        P(),
        P(dp, tensor),
        P(tensor),
        P(dp, tensor),
        P(),
        P(),
        P(),
        rows,
    )
    out_specs = (
        rows,
        rows,
        P(dp, None, tensor),
        P(None, tensor),
        P(dp, tensor),
        P(dp, tensor),
        P(tensor),
        P(dp, tensor),
        P(),
    )
    return jax.shard_map(partial(local, g), mesh=g.mesh, in_specs=in_specs, out_specs=out_specs, check_vma=False)
```

```python
from functools import partial

import jax
import jax.numpy as jnp
from jax import lax
from jax.experimental import pallas as pl
from jax.experimental.pallas import tpu as pltpu
from jax.sharding import Mesh
from jax.sharding import PartitionSpec as P

HEAD_DIM = 64
PAIR = 2 * HEAD_DIM
EPSILON = 1e-12
MASKED = -1e30
BLOCK = 256
ROW_BLOCK = 256
F32 = jnp.float32
BF16 = jnp.bfloat16
MIB = 1 << 20
COST = 1


def dot_nn(left, right):
    return jnp.dot(left, right, preferred_element_type=F32)


def dot_nt(left, right):
    return lax.dot_general(left, right, (((1,), (1,)), ((), ())), preferred_element_type=F32)


def call(body, outs, ins, in_specs=None, out_specs=None, scratch=(), grid=(), flops=0, name=None, vmem=60, alias=None):
    moved = sum(a.size * a.dtype.itemsize for a in ins) + sum(o.size * o.dtype.itemsize for o in outs)
    return pl.pallas_call(
        body,
        grid=grid,
        out_shape=outs,
        in_specs=in_specs or [VMEM] * len(ins),
        out_specs=out_specs or [VMEM] * len(outs),
        scratch_shapes=list(scratch),
        compiler_params=pltpu.CompilerParams(vmem_limit_bytes=vmem * MIB),
        cost_estimate=pl.CostEstimate(flops=int(flops) // COST, bytes_accessed=int(moved) // COST, transcendentals=0),
        input_output_aliases=alias or {},
        name=name,
    )(*ins)


ANY = pl.BlockSpec(memory_space=pl.ANY)
SMEM = pl.BlockSpec(memory_space=pltpu.SMEM)
VMEM = pl.BlockSpec(memory_space=pltpu.VMEM)


def shape_of(shape, dtype):
    return jax.ShapeDtypeStruct(shape, dtype)


def after(values, done):
    return lax.optimization_barrier((values, done))[0]


class Grid:
    def __init__(self, mesh):
        n_dp, n_tensor = mesh.devices.shape
        assert n_tensor == 4 and n_dp % 2 == 0
        self.nz = n_dp // 2
        self.n_dp = n_dp
        self.mesh = Mesh(mesh.devices.reshape(self.nz, 2, 2, 2), ("z", "y", "x", "c"))

    def swap(self, array, axis, r=1):
        size = self.nz if axis == "z" else 2
        return lax.ppermute(array, axis, [(i, i ^ r) for i in range(size)])

    def regular(self, rows):
        return rows % 32 == 0 and self.nz & (self.nz - 1) == 0

    def total_dp(self, array):
        if self.nz & (self.nz - 1):
            return lax.psum(array, ("z", "y"))
        array = array + self.swap(array, "y")
        r = 1
        while r < self.nz:
            array = array + self.swap(array, "z", r)
            r *= 2
        return array


class Gather:
    def __init__(self, g, shard):
        self.g, self.shard, self.rows = g, shard, shard.shape[0]
        self.regular = g.regular(self.rows)

    def line(self):
        g, half = self.g, self.rows // 2
        if not self.regular:
            full = lax.all_gather(self.shard, ("z", "y"), axis=0, tiled=True)[None, None]
            self.arrays = [full, g.swap(full, "x")]
            self.entries = [(n, 0, 0, n, 0, 0, full.shape[2]) for n in range(2)]
            return self.arrays
        near = [self.shard] + [g.swap(self.shard, "z", r) for r in range(1, g.nz)]
        self.lines = [jnp.stack([part[:half] for part in near]), jnp.stack([part[half:] for part in near])]
        return self.lines

    def wait(self, step, done):
        if self.regular:
            setattr(self, step, after(getattr(self, step), done))

    def first(self, done=()):
        if not self.regular:
            return self.arrays
        arrived = after([self.g.swap(line, axis) for line, axis in zip(self.lines, "xy")], done)
        self.twos = [jnp.stack([line, other]) for line, other in zip(self.lines, arrived)]
        return arrived

    def second(self):
        if not self.regular:
            return self.arrays
        half = self.rows // 2
        self.arrays, self.entries = [], []
        for number, axis in enumerate("xy"):
            two = self.twos[number]
            four = self.g.swap(two, "yx"[number])
            for index, array in ((0, two), (1, four)):
                for i in range(2):
                    rx, ry = (i, index) if axis == "x" else (index, i)
                    for k in range(self.g.nz):
                        self.entries.append((len(self.arrays), i, k, rx, k * 2 + ry, number * half, half))
                self.arrays.append(array)
        return self.arrays


def load_pieces(entries, refs, index, target, sems, lanes):
    slots = 1 + max(entry[4] for entry in entries)
    copies = []
    for number, (a, i, k, place, slot, first, size) in enumerate(entries):
        row = pl.multiple_of((slot ^ index) * (target.shape[1] // slots) + first, 16)
        copies.append(
            pltpu.make_async_copy(refs[a].at[i, k, :, lanes], target.at[place, pl.ds(row, size)], sems.at[number])
        )
    for copy in copies:
        copy.start()
    for copy in copies:
        copy.wait()


def gather_everywhere(g, shard):
    if g.regular(shard.shape[0]):
        full = lax.all_gather(shard, ("z", "y", "x", "c"), axis=0)
        return full.reshape(g.n_dp, 4, *shard.shape)
    full = lax.all_gather(shard, ("z", "y"), axis=0, tiled=True)
    return lax.all_gather(full, ("x", "c"), axis=0)[None]


def everywhere_copies(source, me, target, sems, lanes):
    blocks, places, rows = source.shape[:3]
    return [
        pltpu.make_async_copy(
            source.at[block, t, :, lanes],
            target.at[t ^ me, pl.ds(block * rows, rows)],
            sems.at[block * places + t],
        )
        for block in range(blocks)
        for t in range(places)
    ]


SPARE = 16


class Scatter:
    def __init__(self, g, rows, arrays, vector=None):
        self.g, self.rows = g, rows
        self.regular = g.regular(rows)
        self.arrays = arrays
        self.vector = vector

    @staticmethod
    def shapes(g, rows, lanes, spare=0, weights=None):
        lead = () if weights is None else (weights,)
        if not g.regular(rows):
            return [shape_of((*lead, 2, rows * g.n_dp, lanes), BF16)]
        size = 2 * g.nz * rows // 2
        block = shape_of((*lead, size, lanes), BF16)
        return [block, shape_of((*lead, size + spare, lanes), BF16), block, block]

    def first(self, done=()):
        g = self.g
        if not self.regular:
            (whole,) = self.arrays
            both = whole[..., 0, :, :].astype(F32) + g.swap(whole[..., 1, :, :], "x").astype(F32)
            self.sum = lax.psum_scatter(both, ("z", "y"), scatter_dimension=both.ndim - 2, tiled=True)
            if self.vector is not None:
                self.vector = lax.psum(self.vector[0] + g.swap(self.vector[1], "x"), ("z", "y"))
            return [self.sum]
        keep_x, send_x, keep_y, send_y = self.arrays
        self.got = after([g.swap(send_x, "x"), g.swap(send_y, "y")], done)
        lead, half, lanes = keep_x.shape[:-2], keep_x.shape[-2] // 2, keep_x.shape[-1]
        outs, ins = [shape_of((*lead, half, lanes), BF16)] * 2, [keep_x, self.got[0], keep_y, self.got[1]]
        if self.vector is not None:
            outs = [shape_of((half + SPARE, lanes), BF16), outs[1], shape_of((SPARE // 2, lanes), F32)]
            ins.append(self.vector[0])
        self.away = call(sum_away, outs, ins, name="sum_away", vmem=SUM_VMEM)
        return self.away

    def second(self, done=()):
        if not self.regular:
            return [self.sum]
        g = self.g
        seconds = after([g.swap(self.away[0], "y"), g.swap(self.away[1], "x")], done)
        lead, lanes = self.away[1].shape[:-2], self.away[1].shape[-1]
        outs = [shape_of((*lead, self.rows, lanes), F32)]
        ins = [self.arrays[0], self.got[0], seconds[0], self.arrays[2], self.got[1], seconds[1]]
        far_rows = self.rows
        if self.vector is not None:
            outs.append(shape_of((SPARE // 2, lanes), F32))
            ins.append(self.away[2])
            far_rows += SPARE
        outs += [shape_of((*lead, far_rows, lanes), BF16)] * (g.nz - 1)
        self.line = call(partial(sum_line, g.nz), outs, ins, name="sum_line", vmem=SUM_VMEM)
        return self.line

    def third(self, done=()):
        if not self.regular:
            return [self.sum] if self.vector is None else [self.sum, self.vector]
        count = 1 if self.vector is None else 2
        arrived = [self.g.swap(far, "z", r + 1) for r, far in enumerate(self.line[count:])]
        return [*self.line[:count], *after(arrived, done)]


SUM_VMEM = 12
VM_HEADS = 60
VM_ROWS = 60
VM_GRAD = 40
VM_PART = 60
VM_START = 60
VM_BACK = 36
VM_PROJ = 36


def split_in_two(value):
    high = value.astype(BF16)
    return jnp.concatenate([high, (value - high.astype(F32)).astype(BF16)], axis=0)


def join_two(ref):
    spare = ref[ref.shape[0] - SPARE :, :].astype(F32)
    return spare[: SPARE // 2] + spare[SPARE // 2 :]


def sum_away(keep_x, got_x, keep_y, got_y, *refs):
    half = keep_x.shape[-2] // 2
    if len(refs) == 4:
        vector, out_x, out_y, vector_out = refs
        total = vector[...] + join_two(got_x)
        vector_out[...] = total
        out_x[half:, :] = split_in_two(total)
    else:
        out_x, out_y = refs
    for keep, got, out in ((keep_x, got_x, out_x), (keep_y, got_y, out_y)):
        away = keep[..., half:, :].astype(F32) + got[..., half : 2 * half, :].astype(F32)
        out[..., :half, :] = away.astype(BF16)


def sum_line(nz, keep_x, got_x, last_x, keep_y, got_y, last_y, *refs):
    size = keep_x.shape[-2] // (2 * nz)
    if len(refs) > nz:
        vector, near, vector_out, *far = refs
        total = vector[...] + join_two(last_x)
        vector_out[...] = total
        parts = split_in_two(total)
        for out in far:
            out[2 * size :, :] = parts
    else:
        near, *far = refs
    for n, (keep, got, last) in enumerate(((keep_x, got_x, last_x), (keep_y, got_y, last_y))):
        for r in range(nz):
            at = slice(r * size, (r + 1) * size)
            total = keep[..., at, :].astype(F32) + got[..., at, :].astype(F32) + last[..., at, :].astype(F32)
            out = far[r - 1] if r else near
            out[..., n * size : (n + 1) * size, :] = total.astype(out.dtype)


def store_blocks(value, outs, stage, place, index, nz):
    value = value.astype(BF16)
    if len(outs) == 1:
        outs[0][place] = value
        return
    by_x = outs[place]
    half = stage.shape[1] // (2 * nz)
    for block in range(value.shape[0] // (2 * half)):
        slot = block ^ index
        ry, rz = lax.rem(slot, 2), lax.div(slot, 2)
        row = pl.multiple_of((ry * nz + rz) * half, 16)
        by_x[pl.ds(row, half), :] = value[2 * block * half : (2 * block + 1) * half]
        row = pl.multiple_of((place * nz + rz) * half, 16)
        stage[ry, pl.ds(row, half), :] = value[(2 * block + 1) * half : (2 * block + 2) * half]
    if place == 1:
        outs[2][...] = stage[0]
        outs[3][...] = stage[1]


SUMMED = HEAD_DIM + 16


def heads_forward(entries, count, meta, lows, highs, *refs):
    pieces = refs[:count]
    own, other, bias, seg_row = refs[count : count + 4]
    q, k, v, w_out, ctx_own, ctx_other, lse = refs[count + 4 : count + 11]
    weights, v_t, q_masked, powers, seg_col, sems = refs[count + 11 :]
    rows = own.shape[0]
    core = meta[0]
    load_pieces(entries, pieces, meta[1], weights, sems, slice(None))
    d = HEAD_DIM
    width = q.shape[1]
    pairs = width // PAIR
    for j in range(pairs):
        for kind in range(3):
            at = slice((3 * j + kind) * d, (3 * j + kind + 1) * d)
            pair = jnp.concatenate([weights[0][:, at], weights[1][:, at]], axis=1)
            w_out[:, kind * width + j * PAIR : kind * width + (j + 1) * PAIR] = pair
    ones = jnp.ones((SUMMED - d, BLOCK), BF16)
    for source, base in ((own, core * rows), (other, (1 - core) * rows)):

        def project(n, carry):
            at = pl.ds(pl.multiple_of(base + n * BLOCK, BLOCK), BLOCK)
            block = source[pl.ds(pl.multiple_of(n * BLOCK, BLOCK), BLOCK), :]
            all_three = dot_nn(block, w_out[...])
            query = (all_three[:, :width] + bias[0:1, :]).astype(BF16)
            q[at, :] = (query.astype(F32) * d**-0.5).astype(BF16)
            k[at, :] = all_three[:, width : 2 * width].astype(BF16)
            values = (all_three[:, 2 * width :] + bias[1:2, :]).astype(BF16)
            v[at, :] = values
            for p in range(pairs):
                columns = values[:, p * PAIR : (p + 1) * PAIR].T
                for h in range(2):
                    v_t[2 * p + h, :d, at] = columns[h * d : (h + 1) * d]
                    v_t[2 * p + h, d:, at] = ones
            return carry

        lax.fori_loop(0, rows // BLOCK, project, 0)
    left = lax.broadcasted_iota(jnp.int32, (BLOCK, PAIR), 1) < d
    half = rows // BLOCK
    for b in range(2 * half):
        seg_col[b * BLOCK : (b + 1) * BLOCK, :] = column_of(seg_row[b])

    def query_block(i, carry):
        at = pl.ds(pl.multiple_of(i * BLOCK, BLOCK), BLOCK)
        seg_q = seg_row[i]
        for p in range(pairs):
            query = q[at, p * PAIR : (p + 1) * PAIR].astype(F32)
            q_masked[2 * p] = jnp.where(left, query, 0.0).astype(BF16)
            q_masked[2 * p + 1] = jnp.where(left, 0.0, query).astype(BF16)

        def key_block(b, carry):
            tops, sums = carry
            rows = pl.ds(pl.multiple_of(b * BLOCK, BLOCK), BLOCK)
            same = seg_col[rows, :] == seg_q
            new_tops, new_sums = [], []
            for h in range(2 * pairs):
                s = dot_nt(k[rows, (h // 2) * PAIR : (h // 2 + 1) * PAIR], q_masked[h])
                s = jnp.where(same, s, MASKED)
                top = jnp.maximum(tops[h], jnp.max(s, axis=0, keepdims=True))
                powers[h] = jnp.exp(s - top).astype(BF16)
                new_tops.append(top)
            for h in range(2 * pairs):
                scale = jnp.exp(tops[h] - new_tops[h])
                new_sums.append(sums[h] * scale + dot_nn(v_t[h, :, rows], powers[h]))
            return tuple(new_tops), tuple(new_sums)

        first_top = jnp.full((1, BLOCK), MASKED, F32)
        first_sum = jnp.zeros((SUMMED, BLOCK), F32)
        tops, sums = lax.fori_loop(
            lows[i], highs[i], key_block, ((first_top,) * (2 * pairs), (first_sum,) * (2 * pairs))
        )
        for p in range(pairs):
            parts = []
            for h in (2 * p, 2 * p + 1):
                total = sums[h][d : d + 1, :]
                lse[i, h : h + 1, :] = tops[h] + jnp.log(total)
                parts.append(sums[h][:d, :] / total)
            ctx = jnp.concatenate(parts, axis=0).T.astype(BF16)
            lanes = slice(p * PAIR, (p + 1) * PAIR)
            own_half = lax.div(i, half) == core
            within = pl.ds(pl.multiple_of(lax.rem(i, half) * BLOCK, BLOCK), BLOCK)

            @pl.when(own_half)
            def _():
                ctx_own[within, lanes] = ctx

            @pl.when(jnp.logical_not(own_half))
            def _():
                ctx_other[within, lanes] = ctx

        return carry

    lax.fori_loop(0, 2 * half, query_block, 0)


def heads_back_start(meta, da_own, da_other, ctx_own, ctx_other, wo, dctx, delta, out_grad, left_t):
    rows = da_own.shape[0]
    core = meta[0]
    d = HEAD_DIM
    pairs = ctx_own.shape[1] // PAIR
    for source, values, base in ((da_own, ctx_own, core * rows), (da_other, ctx_other, (1 - core) * rows)):

        def context_grad(n, carry):
            here = pl.ds(pl.multiple_of(n * BLOCK, BLOCK), BLOCK)
            at = pl.ds(pl.multiple_of(base + n * BLOCK, BLOCK), BLOCK)
            block = base // BLOCK + n
            left_t[:, here] = source[here, :].T
            grads = dot_nn(source[here, :], wo[...]).astype(BF16)
            dctx[at, :] = grads
            for p in range(pairs):
                lanes = slice(p * PAIR, (p + 1) * PAIR)
                prod = (grads[:, lanes].astype(F32) * values[here, lanes].astype(F32)).T
                delta[block, 2 * p : 2 * p + 1, :] = jnp.sum(prod[:d], axis=0, keepdims=True)
                delta[block, 2 * p + 1 : 2 * p + 2, :] = jnp.sum(prod[d:], axis=0, keepdims=True)
            return carry

        lax.fori_loop(0, rows // BLOCK, context_grad, 0)
        part = dot_nn(left_t[...], values[...])
        if source is da_own:
            out_grad[...] = part
        else:
            out_grad[...] += part


def attention_backward(first, last, given, meta, lows, highs, q, k, v, dctx, lse, delta, seg_row, *refs):
    dq_in, (dq_t, dkv, dk_sum, dv_sum, powers, slopes) = refs[:given], refs[given:]
    d = HEAD_DIM
    width = q.shape[1]
    pairs = width // PAIR
    left = lax.broadcasted_iota(jnp.int32, (BLOCK, PAIR), 1) < d
    dq_t[...] = dq_in[0][...] if given else jnp.zeros_like(dq_t)

    def key_block(b, carry):
        at = pl.ds(pl.multiple_of(b * BLOCK, BLOCK), BLOCK)
        seg_k = column_of(seg_row[b])
        dk_sum[...] = jnp.zeros_like(dk_sum)
        dv_sum[...] = jnp.zeros_like(dv_sum)
        keys, values, keys_t = [], [], []
        for p in range(pairs):
            lanes = slice(p * PAIR, (p + 1) * PAIR)
            key, value = k[at, lanes].astype(F32), v[at, lanes].astype(F32)
            keys += [jnp.where(left, key, 0.0).astype(BF16), jnp.where(left, 0.0, key).astype(BF16)]
            values += [jnp.where(left, value, 0.0).astype(BF16), jnp.where(left, 0.0, value).astype(BF16)]
            keys_t.append(k[at, lanes].T)

        def query_block(i, carry):
            rows_q = pl.ds(pl.multiple_of(i * BLOCK, BLOCK), BLOCK)
            same = seg_k == seg_row[i]
            for h in range(2 * pairs):
                lanes = slice((h // 2) * PAIR, (h // 2 + 1) * PAIR)
                s = jnp.where(same, dot_nt(keys[h], q[rows_q, lanes]), MASKED)
                p = jnp.exp(s - lse[i, h : h + 1, :])
                dp = dot_nt(values[h], dctx[rows_q, lanes])
                powers[h] = p.astype(BF16)
                slopes[h] = (p * (dp - delta[i, h : h + 1, :])).astype(BF16)
            for h in range(2 * pairs):
                p, half = h // 2, slice((h % 2) * d, (h % 2 + 1) * d)
                lanes = slice(p * PAIR, (p + 1) * PAIR)
                dv_sum[h] += dot_nn(powers[h], dctx[rows_q, lanes])
                dk_sum[h] += dot_nn(slopes[h], q[rows_q, lanes])
                dq_t[p, half, rows_q] += dot_nn(keys_t[p][half, :], slopes[h])
            return carry

        lax.fori_loop(lows[b], highs[b], query_block, 0)
        for p in range(pairs):
            for n, total in ((1, dk_sum), (2, dv_sum)):
                value = jnp.where(left, total[2 * p], total[2 * p + 1])
                here = pl.ds(pl.multiple_of((b - first) * BLOCK, BLOCK), BLOCK)
                dkv[here, (n - 1) * width + p * PAIR : (n - 1) * width + (p + 1) * PAIR] = value.astype(BF16)
        return carry

    lax.fori_loop(first, last, key_block, 0)


def column_of(row):
    return jnp.broadcast_to(row.astype(F32), (128, BLOCK)).T[:, 0:1].astype(jnp.int32)


def transpose_tokens(meta, own, other, out):
    rows = own.shape[0]
    for base, source in ((meta[0] * rows, own), ((1 - meta[0]) * rows, other)):
        for r in range(0, rows, BLOCK):
            out[:, pl.ds(pl.multiple_of(base + r, BLOCK), BLOCK)] = source[r : r + BLOCK, :].T


def projection_grad(nz, meta, token_t, out_grad, dq_t, dkv_one, dkv_two, vector, *refs):
    outs, dqkv, stage = refs[:-2], refs[-2], refs[-1]
    d = HEAD_DIM
    seq = token_t.shape[1]
    width = out_grad.shape[1]

    def join(n, total):
        at = pl.ds(pl.multiple_of(n * BLOCK, BLOCK), BLOCK)
        for p in range(width // PAIR):
            dqkv[at, p * PAIR : (p + 1) * PAIR] = (dq_t[p, :, at].T * d**-0.5).astype(BF16)
        return total + column_sum(dqkv[at, :width].astype(F32))

    dqkv[: seq // 2, width:] = dkv_one[...]
    dqkv[seq // 2 :, width:] = dkv_two[...]
    q_sum = lax.fori_loop(0, seq // BLOCK, join, jnp.zeros((1, width), F32))
    v_sum = column_sum(dkv_one[:, width:].astype(F32)) + column_sum(dkv_two[:, width:].astype(F32))
    full = dot_nn(token_t[...], dqkv[...])
    vectors = []
    for place in range(2):
        lanes, biases = [], []
        for j in range(width // PAIR):
            at = j * PAIR + place * d
            lanes += [full[:, n * width + at : n * width + at + d] for n in range(3)] + [out_grad[:, at : at + d]]
        store_blocks(jnp.concatenate(lanes, axis=1), outs[:-1], stage, place, meta[1], nz)
        for total in (q_sum, v_sum):
            biases += [total[:, j * PAIR + place * d : j * PAIR + (place + 1) * d] for j in range(width // PAIR)]
        biases.append(jnp.zeros((1, vector.shape[2] - len(biases) * d), F32))
        vectors.append(jnp.concatenate([vector[place], jnp.concatenate(biases, axis=1)], axis=0))
    outs[-1][0] = vectors[0]
    outs[-1][1] = vectors[1]
    if len(outs) > 2:
        outs[1][outs[0].shape[0] :, :] = split_in_two(vectors[1])


def input_grad_other(meta, dqkv, w, out):
    rows = out.shape[0]
    base = (1 - meta[0]) * rows
    for r in range(0, rows, BLOCK):
        at = pl.ds(pl.multiple_of(base + r, BLOCK), BLOCK)
        out[r : r + BLOCK, :] = dot_nt(dqkv[at, :], w[...]).astype(BF16)


def input_grad_own(meta, dqkv, w, dr1, arrived, out):
    rows = out.shape[0]
    base = meta[0] * rows
    for r in range(0, rows, BLOCK):
        at = pl.ds(pl.multiple_of(base + r, BLOCK), BLOCK)
        here = slice(r, r + BLOCK)
        out[here, :] = dot_nt(dqkv[at, :], w[...]) + dr1[here, :] + arrived[here, :].astype(F32)


def finish_heads(count, near, vector, *refs):
    arrived, (qkv_out, out_out, six_out, hidden_out, head_out) = refs[:count], refs[count:]
    total, sums = near[...], vector[...]
    rows = total.shape[0]
    for part in arrived:
        total = total + part[:rows, :].astype(F32)
        sums = sums + join_two(part)
    d = HEAD_DIM
    heads = total.shape[1] // (4 * d)
    for kind in range(4):
        value = jnp.concatenate([total[:, (4 * j + kind) * d : (4 * j + kind + 1) * d] for j in range(heads)], axis=1)
        if kind == 3:
            out_out[...] = value
        else:
            qkv_out[kind] = value
    lanes = heads * d
    six_out[...] = sums[:6]
    hidden_out[...] = sums[6:7]
    head_out[0:1, :] = sums[7:8, :lanes]
    head_out[1:2, :] = sums[7:8, lanes : 2 * lanes]


def normalize(values):
    center = jnp.mean(values, axis=-1, keepdims=True)
    offset = values - center
    inverse = lax.rsqrt(jnp.mean(offset * offset, axis=-1, keepdims=True) + EPSILON)
    return offset * inverse, inverse


def normalize_back(incoming, normed, inverse, gain):
    weighted = incoming * gain
    centered = weighted - jnp.mean(weighted, axis=-1, keepdims=True)
    centered = centered - normed * jnp.mean(weighted * normed, axis=-1, keepdims=True)
    return centered * inverse


def column_sum(values):
    return jnp.sum(values, axis=0, keepdims=True)


def rows_step(
    meta, everywhere, tokens, vectors, ctx_own, ctx_other, bias, out_grad,
    output, dr1_out, da_out, act_out, du_out, df_t, low_t, sums, bias_sums, wo_own,
    w_out, w_all, slope, sems,
):
    hidden = tokens.shape[1]
    half = ctx_own.shape[1]
    copies = everywhere_copies(everywhere, meta[2], w_all, sems, slice(None))
    w_up = w_all.at[:, :, :hidden]
    w_down = w_all.at[:, :, hidden : 2 * hidden]
    start = pl.program_id(0) == 0

    @pl.when(start)
    def _():
        for copy in copies:
            copy.start()
        for copy in copies:
            copy.wait()
        d = HEAD_DIM
        for core in range(2):
            for j in range(half // PAIR):
                first = 2 * hidden + j * d
                pair = [w_all[2 * place + core, :, first : first + d] for place in range(2)]
                at = core * half + j * PAIR
                w_out[:, at : at + PAIR] = jnp.concatenate(pair, axis=1)
        wo_own[...] = w_out[:, :half]
        sums[...] = jnp.zeros_like(sums)
        bias_sums[...] = jnp.zeros_like(bias_sums)

    out_bias, gain_one, shift_one, down_bias, gain_two, shift_two = (vectors[n : n + 1, :] for n in range(6))
    mixed = dot_nt(jnp.concatenate([ctx_own[...], ctx_other[...]], axis=1), w_out[...])
    normed_one, inverse_one = normalize(tokens[...].astype(F32) + mixed + out_bias)
    first = normed_one * gain_one + shift_one
    low = first.astype(BF16)
    low_t[...] = low.T

    for t in range(4):
        for n in range(0, hidden, BLOCK):
            at = slice(t * hidden + n, t * hidden + n + BLOCK)
            u = dot_nn(low, w_up[t, :, n : n + BLOCK]) + bias[:, at]
            share = 0.5 + 0.5 * lax.erf(u * 0.5**0.5)
            act_out[:, at] = (u * share).astype(BF16)
            slope[:, at] = share + u * (jnp.exp(-0.5 * u * u) * 0.3989422804014327)

    fed = first + down_bias
    for t in range(4):
        fed = fed + dot_nt(act_out[:, t * hidden : (t + 1) * hidden], w_down[t])
    normed, inverse = normalize(fed)
    output[...] = (normed * gain_two + shift_two).astype(BF16)
    incoming = out_grad[...].astype(F32)
    dr2 = normalize_back(incoming, normed, inverse, gain_two)
    df = dr2.astype(BF16)
    df_t[...] = df.T
    sums[3:4, :] += column_sum(df.astype(F32))
    sums[4:5, :] += column_sum(incoming * normed)
    sums[5:6, :] += column_sum(incoming)
    for t in range(4):
        for n in range(0, hidden, BLOCK):
            at = slice(t * hidden + n, t * hidden + n + BLOCK)
            du = (dot_nn(df, w_down[t, :, n : n + BLOCK]) * slope[:, at]).astype(BF16)
            du_out[:, at] = du
            bias_sums[0:1, at] += column_sum(du.astype(F32))
    incoming = dr2
    for t in range(4):
        incoming = incoming + dot_nt(du_out[:, t * hidden : (t + 1) * hidden], w_up[t])
    dr1 = normalize_back(incoming, normed_one, inverse_one, gain_one)
    dr1_out[...] = dr1
    da = dr1.astype(BF16)
    da_out[...] = da
    sums[0:1, :] += column_sum(da.astype(F32))
    sums[1:2, :] += column_sum(incoming * normed_one)
    sums[2:3, :] += column_sum(incoming)


def grad_for_partner(df_t, low_t, act_one, act_two, du_one, du_two, out_one, out_two):
    for out, act, du in ((out_one, act_one, du_one), (out_two, act_two, du_two)):
        out[0] = dot_nn(df_t[...], act[...]).astype(BF16)
        out[1] = dot_nn(low_t[...], du[...]).astype(BF16)


def grad_for_chip(nz, meta, df_t, low_t, act_one, act_two, du_one, du_two, received_one, received_two, *refs):
    outs, stage = refs[:-1], refs[-1]
    for n, left_t, rights in ((0, df_t, (act_one, act_two)), (1, low_t, (du_one, du_two))):
        for place, received in ((0, received_one), (1, received_two)):
            value = dot_nn(left_t[...], rights[place][...]) + received[n].astype(F32)
            store_blocks(value, [out.at[n] for out in outs], stage.at[n], place, meta[1], nz)


def local(
    g,
    tokens,
    segment_ids,
    qkv_weight,
    qv_bias,
    out_weight,
    out_bias,
    first_gain,
    first_shift,
    up_weight,
    up_bias,
    down_weight,
    down_bias,
    second_gain,
    second_shift,
    output_grad,
):
    rows, width = tokens.shape
    seq = segment_ids.shape[1]
    heads = qkv_weight.shape[2] // HEAD_DIM
    hidden = up_weight.shape[1]
    shard = qkv_weight.shape[0]
    assert seq == 2 * rows and rows % BLOCK == 0 and hidden == width
    d = HEAD_DIM
    local_width = heads * d
    z, y, x, c = (lax.axis_index(name) for name in ("z", "y", "x", "c"))
    regular = g.regular(shard)
    meta = jnp.stack([c, (z * 2 + y) if regular else c * 0, x * 2 + c]).astype(jnp.int32)

    segments = lax.dynamic_index_in_dim(segment_ids, x, 0, keepdims=False)
    blocks = seq // BLOCK
    by_block = segments.reshape(blocks, BLOCK)
    lows = jnp.sum((segments[None, :] < by_block[:, :1]).astype(jnp.int32), axis=1) // BLOCK
    highs = (jnp.sum((segments[None, :] <= by_block[:, -1:]).astype(jnp.int32), axis=1) + BLOCK - 1) // BLOCK
    seg_row = segments.reshape(blocks, 1, BLOCK)

    small = jnp.concatenate([up_bias, qv_bias.reshape(-1)]).reshape(1, -1)
    small = jnp.concatenate([small, g.swap(small, "x")], axis=0)
    small = jnp.stack([small, g.swap(small, "c")], axis=1).reshape(4, -1).astype(F32)
    hidden_bias = small[:, :hidden].reshape(1, 4 * hidden)
    pair_bias = small[:, hidden:].reshape(2, 2, 2, heads, d)[:, 0].transpose(1, 2, 0, 3)
    pair_bias = pair_bias.reshape(2, heads * PAIR)
    vectors = jnp.stack(
        [out_bias, first_gain, first_shift, down_bias, second_gain, second_shift, out_bias, out_bias]
    ).astype(F32)

    parts = []
    for j in range(heads):
        at = slice(j * d, (j + 1) * d)
        parts += [qkv_weight[:, n, at] for n in range(3)]
    parts.append(jnp.zeros((shard, -3 * local_width % 128), BF16))
    head_weights = Gather(g, jnp.concatenate(parts, axis=1))
    rest = jnp.zeros((shard, -local_width % 128), BF16)
    rest = jnp.concatenate([up_weight, after(down_weight, head_weights.shard), out_weight, rest], axis=1)
    both = gather_everywhere(g, rest)
    other_tokens = g.swap(tokens, "c")
    head_weights.line()
    head_weights.wait("lines", small)
    (token_t,) = call(
        transpose_tokens,
        [shape_of((width, seq), BF16)],
        [meta, tokens, other_tokens],
        in_specs=[SMEM, VMEM, VMEM],
        name="transpose_tokens",
        vmem=16,
    )
    head_weights.first(token_t)
    head_weights.second()

    lanes = heads * PAIR
    blocks = seq // BLOCK
    count = len(head_weights.arrays)
    q, k, v, w, ctx_own, ctx_send, lse = call(
        partial(heads_forward, head_weights.entries, count),
        [shape_of((seq, lanes), BF16)] * 3
        + [shape_of((width, 3 * lanes), BF16)]
        + [shape_of((rows, lanes), BF16)] * 2
        + [shape_of((blocks, 8, BLOCK), F32)],
        [meta, lows, highs, *head_weights.arrays, tokens, other_tokens, pair_bias, seg_row],
        in_specs=[SMEM] * 3 + [ANY] * count + [VMEM] * 4,
        scratch=[
            pltpu.VMEM((2, width, head_weights.shard.shape[1]), BF16),
            pltpu.VMEM((2 * heads, SUMMED, seq), BF16),
            pltpu.VMEM((2 * heads, BLOCK, PAIR), BF16),
            pltpu.VMEM((2 * heads, BLOCK, BLOCK), BF16),
            pltpu.VMEM((seq, 1), jnp.int32),
            pltpu.SemaphoreType.DMA((len(head_weights.entries),)),
        ],
        flops=2 * seq * width * 3 * lanes + 4 * seq * seq * lanes,
        name="heads_forward",
        vmem=VM_HEADS,
    )
    ctx_other = g.swap(ctx_send, "c")

    def by_rows(lanes):
        return pl.BlockSpec((ROW_BLOCK, lanes), lambda i: (i, 0))

    def by_columns(array_rows):
        return pl.BlockSpec((array_rows, ROW_BLOCK), lambda i: (0, i))

    def fixed(array):
        return pl.BlockSpec(array.shape, lambda i: (0,) * len(array.shape))

    ffn = 2 * rows * width * 4 * hidden
    sums_shape = shape_of((8, width), F32)
    bias_shape = shape_of((8, 4 * hidden), F32)
    weight_sems = pltpu.SemaphoreType.DMA((both.shape[0] * both.shape[1],))
    output, dr1, da, act, du, df_t, low_t, sums_rows, hidden_sums, wo = call(
        rows_step,
        [
            shape_of((rows, width), BF16),
            shape_of((rows, width), F32),
            shape_of((rows, width), BF16),
            shape_of((rows, 4 * hidden), BF16),
            shape_of((rows, 4 * hidden), BF16),
            shape_of((width, rows), BF16),
            shape_of((width, rows), BF16),
            sums_shape,
            bias_shape,
            shape_of((width, lanes), BF16),
        ],
        [meta, both, tokens, vectors, ctx_own, ctx_other, hidden_bias, output_grad],
        in_specs=[SMEM, ANY, by_rows(width), fixed(vectors), by_rows(lanes), by_rows(lanes)]
        + [fixed(hidden_bias), by_rows(width)],
        out_specs=[by_rows(width)] * 3
        + [by_rows(4 * hidden)] * 2
        + [by_columns(width)] * 2
        + [fixed(sums_shape), fixed(bias_shape), pl.BlockSpec((width, lanes), lambda i: (0, 0))],
        scratch=[
            pltpu.VMEM((width, width), BF16),
            pltpu.VMEM((4, width, both.shape[3]), BF16),
            pltpu.VMEM((ROW_BLOCK, 4 * hidden), F32),
            weight_sems,
        ],
        grid=(rows // ROW_BLOCK,),
        flops=4 * ffn + 2 * rows * width * width,
        name="rows_step",
        vmem=VM_ROWS,
    )
    other_da = g.swap(da, "c")
    tiles = hidden // BLOCK
    left_spec = pl.BlockSpec((width, rows), lambda i: (0, 0))

    def right_specs(places):
        return [pl.BlockSpec((rows, BLOCK), lambda i, t=t: (0, t * tiles + i)) for t in places] * 2

    partner_spec = pl.BlockSpec((2, width, BLOCK), lambda i: (0, 0, i))
    for_partner = call(
        grad_for_partner,
        [shape_of((2, width, hidden), BF16)] * 2,
        [df_t, low_t, act, act, du, du],
        in_specs=[left_spec] * 2 + right_specs((1, 3)),
        out_specs=[partner_spec] * 2,
        grid=(tiles,),
        flops=ffn,
        name="grad_for_partner",
        vmem=VM_PART,
    )
    dctx, delta, out_grad = call(
        heads_back_start,
        [shape_of((seq, lanes), BF16), shape_of((blocks, 8, BLOCK), F32), shape_of((width, lanes), F32)],
        [meta, da, other_da, ctx_own, ctx_send, wo],
        in_specs=[SMEM] + [VMEM] * 5,
        scratch=[pltpu.VMEM((width, rows), BF16)],
        flops=4 * seq * width * lanes,
        name="heads_back_start",
        vmem=VM_START,
    )
    received = [g.swap(a, "c") for a in after(for_partner, other_da)]
    leaving = Scatter.shapes(g, shard, hidden, weights=2)
    ffn_grad = Scatter(
        g,
        shard,
        call(
            partial(grad_for_chip, g.nz),
            leaving,
            [meta, after(df_t, dctx), low_t, act, act, du, du, *received],
            in_specs=[SMEM] + [left_spec] * 2 + right_specs((0, 2)) + [partner_spec] * 2,
            out_specs=[
                pl.BlockSpec((*a.shape[:-1], BLOCK), lambda i, n=len(a.shape) - 1: (0,) * n + (i,)) for a in leaving
            ],
            scratch=[pltpu.VMEM((2, 2, leaving[0].shape[-2], BLOCK), BF16)],
            grid=(tiles,),
            flops=ffn,
            name="grad_for_chip",
            vmem=VM_GRAD,
        ),
    )

    def attend_back(first, last, dctx, *dq):
        return call(
            partial(attention_backward, first, last, len(dq)),
            [shape_of((heads, PAIR, seq), F32), shape_of(((last - first) * BLOCK, 2 * lanes), BF16)],
            [meta, lows, highs, q, k, v, dctx, lse, delta, seg_row, *dq],
            in_specs=[SMEM] * 3 + [VMEM] * (7 + len(dq)),
            scratch=[pltpu.VMEM((2 * heads, BLOCK, PAIR), F32)] * 2 + [pltpu.VMEM((2 * heads, BLOCK, BLOCK), BF16)] * 2,
            flops=5 * seq * seq * lanes,
            name="attention_backward",
            vmem=VM_BACK,
        )

    dq_t, dkv_one = attend_back(0, blocks // 2, after(dctx, ffn_grad.arrays))
    ffn_away = ffn_grad.first(dkv_one)
    dq_t, dkv_two = attend_back(blocks // 2, blocks, after(dctx, ffn_away), dq_t)
    ffn_second = ffn_grad.second(dkv_two)

    six = sums_rows[:6]
    six = six + g.swap(six, "c")
    hidden_sums = hidden_sums[0].reshape(2, 2, hidden)
    hidden_sums = hidden_sums[:, 0] + g.swap(hidden_sums[:, 1], "c")
    vector = jnp.concatenate([jnp.stack([six, six]), hidden_sums[:, None]], axis=1)
    *arrays, vector, dqkv = call(
        partial(projection_grad, g.nz),
        Scatter.shapes(g, shard, 2 * lanes, SPARE) + [shape_of((2, 8, width), F32), shape_of((seq, 3 * lanes), BF16)],
        [meta, token_t, out_grad, after(dq_t, ffn_second), dkv_one, dkv_two, vector],
        in_specs=[SMEM] + [VMEM] * 6,
        scratch=[pltpu.VMEM((2, width // 2, 2 * lanes), BF16)],
        flops=2 * seq * width * 3 * lanes,
        name="projection_grad",
        vmem=VM_PROJ,
    )
    head_grad = Scatter(g, shard, arrays, (vector[0], vector[1]))
    ffn_parts = ffn_grad.third(arrays)
    ffn_share = ffn_parts[0] + sum(part.astype(F32) for part in ffn_parts[1:])
    (ig_other,) = call(
        input_grad_other,
        [shape_of((rows, width), BF16)],
        [meta, dqkv, w],
        in_specs=[SMEM] + [VMEM] * 2,
        flops=seq * width * 3 * lanes,
        name="input_grad_other",
        vmem=VM_PROJ,
    )
    head_away = head_grad.first((ffn_share, ig_other))
    ig_arrived = g.swap(after(ig_other, head_away), "c")
    (input_grad,) = call(
        input_grad_own,
        [shape_of((rows, width), F32)],
        [meta, dqkv, w, dr1, ig_arrived],
        in_specs=[SMEM] + [VMEM] * 4,
        flops=seq * width * 3 * lanes,
        name="input_grad_own",
        vmem=VM_PROJ,
    )
    head_grad.second(input_grad)
    down_share, up_share = ffn_share[0], ffn_share[1]
    parts = head_grad.third()
    if regular:
        qkv_share, out_share, vectors_grad, up_bias_share, qv_share = call(
            partial(finish_heads, len(parts) - 2),
            [shape_of((3, shard, local_width), F32), shape_of((shard, local_width), F32), shape_of((6, width), F32)]
            + [shape_of((1, width), F32), shape_of((2, local_width), F32)],
            parts,
            name="finish_heads",
            vmem=SUM_VMEM,
        )
    else:
        shares, summed = parts
        shares = shares.reshape(shard, heads, 4, d).transpose(2, 0, 1, 3).reshape(4, shard, local_width)
        qkv_share, out_share = shares[:3], shares[3]
        vectors_grad, up_bias_share = summed[:6], summed[6:7]
        qv_share = summed[7, : 2 * local_width].reshape(2, local_width)
    qkv_share = qkv_share.transpose(1, 0, 2)
    up_bias_share = up_bias_share.reshape(-1)
    return (output, input_grad, qkv_share, qv_share, out_share, up_share, up_bias_share, down_share, vectors_grad)


def solution(mesh):
    g = Grid(mesh)
    dp, tensor = ("z", "y"), ("x", "c")
    rows = P(dp + tensor, None)
    in_specs = (
        rows,
        P(dp, None),
        P(dp, None, tensor),
        P(None, tensor),
        P(dp, tensor),
        P(),
        P(),
        P(),
        P(dp, tensor),
        P(tensor),
        P(dp, tensor),
        P(),
        P(),
        P(),
        rows,
    )
    out_specs = (
        rows,
        rows,
        P(dp, None, tensor),
        P(None, tensor),
        P(dp, tensor),
        P(dp, tensor),
        P(tensor),
        P(dp, tensor),
        P(),
    )
    return jax.shard_map(partial(local, g), mesh=g.mesh, in_specs=in_specs, out_specs=out_specs, check_vma=False)
```

```python
from functools import partial

import jax
import jax.numpy as jnp
from jax import lax
from jax.experimental import pallas as pl
from jax.experimental.pallas import tpu as pltpu
from jax.sharding import Mesh
from jax.sharding import PartitionSpec as P

HEAD_DIM = 64
PAIR = 2 * HEAD_DIM
EPSILON = 1e-12
MASKED = -1e30
BLOCK = 256
ROW_BLOCK = 256
F32 = jnp.float32
BF16 = jnp.bfloat16
MIB = 1 << 20
COST = 1


def dot_nn(left, right):
    return jnp.dot(left, right, preferred_element_type=F32)


def dot_nt(left, right):
    return lax.dot_general(left, right, (((1,), (1,)), ((), ())), preferred_element_type=F32)


def call(body, outs, ins, in_specs=None, out_specs=None, scratch=(), grid=(), flops=0, name=None, vmem=60, alias=None):
    moved = sum(a.size * a.dtype.itemsize for a in ins) + sum(o.size * o.dtype.itemsize for o in outs)
    return pl.pallas_call(
        body,
        grid=grid,
        out_shape=outs,
        in_specs=in_specs or [VMEM] * len(ins),
        out_specs=out_specs or [VMEM] * len(outs),
        scratch_shapes=list(scratch),
        compiler_params=pltpu.CompilerParams(vmem_limit_bytes=vmem * MIB),
        cost_estimate=pl.CostEstimate(flops=int(flops) // COST, bytes_accessed=int(moved) // COST, transcendentals=0),
        input_output_aliases=alias or {},
        name=name,
    )(*ins)


ANY = pl.BlockSpec(memory_space=pl.ANY)
SMEM = pl.BlockSpec(memory_space=pltpu.SMEM)
VMEM = pl.BlockSpec(memory_space=pltpu.VMEM)


def shape_of(shape, dtype):
    return jax.ShapeDtypeStruct(shape, dtype)


def after(values, done):
    return lax.optimization_barrier((values, done))[0]


class Grid:
    def __init__(self, mesh):
        n_dp, n_tensor = mesh.devices.shape
        assert n_tensor == 4 and n_dp % 2 == 0
        self.nz = n_dp // 2
        self.n_dp = n_dp
        self.mesh = Mesh(mesh.devices.reshape(self.nz, 2, 2, 2), ("z", "y", "x", "c"))

    def swap(self, array, axis, r=1):
        size = self.nz if axis == "z" else 2
        return lax.ppermute(array, axis, [(i, i ^ r) for i in range(size)])

    def regular(self, rows):
        return rows % 32 == 0 and self.nz & (self.nz - 1) == 0

    def total_dp(self, array):
        if self.nz & (self.nz - 1):
            return lax.psum(array, ("z", "y"))
        array = array + self.swap(array, "y")
        r = 1
        while r < self.nz:
            array = array + self.swap(array, "z", r)
            r *= 2
        return array


class Gather:
    def __init__(self, g, shard):
        self.g, self.shard, self.rows = g, shard, shard.shape[0]
        self.regular = g.regular(self.rows)

    def line(self):
        g, half = self.g, self.rows // 2
        if not self.regular:
            full = lax.all_gather(self.shard, ("z", "y"), axis=0, tiled=True)[None, None]
            self.arrays = [full, g.swap(full, "x")]
            self.entries = [(n, 0, 0, n, 0, 0, full.shape[2]) for n in range(2)]
            return self.arrays
        near = [self.shard] + [g.swap(self.shard, "z", r) for r in range(1, g.nz)]
        self.lines = [jnp.stack([part[:half] for part in near]), jnp.stack([part[half:] for part in near])]
        return self.lines

    def wait(self, step, done):
        if self.regular:
            setattr(self, step, after(getattr(self, step), done))

    def first(self, done=()):
        if not self.regular:
            return self.arrays
        arrived = after([self.g.swap(line, axis) for line, axis in zip(self.lines, "xy")], done)
        self.twos = [jnp.stack([line, other]) for line, other in zip(self.lines, arrived)]
        return arrived

    def second(self):
        if not self.regular:
            return self.arrays
        half = self.rows // 2
        self.arrays, self.entries = [], []
        for number, axis in enumerate("xy"):
            two = self.twos[number]
            four = self.g.swap(two, "yx"[number])
            for index, array in ((0, two), (1, four)):
                for i in range(2):
                    rx, ry = (i, index) if axis == "x" else (index, i)
                    for k in range(self.g.nz):
                        self.entries.append((len(self.arrays), i, k, rx, k * 2 + ry, number * half, half))
                self.arrays.append(array)
        return self.arrays


def load_pieces(entries, refs, index, target, sems, lanes):
    slots = 1 + max(entry[4] for entry in entries)
    copies = []
    for number, (a, i, k, place, slot, first, size) in enumerate(entries):
        row = pl.multiple_of((slot ^ index) * (target.shape[1] // slots) + first, 16)
        copies.append(
            pltpu.make_async_copy(refs[a].at[i, k, :, lanes], target.at[place, pl.ds(row, size)], sems.at[number])
        )
    for copy in copies:
        copy.start()
    for copy in copies:
        copy.wait()


def gather_everywhere(g, shard):
    if g.regular(shard.shape[0]):
        full = lax.all_gather(shard, ("z", "y", "x", "c"), axis=0)
        return full.reshape(g.n_dp, 4, *shard.shape)
    full = lax.all_gather(shard, ("z", "y"), axis=0, tiled=True)
    return lax.all_gather(full, ("x", "c"), axis=0)[None]


def everywhere_copies(source, me, target, sems, lanes):
    blocks, places, rows = source.shape[:3]
    return [
        pltpu.make_async_copy(
            source.at[block, t, :, lanes],
            target.at[t ^ me, pl.ds(block * rows, rows), lanes],
            sems.at[block * places + t],
        )
        for block in range(blocks)
        for t in range(places)
    ]


SPARE = 16


class Scatter:
    def __init__(self, g, rows, arrays, vector=None):
        self.g, self.rows = g, rows
        self.regular = g.regular(rows)
        self.arrays = arrays
        self.vector = vector

    @staticmethod
    def shapes(g, rows, lanes, spare=0, weights=None):
        lead = () if weights is None else (weights,)
        if not g.regular(rows):
            return [shape_of((*lead, 2, rows * g.n_dp, lanes), BF16)]
        size = 2 * g.nz * rows // 2
        block = shape_of((*lead, size, lanes), BF16)
        return [block, shape_of((*lead, size + spare, lanes), BF16), block, block]

    def first(self, done=()):
        g = self.g
        if not self.regular:
            (whole,) = self.arrays
            both = whole[..., 0, :, :].astype(F32) + g.swap(whole[..., 1, :, :], "x").astype(F32)
            self.sum = lax.psum_scatter(both, ("z", "y"), scatter_dimension=both.ndim - 2, tiled=True)
            if self.vector is not None:
                self.vector = lax.psum(self.vector[0] + g.swap(self.vector[1], "x"), ("z", "y"))
            return [self.sum]
        keep_x, send_x, keep_y, send_y = self.arrays
        self.got = after([g.swap(send_x, "x"), g.swap(send_y, "y")], done)
        lead, half, lanes = keep_x.shape[:-2], keep_x.shape[-2] // 2, keep_x.shape[-1]
        outs, ins = [shape_of((*lead, half, lanes), BF16)] * 2, [keep_x, self.got[0], keep_y, self.got[1]]
        if self.vector is not None:
            outs = [shape_of((half + SPARE, lanes), BF16), outs[1], shape_of((SPARE // 2, lanes), F32)]
            ins.append(self.vector[0])
        self.away = call(sum_away, outs, ins, name="sum_away", vmem=SUM_VMEM)
        return self.away

    def second(self, done=()):
        if not self.regular:
            return [self.sum]
        g = self.g
        seconds = after([g.swap(self.away[0], "y"), g.swap(self.away[1], "x")], done)
        lead, lanes = self.away[1].shape[:-2], self.away[1].shape[-1]
        outs = [shape_of((*lead, self.rows, lanes), F32)]
        ins = [self.arrays[0], self.got[0], seconds[0], self.arrays[2], self.got[1], seconds[1]]
        far_rows = self.rows
        if self.vector is not None:
            outs.append(shape_of((SPARE // 2, lanes), F32))
            ins.append(self.away[2])
            far_rows += SPARE
        outs += [shape_of((*lead, far_rows, lanes), BF16)] * (g.nz - 1)
        self.line = call(partial(sum_line, g.nz), outs, ins, name="sum_line", vmem=SUM_VMEM)
        return self.line

    def third(self, done=()):
        if not self.regular:
            return [self.sum] if self.vector is None else [self.sum, self.vector]
        count = 1 if self.vector is None else 2
        arrived = [self.g.swap(far, "z", r + 1) for r, far in enumerate(self.line[count:])]
        return [*self.line[:count], *after(arrived, done)]


SUM_VMEM = 12
VM_HEADS = 60
VM_ROWS = 60
VM_GRAD = 40
VM_PART = 60
VM_START = 60
VM_BACK = 36
VM_PROJ = 36


def split_in_two(value):
    high = value.astype(BF16)
    return jnp.concatenate([high, (value - high.astype(F32)).astype(BF16)], axis=0)


def join_two(ref):
    spare = ref[ref.shape[0] - SPARE :, :].astype(F32)
    return spare[: SPARE // 2] + spare[SPARE // 2 :]


def sum_away(keep_x, got_x, keep_y, got_y, *refs):
    half = keep_x.shape[-2] // 2
    if len(refs) == 4:
        vector, out_x, out_y, vector_out = refs
        total = vector[...] + join_two(got_x)
        vector_out[...] = total
        out_x[half:, :] = split_in_two(total)
    else:
        out_x, out_y = refs
    for keep, got, out in ((keep_x, got_x, out_x), (keep_y, got_y, out_y)):
        away = keep[..., half:, :].astype(F32) + got[..., half : 2 * half, :].astype(F32)
        out[..., :half, :] = away.astype(BF16)


def sum_line(nz, keep_x, got_x, last_x, keep_y, got_y, last_y, *refs):
    size = keep_x.shape[-2] // (2 * nz)
    if len(refs) > nz:
        vector, near, vector_out, *far = refs
        total = vector[...] + join_two(last_x)
        vector_out[...] = total
        parts = split_in_two(total)
        for out in far:
            out[2 * size :, :] = parts
    else:
        near, *far = refs
    for n, (keep, got, last) in enumerate(((keep_x, got_x, last_x), (keep_y, got_y, last_y))):
        for r in range(nz):
            at = slice(r * size, (r + 1) * size)
            total = keep[..., at, :].astype(F32) + got[..., at, :].astype(F32) + last[..., at, :].astype(F32)
            out = far[r - 1] if r else near
            out[..., n * size : (n + 1) * size, :] = total.astype(out.dtype)


def store_blocks(value, outs, stage, place, index, nz):
    value = value.astype(BF16)
    if len(outs) == 1:
        outs[0][place] = value
        return
    by_x = outs[place]
    half = stage.shape[1] // (2 * nz)
    for block in range(value.shape[0] // (2 * half)):
        slot = block ^ index
        ry, rz = lax.rem(slot, 2), lax.div(slot, 2)
        row = pl.multiple_of((ry * nz + rz) * half, 16)
        by_x[pl.ds(row, half), :] = value[2 * block * half : (2 * block + 1) * half]
        row = pl.multiple_of((place * nz + rz) * half, 16)
        stage[ry, pl.ds(row, half), :] = value[(2 * block + 1) * half : (2 * block + 2) * half]
    if place == 1:
        outs[2][...] = stage[0]
        outs[3][...] = stage[1]


SUMMED = HEAD_DIM + 16


def heads_forward(entries, count, meta, lows, highs, *refs):
    pieces = refs[:count]
    own, other, bias, seg_row = refs[count : count + 4]
    q, k, v, w_out, ctx_own, ctx_other, lse = refs[count + 4 : count + 11]
    weights, v_t, q_masked, powers, seg_col, sems = refs[count + 11 :]
    rows = own.shape[0]
    core = meta[0]
    load_pieces(entries, pieces, meta[1], weights, sems, slice(None))
    d = HEAD_DIM
    width = q.shape[1]
    pairs = width // PAIR
    for j in range(pairs):
        for kind in range(3):
            at = slice((3 * j + kind) * d, (3 * j + kind + 1) * d)
            pair = jnp.concatenate([weights[0][:, at], weights[1][:, at]], axis=1)
            w_out[:, kind * width + j * PAIR : kind * width + (j + 1) * PAIR] = pair
    ones = jnp.ones((SUMMED - d, BLOCK), BF16)
    for source, base in ((own, core * rows), (other, (1 - core) * rows)):

        def project(n, carry):
            at = pl.ds(pl.multiple_of(base + n * BLOCK, BLOCK), BLOCK)
            block = source[pl.ds(pl.multiple_of(n * BLOCK, BLOCK), BLOCK), :]
            all_three = dot_nn(block, w_out[...])
            query = (all_three[:, :width] + bias[0:1, :]).astype(BF16)
            q[at, :] = (query.astype(F32) * d**-0.5).astype(BF16)
            k[at, :] = all_three[:, width : 2 * width].astype(BF16)
            values = (all_three[:, 2 * width :] + bias[1:2, :]).astype(BF16)
            v[at, :] = values
            for p in range(pairs):
                columns = values[:, p * PAIR : (p + 1) * PAIR].T
                for h in range(2):
                    v_t[2 * p + h, :d, at] = columns[h * d : (h + 1) * d]
                    v_t[2 * p + h, d:, at] = ones
            return carry

        lax.fori_loop(0, rows // BLOCK, project, 0)
    left = lax.broadcasted_iota(jnp.int32, (BLOCK, PAIR), 1) < d
    half = rows // BLOCK
    for b in range(2 * half):
        seg_col[b * BLOCK : (b + 1) * BLOCK, :] = column_of(seg_row[b])

    def query_block(i, carry):
        at = pl.ds(pl.multiple_of(i * BLOCK, BLOCK), BLOCK)
        seg_q = seg_row[i]
        for p in range(pairs):
            query = q[at, p * PAIR : (p + 1) * PAIR].astype(F32)
            q_masked[2 * p] = jnp.where(left, query, 0.0).astype(BF16)
            q_masked[2 * p + 1] = jnp.where(left, 0.0, query).astype(BF16)

        def key_block(b, carry):
            tops, sums = carry
            rows = pl.ds(pl.multiple_of(b * BLOCK, BLOCK), BLOCK)
            same = seg_col[rows, :] == seg_q
            new_tops, new_sums = [], []
            for h in range(2 * pairs):
                s = dot_nt(k[rows, (h // 2) * PAIR : (h // 2 + 1) * PAIR], q_masked[h])
                s = jnp.where(same, s, MASKED)
                top = jnp.maximum(tops[h], jnp.max(s, axis=0, keepdims=True))
                powers[h] = jnp.exp(s - top).astype(BF16)
                new_tops.append(top)
            for h in range(2 * pairs):
                scale = jnp.exp(tops[h] - new_tops[h])
                new_sums.append(sums[h] * scale + dot_nn(v_t[h, :, rows], powers[h]))
            return tuple(new_tops), tuple(new_sums)

        first_top = jnp.full((1, BLOCK), MASKED, F32)
        first_sum = jnp.zeros((SUMMED, BLOCK), F32)
        tops, sums = lax.fori_loop(
            lows[i], highs[i], key_block, ((first_top,) * (2 * pairs), (first_sum,) * (2 * pairs))
        )
        for p in range(pairs):
            parts = []
            for h in (2 * p, 2 * p + 1):
                total = sums[h][d : d + 1, :]
                lse[i, h : h + 1, :] = tops[h] + jnp.log(total)
                parts.append(sums[h][:d, :] / total)
            ctx = jnp.concatenate(parts, axis=0).T.astype(BF16)
            lanes = slice(p * PAIR, (p + 1) * PAIR)
            own_half = lax.div(i, half) == core
            within = pl.ds(pl.multiple_of(lax.rem(i, half) * BLOCK, BLOCK), BLOCK)

            @pl.when(own_half)
            def _():
                ctx_own[within, lanes] = ctx

            @pl.when(jnp.logical_not(own_half))
            def _():
                ctx_other[within, lanes] = ctx

        return carry

    lax.fori_loop(0, 2 * half, query_block, 0)


def heads_back_start(meta, da_own, da_other, ctx_own, ctx_other, wo, dctx, delta, out_grad, left_t):
    rows = da_own.shape[0]
    core = meta[0]
    d = HEAD_DIM
    pairs = ctx_own.shape[1] // PAIR
    for source, values, base in ((da_own, ctx_own, core * rows), (da_other, ctx_other, (1 - core) * rows)):

        def context_grad(n, carry):
            here = pl.ds(pl.multiple_of(n * BLOCK, BLOCK), BLOCK)
            at = pl.ds(pl.multiple_of(base + n * BLOCK, BLOCK), BLOCK)
            block = base // BLOCK + n
            left_t[:, here] = source[here, :].T
            grads = dot_nn(source[here, :], wo[...]).astype(BF16)
            dctx[at, :] = grads
            for p in range(pairs):
                lanes = slice(p * PAIR, (p + 1) * PAIR)
                prod = (grads[:, lanes].astype(F32) * values[here, lanes].astype(F32)).T
                delta[block, 2 * p : 2 * p + 1, :] = jnp.sum(prod[:d], axis=0, keepdims=True)
                delta[block, 2 * p + 1 : 2 * p + 2, :] = jnp.sum(prod[d:], axis=0, keepdims=True)
            return carry

        lax.fori_loop(0, rows // BLOCK, context_grad, 0)
        part = dot_nn(left_t[...], values[...])
        if source is da_own:
            out_grad[...] = part
        else:
            out_grad[...] += part


def attention_backward(first, last, given, meta, lows, highs, q, k, v, dctx, lse, delta, seg_row, *refs):
    dq_in, (dq_t, dkv, dk_sum, dv_sum, powers, slopes) = refs[:given], refs[given:]
    d = HEAD_DIM
    width = q.shape[1]
    pairs = width // PAIR
    left = lax.broadcasted_iota(jnp.int32, (BLOCK, PAIR), 1) < d
    dq_t[...] = dq_in[0][...] if given else jnp.zeros_like(dq_t)

    def key_block(b, carry):
        at = pl.ds(pl.multiple_of(b * BLOCK, BLOCK), BLOCK)
        seg_k = column_of(seg_row[b])
        dk_sum[...] = jnp.zeros_like(dk_sum)
        dv_sum[...] = jnp.zeros_like(dv_sum)
        keys, values, keys_t = [], [], []
        for p in range(pairs):
            lanes = slice(p * PAIR, (p + 1) * PAIR)
            key, value = k[at, lanes].astype(F32), v[at, lanes].astype(F32)
            keys += [jnp.where(left, key, 0.0).astype(BF16), jnp.where(left, 0.0, key).astype(BF16)]
            values += [jnp.where(left, value, 0.0).astype(BF16), jnp.where(left, 0.0, value).astype(BF16)]
            keys_t.append(k[at, lanes].T)

        def query_block(i, carry):
            rows_q = pl.ds(pl.multiple_of(i * BLOCK, BLOCK), BLOCK)
            same = seg_k == seg_row[i]
            for h in range(2 * pairs):
                lanes = slice((h // 2) * PAIR, (h // 2 + 1) * PAIR)
                s = jnp.where(same, dot_nt(keys[h], q[rows_q, lanes]), MASKED)
                p = jnp.exp(s - lse[i, h : h + 1, :])
                dp = dot_nt(values[h], dctx[rows_q, lanes])
                powers[h] = p.astype(BF16)
                slopes[h] = (p * (dp - delta[i, h : h + 1, :])).astype(BF16)
            for h in range(2 * pairs):
                p, half = h // 2, slice((h % 2) * d, (h % 2 + 1) * d)
                lanes = slice(p * PAIR, (p + 1) * PAIR)
                dv_sum[h] += dot_nn(powers[h], dctx[rows_q, lanes])
                dk_sum[h] += dot_nn(slopes[h], q[rows_q, lanes])
                dq_t[p, half, rows_q] += dot_nn(keys_t[p][half, :], slopes[h])
            return carry

        lax.fori_loop(lows[b], highs[b], query_block, 0)
        for p in range(pairs):
            for n, total in ((1, dk_sum), (2, dv_sum)):
                value = jnp.where(left, total[2 * p], total[2 * p + 1])
                here = pl.ds(pl.multiple_of((b - first) * BLOCK, BLOCK), BLOCK)
                dkv[here, (n - 1) * width + p * PAIR : (n - 1) * width + (p + 1) * PAIR] = value.astype(BF16)
        return carry

    lax.fori_loop(first, last, key_block, 0)


def column_of(row):
    return jnp.broadcast_to(row.astype(F32), (128, BLOCK)).T[:, 0:1].astype(jnp.int32)


def transpose_tokens(meta, own, other, out):
    rows = own.shape[0]
    for base, source in ((meta[0] * rows, own), ((1 - meta[0]) * rows, other)):
        for r in range(0, rows, BLOCK):
            out[:, pl.ds(pl.multiple_of(base + r, BLOCK), BLOCK)] = source[r : r + BLOCK, :].T


def projection_grad(nz, meta, token_t, out_grad, dq_t, dkv_one, dkv_two, sums_own, sums_other, *refs):
    outs, dqkv, stage = refs[:-2], refs[-2], refs[-1]
    d = HEAD_DIM
    seq = token_t.shape[1]
    width = out_grad.shape[1]

    def join(n, total):
        at = pl.ds(pl.multiple_of(n * BLOCK, BLOCK), BLOCK)
        for p in range(width // PAIR):
            dqkv[at, p * PAIR : (p + 1) * PAIR] = (dq_t[p, :, at].T * d**-0.5).astype(BF16)
        return total + column_sum(dqkv[at, :width].astype(F32))

    dqkv[: seq // 2, width:] = dkv_one[...]
    dqkv[seq // 2 :, width:] = dkv_two[...]
    q_sum = lax.fori_loop(0, seq // BLOCK, join, jnp.zeros((1, width), F32))
    v_sum = column_sum(dkv_one[:, width:].astype(F32)) + column_sum(dkv_two[:, width:].astype(F32))
    full = dot_nn(token_t[...], dqkv[...])
    vectors = []
    for place in range(2):
        lanes, biases = [], []
        for j in range(width // PAIR):
            at = j * PAIR + place * d
            lanes += [full[:, n * width + at : n * width + at + d] for n in range(3)] + [out_grad[:, at : at + d]]
        store_blocks(jnp.concatenate(lanes, axis=1), outs[:-1], stage, place, meta[1], nz)
        for total in (q_sum, v_sum):
            biases += [total[:, j * PAIR + place * d : j * PAIR + (place + 1) * d] for j in range(width // PAIR)]
        biases.append(jnp.zeros((1, sums_own.shape[1] - len(biases) * d), F32))
        hidden = sums_own[8 + 2 * place : 9 + 2 * place, :] + sums_other[9 + 2 * place : 10 + 2 * place, :]
        vectors.append(jnp.concatenate([sums_own[:6, :] + sums_other[:6, :], hidden, jnp.concatenate(biases, axis=1)], axis=0))
    outs[-1][0] = vectors[0]
    outs[-1][1] = vectors[1]
    if len(outs) > 2:
        outs[1][outs[0].shape[0] :, :] = split_in_two(vectors[1])


def input_grad_other(meta, dqkv, w, out):
    rows = out.shape[0]
    base = (1 - meta[0]) * rows
    for r in range(0, rows, BLOCK):
        at = pl.ds(pl.multiple_of(base + r, BLOCK), BLOCK)
        out[r : r + BLOCK, :] = dot_nt(dqkv[at, :], w[...]).astype(BF16)


def input_grad_own(meta, dqkv, w, dr1, arrived, out):
    rows = out.shape[0]
    base = meta[0] * rows
    for r in range(0, rows, BLOCK):
        at = pl.ds(pl.multiple_of(base + r, BLOCK), BLOCK)
        here = slice(r, r + BLOCK)
        out[here, :] = dot_nt(dqkv[at, :], w[...]) + dr1[here, :] + arrived[here, :].astype(F32)


def finish_heads(count, near, vector, *refs):
    arrived, (qkv_out, out_out, six_out, hidden_out, head_out) = refs[:count], refs[count:]
    total, sums = near[...], vector[...]
    rows = total.shape[0]
    for part in arrived:
        total = total + part[:rows, :].astype(F32)
        sums = sums + join_two(part)
    d = HEAD_DIM
    heads = total.shape[1] // (4 * d)
    for kind in range(4):
        value = jnp.concatenate([total[:, (4 * j + kind) * d : (4 * j + kind + 1) * d] for j in range(heads)], axis=1)
        if kind == 3:
            out_out[...] = value
        else:
            qkv_out[kind] = value
    lanes = heads * d
    six_out[...] = sums[:6]
    hidden_out[...] = sums[6:7]
    head_out[0:1, :] = sums[7:8, :lanes]
    head_out[1:2, :] = sums[7:8, lanes : 2 * lanes]


def normalize(values):
    center = jnp.mean(values, axis=-1, keepdims=True)
    offset = values - center
    inverse = lax.rsqrt(jnp.mean(offset * offset, axis=-1, keepdims=True) + EPSILON)
    return offset * inverse, inverse


def normalize_back(incoming, normed, inverse, gain):
    weighted = incoming * gain
    centered = weighted - jnp.mean(weighted, axis=-1, keepdims=True)
    centered = centered - normed * jnp.mean(weighted * normed, axis=-1, keepdims=True)
    return centered * inverse


def column_sum(values):
    return jnp.sum(values, axis=0, keepdims=True)


def rows_step(
    meta, everywhere, tokens, vectors, ctx_own, ctx_other, bias, out_grad,
    output, dr1_out, da_out, act_out, du_out, df_t, low_t, sums, wo_own,
    w_out, w_all, slope, sems_out, sems,
):
    hidden = tokens.shape[1]
    half = ctx_own.shape[1]
    copies_out = everywhere_copies(everywhere, meta[2], w_all, sems_out, slice(2 * hidden, None))
    copies = everywhere_copies(everywhere, meta[2], w_all, sems, slice(0, 2 * hidden))
    w_up = w_all.at[:, :, :hidden]
    w_down = w_all.at[:, :, hidden : 2 * hidden]
    start = pl.program_id(0) == 0

    @pl.when(start)
    def _():
        for copy in copies_out + copies:
            copy.start()
        for copy in copies_out:
            copy.wait()
        d = HEAD_DIM
        for core in range(2):
            for j in range(half // PAIR):
                first = 2 * hidden + j * d
                pair = [w_all[2 * place + core, :, first : first + d] for place in range(2)]
                at = core * half + j * PAIR
                w_out[:, at : at + PAIR] = jnp.concatenate(pair, axis=1)
        wo_own[...] = w_out[:, :half]
        sums[...] = jnp.zeros_like(sums)

    out_bias, gain_one, shift_one, down_bias, gain_two, shift_two = (vectors[n : n + 1, :] for n in range(6))
    mixed = dot_nt(jnp.concatenate([ctx_own[...], ctx_other[...]], axis=1), w_out[...])
    normed_one, inverse_one = normalize(tokens[...].astype(F32) + mixed + out_bias)
    first = normed_one * gain_one + shift_one
    low = first.astype(BF16)
    low_t[...] = low.T

    @pl.when(start)
    def _():
        for copy in copies:
            copy.wait()

    for t in range(4):
        for n in range(0, hidden, BLOCK):
            at = slice(t * hidden + n, t * hidden + n + BLOCK)
            u = dot_nn(low, w_up[t, :, n : n + BLOCK]) + bias[:, at]
            share = 0.5 + 0.5 * lax.erf(u * 0.5**0.5)
            act_out[:, at] = (u * share).astype(BF16)
            slope[:, at] = share + u * (jnp.exp(-0.5 * u * u) * 0.3989422804014327)

    fed = first + down_bias
    for t in range(4):
        fed = fed + dot_nt(act_out[:, t * hidden : (t + 1) * hidden], w_down[t])
    normed, inverse = normalize(fed)
    output[...] = (normed * gain_two + shift_two).astype(BF16)
    incoming = out_grad[...].astype(F32)
    dr2 = normalize_back(incoming, normed, inverse, gain_two)
    df = dr2.astype(BF16)
    df_t[...] = df.T
    sums[3:4, :] += column_sum(df.astype(F32))
    sums[4:5, :] += column_sum(incoming * normed)
    sums[5:6, :] += column_sum(incoming)
    for t in range(4):
        for n in range(0, hidden, BLOCK):
            at = slice(t * hidden + n, t * hidden + n + BLOCK)
            du = (dot_nn(df, w_down[t, :, n : n + BLOCK]) * slope[:, at]).astype(BF16)
            du_out[:, at] = du
            sums[8 + t : 9 + t, n : n + BLOCK] += column_sum(du.astype(F32))
    incoming = dr2
    for t in range(4):
        incoming = incoming + dot_nt(du_out[:, t * hidden : (t + 1) * hidden], w_up[t])
    dr1 = normalize_back(incoming, normed_one, inverse_one, gain_one)
    dr1_out[...] = dr1
    da = dr1.astype(BF16)
    da_out[...] = da
    sums[0:1, :] += column_sum(da.astype(F32))
    sums[1:2, :] += column_sum(incoming * normed_one)
    sums[2:3, :] += column_sum(incoming)


def grad_for_partner(df_t, low_t, act_one, act_two, du_one, du_two, out_one, out_two):
    for out, act, du in ((out_one, act_one, du_one), (out_two, act_two, du_two)):
        out[0] = dot_nn(df_t[...], act[...]).astype(BF16)
        out[1] = dot_nn(low_t[...], du[...]).astype(BF16)


def grad_for_chip(nz, meta, df_t, low_t, act_one, act_two, du_one, du_two, received_one, received_two, *refs):
    outs, stage = refs[:-1], refs[-1]
    for n, left_t, rights in ((0, df_t, (act_one, act_two)), (1, low_t, (du_one, du_two))):
        for place, received in ((0, received_one), (1, received_two)):
            value = dot_nn(left_t[...], rights[place][...]) + received[n].astype(F32)
            store_blocks(value, [out.at[n] for out in outs], stage.at[n], place, meta[1], nz)


def local(
    g,
    tokens,
    segment_ids,
    qkv_weight,
    qv_bias,
    out_weight,
    out_bias,
    first_gain,
    first_shift,
    up_weight,
    up_bias,
    down_weight,
    down_bias,
    second_gain,
    second_shift,
    output_grad,
):
    rows, width = tokens.shape
    seq = segment_ids.shape[1]
    heads = qkv_weight.shape[2] // HEAD_DIM
    hidden = up_weight.shape[1]
    shard = qkv_weight.shape[0]
    assert seq == 2 * rows and rows % BLOCK == 0 and hidden == width
    d = HEAD_DIM
    local_width = heads * d
    z, y, x, c = (lax.axis_index(name) for name in ("z", "y", "x", "c"))
    regular = g.regular(shard)
    meta = jnp.stack([c, (z * 2 + y) if regular else c * 0, x * 2 + c]).astype(jnp.int32)

    segments = lax.dynamic_index_in_dim(segment_ids, x, 0, keepdims=False)
    blocks = seq // BLOCK
    by_block = segments.reshape(blocks, BLOCK)
    lows = jnp.sum((segments[None, :] < by_block[:, :1]).astype(jnp.int32), axis=1) // BLOCK
    highs = (jnp.sum((segments[None, :] <= by_block[:, -1:]).astype(jnp.int32), axis=1) + BLOCK - 1) // BLOCK
    seg_row = segments.reshape(blocks, 1, BLOCK)

    small = jnp.concatenate([up_bias, qv_bias.reshape(-1)]).reshape(1, -1)
    small = jnp.concatenate([small, g.swap(small, "x")], axis=0)
    small = jnp.stack([small, g.swap(small, "c")], axis=1).reshape(4, -1).astype(F32)
    hidden_bias = small[:, :hidden].reshape(1, 4 * hidden)
    pair_bias = small[:, hidden:].reshape(2, 2, 2, heads, d)[:, 0].transpose(1, 2, 0, 3)
    pair_bias = pair_bias.reshape(2, heads * PAIR)
    vectors = jnp.stack(
        [out_bias, first_gain, first_shift, down_bias, second_gain, second_shift, out_bias, out_bias]
    ).astype(F32)

    parts = []
    for j in range(heads):
        at = slice(j * d, (j + 1) * d)
        parts += [qkv_weight[:, n, at] for n in range(3)]
    parts.append(jnp.zeros((shard, -3 * local_width % 128), BF16))
    head_weights = Gather(g, jnp.concatenate(parts, axis=1))
    rest = jnp.zeros((shard, -local_width % 128), BF16)
    rest = jnp.concatenate([up_weight, after(down_weight, head_weights.shard), out_weight, rest], axis=1)
    both = gather_everywhere(g, rest)
    other_tokens = g.swap(tokens, "c")
    head_weights.line()
    head_weights.wait("lines", small)
    (token_t,) = call(
        transpose_tokens,
        [shape_of((width, seq), BF16)],
        [meta, tokens, other_tokens],
        in_specs=[SMEM, VMEM, VMEM],
        name="transpose_tokens",
        vmem=16,
    )
    head_weights.first(token_t)
    head_weights.second()

    lanes = heads * PAIR
    blocks = seq // BLOCK
    count = len(head_weights.arrays)
    q, k, v, w, ctx_own, ctx_send, lse = call(
        partial(heads_forward, head_weights.entries, count),
        [shape_of((seq, lanes), BF16)] * 3
        + [shape_of((width, 3 * lanes), BF16)]
        + [shape_of((rows, lanes), BF16)] * 2
        + [shape_of((blocks, 8, BLOCK), F32)],
        [meta, lows, highs, *head_weights.arrays, tokens, other_tokens, pair_bias, seg_row],
        in_specs=[SMEM] * 3 + [ANY] * count + [VMEM] * 4,
        scratch=[
            pltpu.VMEM((2, width, head_weights.shard.shape[1]), BF16),
            pltpu.VMEM((2 * heads, SUMMED, seq), BF16),
            pltpu.VMEM((2 * heads, BLOCK, PAIR), BF16),
            pltpu.VMEM((2 * heads, BLOCK, BLOCK), BF16),
            pltpu.VMEM((seq, 1), jnp.int32),
            pltpu.SemaphoreType.DMA((len(head_weights.entries),)),
        ],
        flops=2 * seq * width * 3 * lanes + 4 * seq * seq * lanes,
        name="heads_forward",
        vmem=VM_HEADS,
    )
    ctx_other = g.swap(ctx_send, "c")

    def by_rows(lanes):
        return pl.BlockSpec((ROW_BLOCK, lanes), lambda i: (i, 0))

    def by_columns(array_rows):
        return pl.BlockSpec((array_rows, ROW_BLOCK), lambda i: (0, i))

    def fixed(array):
        return pl.BlockSpec(array.shape, lambda i: (0,) * len(array.shape))

    ffn = 2 * rows * width * 4 * hidden
    sums_shape = shape_of((16, width), F32)
    weight_sems = pltpu.SemaphoreType.DMA((both.shape[0] * both.shape[1],))
    output, dr1, da, act, du, df_t, low_t, sums, wo = call(
        rows_step,
        [
            shape_of((rows, width), BF16),
            shape_of((rows, width), F32),
            shape_of((rows, width), BF16),
            shape_of((rows, 4 * hidden), BF16),
            shape_of((rows, 4 * hidden), BF16),
            shape_of((width, rows), BF16),
            shape_of((width, rows), BF16),
            sums_shape,
            shape_of((width, lanes), BF16),
        ],
        [meta, both, tokens, vectors, ctx_own, ctx_other, hidden_bias, output_grad],
        in_specs=[SMEM, ANY, by_rows(width), fixed(vectors), by_rows(lanes), by_rows(lanes)]
        + [fixed(hidden_bias), by_rows(width)],
        out_specs=[by_rows(width)] * 3
        + [by_rows(4 * hidden)] * 2
        + [by_columns(width)] * 2
        + [fixed(sums_shape), pl.BlockSpec((width, lanes), lambda i: (0, 0))],
        scratch=[
            pltpu.VMEM((width, width), BF16),
            pltpu.VMEM((4, width, both.shape[3]), BF16),
            pltpu.VMEM((ROW_BLOCK, 4 * hidden), F32),
            weight_sems,
            weight_sems,
        ],
        grid=(rows // ROW_BLOCK,),
        flops=4 * ffn + 2 * rows * width * width,
        name="rows_step",
        vmem=VM_ROWS,
    )
    other_da = g.swap(da, "c")
    tiles = hidden // BLOCK
    left_spec = pl.BlockSpec((width, rows), lambda i: (0, 0))

    def right_specs(places):
        return [pl.BlockSpec((rows, BLOCK), lambda i, t=t: (0, t * tiles + i)) for t in places] * 2

    partner_spec = pl.BlockSpec((2, width, BLOCK), lambda i: (0, 0, i))
    for_partner = call(
        grad_for_partner,
        [shape_of((2, width, hidden), BF16)] * 2,
        [df_t, low_t, act, act, du, du],
        in_specs=[left_spec] * 2 + right_specs((1, 3)),
        out_specs=[partner_spec] * 2,
        grid=(tiles,),
        flops=ffn,
        name="grad_for_partner",
        vmem=VM_PART,
    )
    dctx, delta, out_grad = call(
        heads_back_start,
        [shape_of((seq, lanes), BF16), shape_of((blocks, 8, BLOCK), F32), shape_of((width, lanes), F32)],
        [meta, da, other_da, ctx_own, ctx_send, wo],
        in_specs=[SMEM] + [VMEM] * 5,
        scratch=[pltpu.VMEM((width, rows), BF16)],
        flops=4 * seq * width * lanes,
        name="heads_back_start",
        vmem=VM_START,
    )
    received = [g.swap(a, "c") for a in after(for_partner, other_da)]
    leaving = Scatter.shapes(g, shard, hidden, weights=2)
    ffn_grad = Scatter(
        g,
        shard,
        call(
            partial(grad_for_chip, g.nz),
            leaving,
            [meta, after(df_t, dctx), low_t, act, act, du, du, *received],
            in_specs=[SMEM] + [left_spec] * 2 + right_specs((0, 2)) + [partner_spec] * 2,
            out_specs=[
                pl.BlockSpec((*a.shape[:-1], BLOCK), lambda i, n=len(a.shape) - 1: (0,) * n + (i,)) for a in leaving
            ],
            scratch=[pltpu.VMEM((2, 2, leaving[0].shape[-2], BLOCK), BF16)],
            grid=(tiles,),
            flops=ffn,
            name="grad_for_chip",
            vmem=VM_GRAD,
        ),
    )

    def attend_back(first, last, dctx, *dq):
        return call(
            partial(attention_backward, first, last, len(dq)),
            [shape_of((heads, PAIR, seq), F32), shape_of(((last - first) * BLOCK, 2 * lanes), BF16)],
            [meta, lows, highs, q, k, v, dctx, lse, delta, seg_row, *dq],
            in_specs=[SMEM] * 3 + [VMEM] * (7 + len(dq)),
            scratch=[pltpu.VMEM((2 * heads, BLOCK, PAIR), F32)] * 2 + [pltpu.VMEM((2 * heads, BLOCK, BLOCK), BF16)] * 2,
            flops=5 * seq * seq * lanes,
            name="attention_backward",
            vmem=VM_BACK,
        )

    dq_t, dkv_one = attend_back(0, blocks // 2, after(dctx, ffn_grad.arrays))
    ffn_away = ffn_grad.first(dkv_one)
    dq_t, dkv_two = attend_back(blocks // 2, blocks, after(dctx, ffn_away), dq_t)
    ffn_second = ffn_grad.second(dkv_two)

    *arrays, vector, dqkv = call(
        partial(projection_grad, g.nz),
        Scatter.shapes(g, shard, 2 * lanes, SPARE) + [shape_of((2, 8, width), F32), shape_of((seq, 3 * lanes), BF16)],
        [meta, token_t, out_grad, after(dq_t, ffn_second), dkv_one, dkv_two, sums, g.swap(sums, "c")],
        in_specs=[SMEM] + [VMEM] * 7,
        scratch=[pltpu.VMEM((2, width // 2, 2 * lanes), BF16)],
        flops=2 * seq * width * 3 * lanes,
        name="projection_grad",
        vmem=VM_PROJ,
    )
    head_grad = Scatter(g, shard, arrays, (vector[0], vector[1]))
    ffn_parts = ffn_grad.third(arrays)
    ffn_share = ffn_parts[0] + sum(part.astype(F32) for part in ffn_parts[1:])
    (ig_other,) = call(
        input_grad_other,
        [shape_of((rows, width), BF16)],
        [meta, dqkv, w],
        in_specs=[SMEM] + [VMEM] * 2,
        flops=seq * width * 3 * lanes,
        name="input_grad_other",
        vmem=VM_PROJ,
    )
    head_away = head_grad.first((ffn_share, ig_other))
    ig_arrived = g.swap(after(ig_other, head_away), "c")
    (input_grad,) = call(
        input_grad_own,
        [shape_of((rows, width), F32)],
        [meta, dqkv, w, dr1, ig_arrived],
        in_specs=[SMEM] + [VMEM] * 4,
        flops=seq * width * 3 * lanes,
        name="input_grad_own",
        vmem=VM_PROJ,
    )
    head_grad.second(input_grad)
    down_share, up_share = ffn_share[0], ffn_share[1]
    parts = head_grad.third()
    if regular:
        qkv_share, out_share, vectors_grad, up_bias_share, qv_share = call(
            partial(finish_heads, len(parts) - 2),
            [shape_of((3, shard, local_width), F32), shape_of((shard, local_width), F32), shape_of((6, width), F32)]
            + [shape_of((1, width), F32), shape_of((2, local_width), F32)],
            parts,
            name="finish_heads",
            vmem=SUM_VMEM,
        )
    else:
        shares, summed = parts
        shares = shares.reshape(shard, heads, 4, d).transpose(2, 0, 1, 3).reshape(4, shard, local_width)
        qkv_share, out_share = shares[:3], shares[3]
        vectors_grad, up_bias_share = summed[:6], summed[6:7]
        qv_share = summed[7, : 2 * local_width].reshape(2, local_width)
    qkv_share = qkv_share.transpose(1, 0, 2)
    up_bias_share = up_bias_share.reshape(-1)
    return (output, input_grad, qkv_share, qv_share, out_share, up_share, up_bias_share, down_share, vectors_grad)


def solution(mesh):
    g = Grid(mesh)
    dp, tensor = ("z", "y"), ("x", "c")
    rows = P(dp + tensor, None)
    in_specs = (
        rows,
        P(dp, None),
        P(dp, None, tensor),
        P(None, tensor),
        P(dp, tensor),
        P(),
        P(),
        P(),
        P(dp, tensor),
        P(tensor),
        P(dp, tensor),
        P(),
        P(),
        P(),
        rows,
    )
    out_specs = (
        rows,
        rows,
        P(dp, None, tensor),
        P(None, tensor),
        P(dp, tensor),
        P(dp, tensor),
        P(tensor),
        P(dp, tensor),
        P(),
    )
    return jax.shard_map(partial(local, g), mesh=g.mesh, in_specs=in_specs, out_specs=out_specs, check_vma=False)
```

```python
from functools import partial

import jax
import jax.numpy as jnp
from jax import lax
from jax.experimental import pallas as pl
from jax.experimental.pallas import tpu as pltpu
from jax.sharding import Mesh
from jax.sharding import PartitionSpec as P

HEAD_DIM = 64
PAIR = 2 * HEAD_DIM
EPSILON = 1e-12
MASKED = -1e30
BLOCK = 256
ROW_BLOCK = 256
F32 = jnp.float32
BF16 = jnp.bfloat16
MIB = 1 << 20
COST = 1


def dot_nn(left, right):
    return jnp.dot(left, right, preferred_element_type=F32)


def dot_nt(left, right):
    return lax.dot_general(left, right, (((1,), (1,)), ((), ())), preferred_element_type=F32)


def call(body, outs, ins, in_specs=None, out_specs=None, scratch=(), grid=(), flops=0, name=None, vmem=60, alias=None):
    moved = sum(a.size * a.dtype.itemsize for a in ins) + sum(o.size * o.dtype.itemsize for o in outs)
    return pl.pallas_call(
        body,
        grid=grid,
        out_shape=outs,
        in_specs=in_specs or [VMEM] * len(ins),
        out_specs=out_specs or [VMEM] * len(outs),
        scratch_shapes=list(scratch),
        compiler_params=pltpu.CompilerParams(vmem_limit_bytes=vmem * MIB),
        cost_estimate=pl.CostEstimate(flops=int(flops) // COST, bytes_accessed=int(moved) // COST, transcendentals=0),
        input_output_aliases=alias or {},
        name=name,
    )(*ins)


ANY = pl.BlockSpec(memory_space=pl.ANY)
SMEM = pl.BlockSpec(memory_space=pltpu.SMEM)
VMEM = pl.BlockSpec(memory_space=pltpu.VMEM)


def shape_of(shape, dtype):
    return jax.ShapeDtypeStruct(shape, dtype)


def after(values, done):
    return lax.optimization_barrier((values, done))[0]


class Grid:
    def __init__(self, mesh):
        n_dp, n_tensor = mesh.devices.shape
        assert n_tensor == 4 and n_dp % 2 == 0
        self.nz = n_dp // 2
        self.n_dp = n_dp
        self.mesh = Mesh(mesh.devices.reshape(self.nz, 2, 2, 2), ("z", "y", "x", "c"))

    def swap(self, array, axis, r=1):
        size = self.nz if axis == "z" else 2
        return lax.ppermute(array, axis, [(i, i ^ r) for i in range(size)])

    def regular(self, rows):
        return rows % 32 == 0 and self.nz & (self.nz - 1) == 0

    def total_dp(self, array):
        if self.nz & (self.nz - 1):
            return lax.psum(array, ("z", "y"))
        array = array + self.swap(array, "y")
        r = 1
        while r < self.nz:
            array = array + self.swap(array, "z", r)
            r *= 2
        return array


class Gather:
    def __init__(self, g, shard):
        self.g, self.shard, self.rows = g, shard, shard.shape[0]
        self.regular = g.regular(self.rows)

    def line(self):
        g, half = self.g, self.rows // 2
        if not self.regular:
            full = lax.all_gather(self.shard, ("z", "y"), axis=0, tiled=True)[None, None]
            self.arrays = [full, g.swap(full, "x")]
            self.entries = [(n, 0, 0, n, 0, 0, full.shape[2]) for n in range(2)]
            return self.arrays
        near = [self.shard] + [g.swap(self.shard, "z", r) for r in range(1, g.nz)]
        self.lines = [jnp.stack([part[:half] for part in near]), jnp.stack([part[half:] for part in near])]
        return self.lines

    def wait(self, step, done):
        if self.regular:
            setattr(self, step, after(getattr(self, step), done))

    def first(self, done=()):
        if not self.regular:
            return self.arrays
        arrived = after([self.g.swap(line, axis) for line, axis in zip(self.lines, "xy")], done)
        self.twos = [jnp.stack([line, other]) for line, other in zip(self.lines, arrived)]
        return arrived

    def second(self):
        if not self.regular:
            return self.arrays
        half = self.rows // 2
        self.arrays, self.entries = [], []
        for number, axis in enumerate("xy"):
            two = self.twos[number]
            four = self.g.swap(two, "yx"[number])
            for index, array in ((0, two), (1, four)):
                for i in range(2):
                    rx, ry = (i, index) if axis == "x" else (index, i)
                    for k in range(self.g.nz):
                        self.entries.append((len(self.arrays), i, k, rx, k * 2 + ry, number * half, half))
                self.arrays.append(array)
        return self.arrays


def load_pieces(entries, refs, index, target, sems, lanes):
    slots = 1 + max(entry[4] for entry in entries)
    copies = []
    for number, (a, i, k, place, slot, first, size) in enumerate(entries):
        row = pl.multiple_of((slot ^ index) * (target.shape[1] // slots) + first, 16)
        copies.append(
            pltpu.make_async_copy(refs[a].at[i, k, :, lanes], target.at[place, pl.ds(row, size)], sems.at[number])
        )
    for copy in copies:
        copy.start()
    for copy in copies:
        copy.wait()


def gather_everywhere(g, shard):
    if g.regular(shard.shape[0]):
        full = lax.all_gather(shard, ("z", "y", "x", "c"), axis=0)
        return full.reshape(g.n_dp, 4, *shard.shape)
    full = lax.all_gather(shard, ("z", "y"), axis=0, tiled=True)
    return lax.all_gather(full, ("x", "c"), axis=0)[None]


def everywhere_copies(source, me, target, sems, lanes):
    blocks, places, rows = source.shape[:3]
    return [
        pltpu.make_async_copy(
            source.at[block, t, :, lanes],
            target.at[t ^ me, pl.ds(block * rows, rows), lanes],
            sems.at[block * places + t],
        )
        for block in range(blocks)
        for t in range(places)
    ]


SPARE = 16


class Scatter:
    def __init__(self, g, rows, arrays, vector=None):
        self.g, self.rows = g, rows
        self.regular = g.regular(rows)
        self.arrays = arrays
        self.vector = vector

    @staticmethod
    def shapes(g, rows, lanes, spare=0, weights=None):
        lead = () if weights is None else (weights,)
        if not g.regular(rows):
            return [shape_of((*lead, 2, rows * g.n_dp, lanes), BF16)]
        size = 2 * g.nz * rows // 2
        block = shape_of((*lead, size, lanes), BF16)
        return [block, shape_of((*lead, size + spare, lanes), BF16), block, block]

    def first(self, done=()):
        g = self.g
        if not self.regular:
            (whole,) = self.arrays
            both = whole[..., 0, :, :].astype(F32) + g.swap(whole[..., 1, :, :], "x").astype(F32)
            self.sum = lax.psum_scatter(both, ("z", "y"), scatter_dimension=both.ndim - 2, tiled=True)
            if self.vector is not None:
                self.vector = lax.psum(self.vector[0] + g.swap(self.vector[1], "x"), ("z", "y"))
            return [self.sum]
        keep_x, send_x, keep_y, send_y = self.arrays
        self.got = after([g.swap(send_x, "x"), g.swap(send_y, "y")], done)
        lead, half, lanes = keep_x.shape[:-2], keep_x.shape[-2] // 2, keep_x.shape[-1]
        outs, ins = [shape_of((*lead, half, lanes), BF16)] * 2, [keep_x, self.got[0], keep_y, self.got[1]]
        if self.vector is not None:
            outs = [shape_of((half + SPARE, lanes), BF16), outs[1], shape_of((SPARE // 2, lanes), F32)]
            ins.append(self.vector[0])
        self.away = call(sum_away, outs, ins, name="sum_away", vmem=SUM_VMEM)
        return self.away

    def second(self, done=()):
        if not self.regular:
            return [self.sum]
        g = self.g
        seconds = after([g.swap(self.away[0], "y"), g.swap(self.away[1], "x")], done)
        lead, lanes = self.away[1].shape[:-2], self.away[1].shape[-1]
        outs = [shape_of((*lead, self.rows, lanes), F32)]
        ins = [self.arrays[0], self.got[0], seconds[0], self.arrays[2], self.got[1], seconds[1]]
        far_rows = self.rows
        if self.vector is not None:
            outs.append(shape_of((SPARE // 2, lanes), F32))
            ins.append(self.away[2])
            far_rows += SPARE
        outs += [shape_of((*lead, far_rows, lanes), BF16)] * (g.nz - 1)
        self.line = call(partial(sum_line, g.nz), outs, ins, name="sum_line", vmem=SUM_VMEM)
        return self.line

    def third(self, done=()):
        if not self.regular:
            return [self.sum] if self.vector is None else [self.sum, self.vector]
        count = 1 if self.vector is None else 2
        arrived = [self.g.swap(far, "z", r + 1) for r, far in enumerate(self.line[count:])]
        return [*self.line[:count], *after(arrived, done)]


SUM_VMEM = 12
VM_HEADS = 60
VM_ROWS = 60
VM_GRAD = 28
VM_PART = 60
VM_START = 60
VM_BACK = 36
VM_PROJ = 36


def split_in_two(value):
    high = value.astype(BF16)
    return jnp.concatenate([high, (value - high.astype(F32)).astype(BF16)], axis=0)


def join_two(ref):
    spare = ref[ref.shape[0] - SPARE :, :].astype(F32)
    return spare[: SPARE // 2] + spare[SPARE // 2 :]


def sum_away(keep_x, got_x, keep_y, got_y, *refs):
    half = keep_x.shape[-2] // 2
    if len(refs) == 4:
        vector, out_x, out_y, vector_out = refs
        total = vector[...] + join_two(got_x)
        vector_out[...] = total
        out_x[half:, :] = split_in_two(total)
    else:
        out_x, out_y = refs
    for keep, got, out in ((keep_x, got_x, out_x), (keep_y, got_y, out_y)):
        away = keep[..., half:, :].astype(F32) + got[..., half : 2 * half, :].astype(F32)
        out[..., :half, :] = away.astype(BF16)


def sum_line(nz, keep_x, got_x, last_x, keep_y, got_y, last_y, *refs):
    size = keep_x.shape[-2] // (2 * nz)
    if len(refs) > nz:
        vector, near, vector_out, *far = refs
        total = vector[...] + join_two(last_x)
        vector_out[...] = total
        parts = split_in_two(total)
        for out in far:
            out[2 * size :, :] = parts
    else:
        near, *far = refs
    for n, (keep, got, last) in enumerate(((keep_x, got_x, last_x), (keep_y, got_y, last_y))):
        for r in range(nz):
            at = slice(r * size, (r + 1) * size)
            total = keep[..., at, :].astype(F32) + got[..., at, :].astype(F32) + last[..., at, :].astype(F32)
            out = far[r - 1] if r else near
            out[..., n * size : (n + 1) * size, :] = total.astype(out.dtype)


def store_blocks(value, outs, stage, place, index, nz):
    value = value.astype(BF16)
    if len(outs) == 1:
        outs[0][place] = value
        return
    by_x = outs[place]
    half = stage.shape[1] // (2 * nz)
    for block in range(value.shape[0] // (2 * half)):
        slot = block ^ index
        ry, rz = lax.rem(slot, 2), lax.div(slot, 2)
        row = pl.multiple_of((ry * nz + rz) * half, 16)
        by_x[pl.ds(row, half), :] = value[2 * block * half : (2 * block + 1) * half]
        row = pl.multiple_of((place * nz + rz) * half, 16)
        stage[ry, pl.ds(row, half), :] = value[(2 * block + 1) * half : (2 * block + 2) * half]
    if place == 1:
        outs[2][...] = stage[0]
        outs[3][...] = stage[1]


SUMMED = HEAD_DIM + 16


def heads_forward(entries, count, meta, lows, highs, *refs):
    pieces = refs[:count]
    own, other, bias, seg_row = refs[count : count + 4]
    q, k, v, w_out, ctx_own, ctx_other, lse = refs[count + 4 : count + 11]
    weights, v_t, q_masked, powers, seg_col, sems = refs[count + 11 :]
    rows = own.shape[0]
    core = meta[0]
    load_pieces(entries, pieces, meta[1], weights, sems, slice(None))
    d = HEAD_DIM
    width = q.shape[1]
    pairs = width // PAIR
    for j in range(pairs):
        for kind in range(3):
            at = slice((3 * j + kind) * d, (3 * j + kind + 1) * d)
            pair = jnp.concatenate([weights[0][:, at], weights[1][:, at]], axis=1)
            w_out[:, kind * width + j * PAIR : kind * width + (j + 1) * PAIR] = pair
    ones = jnp.ones((SUMMED - d, BLOCK), BF16)
    for source, base in ((own, core * rows), (other, (1 - core) * rows)):

        def project(n, carry):
            at = pl.ds(pl.multiple_of(base + n * BLOCK, BLOCK), BLOCK)
            block = source[pl.ds(pl.multiple_of(n * BLOCK, BLOCK), BLOCK), :]
            all_three = dot_nn(block, w_out[...])
            query = (all_three[:, :width] + bias[0:1, :]).astype(BF16)
            q[at, :] = (query.astype(F32) * d**-0.5).astype(BF16)
            k[at, :] = all_three[:, width : 2 * width].astype(BF16)
            values = (all_three[:, 2 * width :] + bias[1:2, :]).astype(BF16)
            v[at, :] = values
            for p in range(pairs):
                columns = values[:, p * PAIR : (p + 1) * PAIR].T
                for h in range(2):
                    v_t[2 * p + h, :d, at] = columns[h * d : (h + 1) * d]
                    v_t[2 * p + h, d:, at] = ones
            return carry

        lax.fori_loop(0, rows // BLOCK, project, 0)
    left = lax.broadcasted_iota(jnp.int32, (BLOCK, PAIR), 1) < d
    half = rows // BLOCK
    for b in range(2 * half):
        seg_col[b * BLOCK : (b + 1) * BLOCK, :] = column_of(seg_row[b])

    def query_block(i, carry):
        at = pl.ds(pl.multiple_of(i * BLOCK, BLOCK), BLOCK)
        seg_q = seg_row[i]
        for p in range(pairs):
            query = q[at, p * PAIR : (p + 1) * PAIR].astype(F32)
            q_masked[2 * p] = jnp.where(left, query, 0.0).astype(BF16)
            q_masked[2 * p + 1] = jnp.where(left, 0.0, query).astype(BF16)

        def key_block(b, carry):
            tops, sums = carry
            rows = pl.ds(pl.multiple_of(b * BLOCK, BLOCK), BLOCK)
            same = seg_col[rows, :] == seg_q
            new_tops, new_sums = [], []
            for h in range(2 * pairs):
                s = dot_nt(k[rows, (h // 2) * PAIR : (h // 2 + 1) * PAIR], q_masked[h])
                s = jnp.where(same, s, MASKED)
                top = jnp.maximum(tops[h], jnp.max(s, axis=0, keepdims=True))
                powers[h] = jnp.exp(s - top).astype(BF16)
                new_tops.append(top)
            for h in range(2 * pairs):
                scale = jnp.exp(tops[h] - new_tops[h])
                new_sums.append(sums[h] * scale + dot_nn(v_t[h, :, rows], powers[h]))
            return tuple(new_tops), tuple(new_sums)

        first_top = jnp.full((1, BLOCK), MASKED, F32)
        first_sum = jnp.zeros((SUMMED, BLOCK), F32)
        tops, sums = lax.fori_loop(
            lows[i], highs[i], key_block, ((first_top,) * (2 * pairs), (first_sum,) * (2 * pairs))
        )
        for p in range(pairs):
            parts = []
            for h in (2 * p, 2 * p + 1):
                total = sums[h][d : d + 1, :]
                lse[i, h : h + 1, :] = tops[h] + jnp.log(total)
                parts.append(sums[h][:d, :] / total)
            ctx = jnp.concatenate(parts, axis=0).T.astype(BF16)
            lanes = slice(p * PAIR, (p + 1) * PAIR)
            own_half = lax.div(i, half) == core
            within = pl.ds(pl.multiple_of(lax.rem(i, half) * BLOCK, BLOCK), BLOCK)

            @pl.when(own_half)
            def _():
                ctx_own[within, lanes] = ctx

            @pl.when(jnp.logical_not(own_half))
            def _():
                ctx_other[within, lanes] = ctx

        return carry

    lax.fori_loop(0, 2 * half, query_block, 0)


def heads_back_start(meta, da_own, da_other, ctx_own, ctx_other, wo, dctx, delta, out_grad, left_t):
    rows = da_own.shape[0]
    core = meta[0]
    d = HEAD_DIM
    pairs = ctx_own.shape[1] // PAIR
    for source, values, base in ((da_own, ctx_own, core * rows), (da_other, ctx_other, (1 - core) * rows)):

        def context_grad(n, carry):
            here = pl.ds(pl.multiple_of(n * BLOCK, BLOCK), BLOCK)
            at = pl.ds(pl.multiple_of(base + n * BLOCK, BLOCK), BLOCK)
            block = base // BLOCK + n
            left_t[:, here] = source[here, :].T
            grads = dot_nn(source[here, :], wo[...]).astype(BF16)
            dctx[at, :] = grads
            for p in range(pairs):
                lanes = slice(p * PAIR, (p + 1) * PAIR)
                prod = (grads[:, lanes].astype(F32) * values[here, lanes].astype(F32)).T
                delta[block, 2 * p : 2 * p + 1, :] = jnp.sum(prod[:d], axis=0, keepdims=True)
                delta[block, 2 * p + 1 : 2 * p + 2, :] = jnp.sum(prod[d:], axis=0, keepdims=True)
            return carry

        lax.fori_loop(0, rows // BLOCK, context_grad, 0)
        part = dot_nn(left_t[...], values[...])
        if source is da_own:
            out_grad[...] = part
        else:
            out_grad[...] += part


def attention_backward(first, last, given, meta, lows, highs, q, k, v, dctx, lse, delta, seg_row, *refs):
    dq_in, (dq_t, dkv, dk_sum, dv_sum, powers, slopes) = refs[:given], refs[given:]
    d = HEAD_DIM
    width = q.shape[1]
    pairs = width // PAIR
    left = lax.broadcasted_iota(jnp.int32, (BLOCK, PAIR), 1) < d
    dq_t[...] = dq_in[0][...] if given else jnp.zeros_like(dq_t)

    def key_block(b, carry):
        at = pl.ds(pl.multiple_of(b * BLOCK, BLOCK), BLOCK)
        seg_k = column_of(seg_row[b])
        dk_sum[...] = jnp.zeros_like(dk_sum)
        dv_sum[...] = jnp.zeros_like(dv_sum)
        keys, values, keys_t = [], [], []
        for p in range(pairs):
            lanes = slice(p * PAIR, (p + 1) * PAIR)
            key, value = k[at, lanes].astype(F32), v[at, lanes].astype(F32)
            keys += [jnp.where(left, key, 0.0).astype(BF16), jnp.where(left, 0.0, key).astype(BF16)]
            values += [jnp.where(left, value, 0.0).astype(BF16), jnp.where(left, 0.0, value).astype(BF16)]
            keys_t.append(k[at, lanes].T)

        def query_block(i, carry):
            rows_q = pl.ds(pl.multiple_of(i * BLOCK, BLOCK), BLOCK)
            same = seg_k == seg_row[i]
            for h in range(2 * pairs):
                lanes = slice((h // 2) * PAIR, (h // 2 + 1) * PAIR)
                s = jnp.where(same, dot_nt(keys[h], q[rows_q, lanes]), MASKED)
                p = jnp.exp(s - lse[i, h : h + 1, :])
                dp = dot_nt(values[h], dctx[rows_q, lanes])
                powers[h] = p.astype(BF16)
                slopes[h] = (p * (dp - delta[i, h : h + 1, :])).astype(BF16)
            for h in range(2 * pairs):
                p, half = h // 2, slice((h % 2) * d, (h % 2 + 1) * d)
                lanes = slice(p * PAIR, (p + 1) * PAIR)
                dv_sum[h] += dot_nn(powers[h], dctx[rows_q, lanes])
                dk_sum[h] += dot_nn(slopes[h], q[rows_q, lanes])
                dq_t[p, half, rows_q] += dot_nn(keys_t[p][half, :], slopes[h])
            return carry

        lax.fori_loop(lows[b], highs[b], query_block, 0)
        for p in range(pairs):
            for n, total in ((1, dk_sum), (2, dv_sum)):
                value = jnp.where(left, total[2 * p], total[2 * p + 1])
                here = pl.ds(pl.multiple_of((b - first) * BLOCK, BLOCK), BLOCK)
                dkv[here, (n - 1) * width + p * PAIR : (n - 1) * width + (p + 1) * PAIR] = value.astype(BF16)
        return carry

    lax.fori_loop(first, last, key_block, 0)


def column_of(row):
    return jnp.broadcast_to(row.astype(F32), (128, BLOCK)).T[:, 0:1].astype(jnp.int32)


def transpose_tokens(meta, own, other, out):
    rows = own.shape[0]
    for base, source in ((meta[0] * rows, own), ((1 - meta[0]) * rows, other)):
        for r in range(0, rows, BLOCK):
            out[:, pl.ds(pl.multiple_of(base + r, BLOCK), BLOCK)] = source[r : r + BLOCK, :].T


def projection_grad(nz, meta, token_t, out_grad, dq_t, dkv_one, dkv_two, sums_own, sums_other, *refs):
    outs, dqkv, stage = refs[:-2], refs[-2], refs[-1]
    d = HEAD_DIM
    seq = token_t.shape[1]
    width = out_grad.shape[1]

    def join(n, total):
        at = pl.ds(pl.multiple_of(n * BLOCK, BLOCK), BLOCK)
        for p in range(width // PAIR):
            dqkv[at, p * PAIR : (p + 1) * PAIR] = (dq_t[p, :, at].T * d**-0.5).astype(BF16)
        return total + column_sum(dqkv[at, :width].astype(F32))

    dqkv[: seq // 2, width:] = dkv_one[...]
    dqkv[seq // 2 :, width:] = dkv_two[...]
    q_sum = lax.fori_loop(0, seq // BLOCK, join, jnp.zeros((1, width), F32))
    v_sum = column_sum(dkv_one[:, width:].astype(F32)) + column_sum(dkv_two[:, width:].astype(F32))
    full = dot_nn(token_t[...], dqkv[...])
    vectors = []
    for place in range(2):
        lanes, biases = [], []
        for j in range(width // PAIR):
            at = j * PAIR + place * d
            lanes += [full[:, n * width + at : n * width + at + d] for n in range(3)] + [out_grad[:, at : at + d]]
        store_blocks(jnp.concatenate(lanes, axis=1), outs[:-1], stage, place, meta[1], nz)
        for total in (q_sum, v_sum):
            biases += [total[:, j * PAIR + place * d : j * PAIR + (place + 1) * d] for j in range(width // PAIR)]
        biases.append(jnp.zeros((1, sums_own.shape[1] - len(biases) * d), F32))
        hidden = sums_own[8 + 2 * place : 9 + 2 * place, :] + sums_other[9 + 2 * place : 10 + 2 * place, :]
        vectors.append(jnp.concatenate([sums_own[:6, :] + sums_other[:6, :], hidden, jnp.concatenate(biases, axis=1)], axis=0))
    outs[-1][0] = vectors[0]
    outs[-1][1] = vectors[1]
    if len(outs) > 2:
        outs[1][outs[0].shape[0] :, :] = split_in_two(vectors[1])


def input_grad_other(meta, dqkv, w, out):
    rows = out.shape[0]
    base = (1 - meta[0]) * rows
    for r in range(0, rows, BLOCK):
        at = pl.ds(pl.multiple_of(base + r, BLOCK), BLOCK)
        out[r : r + BLOCK, :] = dot_nt(dqkv[at, :], w[...]).astype(BF16)


def input_grad_own(meta, dqkv, w, dr1, arrived, out):
    rows = out.shape[0]
    base = meta[0] * rows
    for r in range(0, rows, BLOCK):
        at = pl.ds(pl.multiple_of(base + r, BLOCK), BLOCK)
        here = slice(r, r + BLOCK)
        out[here, :] = dot_nt(dqkv[at, :], w[...]) + dr1[here, :] + arrived[here, :].astype(F32)


def finish_heads(count, near, vector, *refs):
    arrived, (qkv_out, out_out, six_out, hidden_out, head_out) = refs[:count], refs[count:]
    total, sums = near[...], vector[...]
    rows = total.shape[0]
    for part in arrived:
        total = total + part[:rows, :].astype(F32)
        sums = sums + join_two(part)
    d = HEAD_DIM
    heads = total.shape[1] // (4 * d)
    for kind in range(4):
        value = jnp.concatenate([total[:, (4 * j + kind) * d : (4 * j + kind + 1) * d] for j in range(heads)], axis=1)
        if kind == 3:
            out_out[...] = value
        else:
            qkv_out[kind] = value
    lanes = heads * d
    six_out[...] = sums[:6]
    hidden_out[...] = sums[6:7]
    head_out[0:1, :] = sums[7:8, :lanes]
    head_out[1:2, :] = sums[7:8, lanes : 2 * lanes]


def normalize(values):
    center = jnp.mean(values, axis=-1, keepdims=True)
    offset = values - center
    inverse = lax.rsqrt(jnp.mean(offset * offset, axis=-1, keepdims=True) + EPSILON)
    return offset * inverse, inverse


def normalize_back(incoming, normed, inverse, gain):
    weighted = incoming * gain
    centered = weighted - jnp.mean(weighted, axis=-1, keepdims=True)
    centered = centered - normed * jnp.mean(weighted * normed, axis=-1, keepdims=True)
    return centered * inverse


def column_sum(values):
    return jnp.sum(values, axis=0, keepdims=True)


def rows_step(
    meta, everywhere, tokens, vectors, ctx_own, ctx_other, bias, out_grad,
    output, dr1_out, da_out, act_out, du_out, df_t, low_t, sums, wo_own,
    w_out, w_all, slope, sems_out, sems,
):
    hidden = tokens.shape[1]
    half = ctx_own.shape[1]
    copies_out = everywhere_copies(everywhere, meta[2], w_all, sems_out, slice(2 * hidden, None))
    copies = everywhere_copies(everywhere, meta[2], w_all, sems, slice(0, 2 * hidden))
    w_up = w_all.at[:, :, :hidden]
    w_down = w_all.at[:, :, hidden : 2 * hidden]
    start = pl.program_id(0) == 0

    @pl.when(start)
    def _():
        for copy in copies_out + copies:
            copy.start()
        for copy in copies_out:
            copy.wait()
        d = HEAD_DIM
        for core in range(2):
            for j in range(half // PAIR):
                first = 2 * hidden + j * d
                pair = [w_all[2 * place + core, :, first : first + d] for place in range(2)]
                at = core * half + j * PAIR
                w_out[:, at : at + PAIR] = jnp.concatenate(pair, axis=1)
        wo_own[...] = w_out[:, :half]
        sums[...] = jnp.zeros_like(sums)

    out_bias, gain_one, shift_one, down_bias, gain_two, shift_two = (vectors[n : n + 1, :] for n in range(6))
    mixed = dot_nt(jnp.concatenate([ctx_own[...], ctx_other[...]], axis=1), w_out[...])
    normed_one, inverse_one = normalize(tokens[...].astype(F32) + mixed + out_bias)
    first = normed_one * gain_one + shift_one
    low = first.astype(BF16)
    low_t[...] = low.T

    @pl.when(start)
    def _():
        for copy in copies:
            copy.wait()

    for t in range(4):
        for n in range(0, hidden, BLOCK):
            at = slice(t * hidden + n, t * hidden + n + BLOCK)
            u = dot_nn(low, w_up[t, :, n : n + BLOCK]) + bias[:, at]
            share = 0.5 + 0.5 * lax.erf(u * 0.5**0.5)
            act_out[:, at] = (u * share).astype(BF16)
            slope[:, at] = share + u * (jnp.exp(-0.5 * u * u) * 0.3989422804014327)

    fed = first + down_bias
    for t in range(4):
        fed = fed + dot_nt(act_out[:, t * hidden : (t + 1) * hidden], w_down[t])
    normed, inverse = normalize(fed)
    output[...] = (normed * gain_two + shift_two).astype(BF16)
    incoming = out_grad[...].astype(F32)
    dr2 = normalize_back(incoming, normed, inverse, gain_two)
    df = dr2.astype(BF16)
    df_t[...] = df.T
    sums[3:4, :] += column_sum(df.astype(F32))
    sums[4:5, :] += column_sum(incoming * normed)
    sums[5:6, :] += column_sum(incoming)
    for t in range(4):
        for n in range(0, hidden, BLOCK):
            at = slice(t * hidden + n, t * hidden + n + BLOCK)
            du = (dot_nn(df, w_down[t, :, n : n + BLOCK]) * slope[:, at]).astype(BF16)
            du_out[:, at] = du
            sums[8 + t : 9 + t, n : n + BLOCK] += column_sum(du.astype(F32))
    incoming = dr2
    for t in range(4):
        incoming = incoming + dot_nt(du_out[:, t * hidden : (t + 1) * hidden], w_up[t])
    dr1 = normalize_back(incoming, normed_one, inverse_one, gain_one)
    dr1_out[...] = dr1
    da = dr1.astype(BF16)
    da_out[...] = da
    sums[0:1, :] += column_sum(da.astype(F32))
    sums[1:2, :] += column_sum(incoming * normed_one)
    sums[2:3, :] += column_sum(incoming)


def grad_for_partner(df_t, low_t, act_one, act_two, du_one, du_two, out_one, out_two):
    for out, act, du in ((out_one, act_one, du_one), (out_two, act_two, du_two)):
        out[0] = dot_nn(df_t[...], act[...]).astype(BF16)
        out[1] = dot_nn(low_t[...], du[...]).astype(BF16)


def grad_for_chip(nz, meta, df_t, low_t, act_one, act_two, du_one, du_two, received_one, received_two, *refs):
    outs, stage = refs[:-1], refs[-1]
    for n, left_t, rights in ((0, df_t, (act_one, act_two)), (1, low_t, (du_one, du_two))):
        for place, received in ((0, received_one), (1, received_two)):
            value = dot_nn(left_t[...], rights[place][...]) + received[n].astype(F32)
            store_blocks(value, [out.at[n] for out in outs], stage.at[n], place, meta[1], nz)


def local(
    g,
    tokens,
    segment_ids,
    qkv_weight,
    qv_bias,
    out_weight,
    out_bias,
    first_gain,
    first_shift,
    up_weight,
    up_bias,
    down_weight,
    down_bias,
    second_gain,
    second_shift,
    output_grad,
):
    rows, width = tokens.shape
    seq = segment_ids.shape[1]
    heads = qkv_weight.shape[2] // HEAD_DIM
    hidden = up_weight.shape[1]
    shard = qkv_weight.shape[0]
    assert seq == 2 * rows and rows % BLOCK == 0 and hidden == width
    d = HEAD_DIM
    local_width = heads * d
    z, y, x, c = (lax.axis_index(name) for name in ("z", "y", "x", "c"))
    regular = g.regular(shard)
    meta = jnp.stack([c, (z * 2 + y) if regular else c * 0, x * 2 + c]).astype(jnp.int32)

    segments = lax.dynamic_index_in_dim(segment_ids, x, 0, keepdims=False)
    blocks = seq // BLOCK
    by_block = segments.reshape(blocks, BLOCK)
    lows = jnp.sum((segments[None, :] < by_block[:, :1]).astype(jnp.int32), axis=1) // BLOCK
    highs = (jnp.sum((segments[None, :] <= by_block[:, -1:]).astype(jnp.int32), axis=1) + BLOCK - 1) // BLOCK
    seg_row = segments.reshape(blocks, 1, BLOCK)

    small = jnp.concatenate([up_bias, qv_bias.reshape(-1)]).reshape(1, -1)
    small = jnp.concatenate([small, g.swap(small, "x")], axis=0)
    small = jnp.stack([small, g.swap(small, "c")], axis=1).reshape(4, -1).astype(F32)
    hidden_bias = small[:, :hidden].reshape(1, 4 * hidden)
    pair_bias = small[:, hidden:].reshape(2, 2, 2, heads, d)[:, 0].transpose(1, 2, 0, 3)
    pair_bias = pair_bias.reshape(2, heads * PAIR)
    vectors = jnp.stack(
        [out_bias, first_gain, first_shift, down_bias, second_gain, second_shift, out_bias, out_bias]
    ).astype(F32)

    parts = []
    for j in range(heads):
        at = slice(j * d, (j + 1) * d)
        parts += [qkv_weight[:, n, at] for n in range(3)]
    parts.append(jnp.zeros((shard, -3 * local_width % 128), BF16))
    head_weights = Gather(g, jnp.concatenate(parts, axis=1))
    rest = jnp.zeros((shard, -local_width % 128), BF16)
    rest = jnp.concatenate([up_weight, after(down_weight, head_weights.shard), out_weight, rest], axis=1)
    both = gather_everywhere(g, rest)
    other_tokens = g.swap(tokens, "c")
    head_weights.line()
    head_weights.wait("lines", small)
    (token_t,) = call(
        transpose_tokens,
        [shape_of((width, seq), BF16)],
        [meta, tokens, other_tokens],
        in_specs=[SMEM, VMEM, VMEM],
        name="transpose_tokens",
        vmem=16,
    )
    head_weights.first(token_t)
    head_weights.second()

    lanes = heads * PAIR
    blocks = seq // BLOCK
    count = len(head_weights.arrays)
    q, k, v, w, ctx_own, ctx_send, lse = call(
        partial(heads_forward, head_weights.entries, count),
        [shape_of((seq, lanes), BF16)] * 3
        + [shape_of((width, 3 * lanes), BF16)]
        + [shape_of((rows, lanes), BF16)] * 2
        + [shape_of((blocks, 8, BLOCK), F32)],
        [meta, lows, highs, *head_weights.arrays, tokens, other_tokens, pair_bias, seg_row],
        in_specs=[SMEM] * 3 + [ANY] * count + [VMEM] * 4,
        scratch=[
            pltpu.VMEM((2, width, head_weights.shard.shape[1]), BF16),
            pltpu.VMEM((2 * heads, SUMMED, seq), BF16),
            pltpu.VMEM((2 * heads, BLOCK, PAIR), BF16),
            pltpu.VMEM((2 * heads, BLOCK, BLOCK), BF16),
            pltpu.VMEM((seq, 1), jnp.int32),
            pltpu.SemaphoreType.DMA((len(head_weights.entries),)),
        ],
        flops=2 * seq * width * 3 * lanes + 4 * seq * seq * lanes,
        name="heads_forward",
        vmem=VM_HEADS,
    )
    ctx_other = g.swap(ctx_send, "c")

    def by_rows(lanes):
        return pl.BlockSpec((ROW_BLOCK, lanes), lambda i: (i, 0))

    def by_columns(array_rows):
        return pl.BlockSpec((array_rows, ROW_BLOCK), lambda i: (0, i))

    def fixed(array):
        return pl.BlockSpec(array.shape, lambda i: (0,) * len(array.shape))

    ffn = 2 * rows * width * 4 * hidden
    sums_shape = shape_of((16, width), F32)
    weight_sems = pltpu.SemaphoreType.DMA((both.shape[0] * both.shape[1],))
    output, dr1, da, act, du, df_t, low_t, sums, wo = call(
        rows_step,
        [
            shape_of((rows, width), BF16),
            shape_of((rows, width), F32),
            shape_of((rows, width), BF16),
            shape_of((rows, 4 * hidden), BF16),
            shape_of((rows, 4 * hidden), BF16),
            shape_of((width, rows), BF16),
            shape_of((width, rows), BF16),
            sums_shape,
            shape_of((width, lanes), BF16),
        ],
        [meta, both, tokens, vectors, ctx_own, ctx_other, hidden_bias, output_grad],
        in_specs=[SMEM, ANY, by_rows(width), fixed(vectors), by_rows(lanes), by_rows(lanes)]
        + [fixed(hidden_bias), by_rows(width)],
        out_specs=[by_rows(width)] * 3
        + [by_rows(4 * hidden)] * 2
        + [by_columns(width)] * 2
        + [fixed(sums_shape), pl.BlockSpec((width, lanes), lambda i: (0, 0))],
        scratch=[
            pltpu.VMEM((width, width), BF16),
            pltpu.VMEM((4, width, both.shape[3]), BF16),
            pltpu.VMEM((ROW_BLOCK, 4 * hidden), F32),
            weight_sems,
            weight_sems,
        ],
        grid=(rows // ROW_BLOCK,),
        flops=4 * ffn + 2 * rows * width * width,
        name="rows_step",
        vmem=VM_ROWS,
    )
    other_da = g.swap(da, "c")
    tiles = hidden // BLOCK
    left_spec = pl.BlockSpec((width, rows), lambda i: (0, 0))

    def right_specs(places):
        return [pl.BlockSpec((rows, BLOCK), lambda i, t=t: (0, t * tiles + i)) for t in places] * 2

    partner_spec = pl.BlockSpec((2, width, BLOCK), lambda i: (0, 0, i))
    for_partner = call(
        grad_for_partner,
        [shape_of((2, width, hidden), BF16)] * 2,
        [df_t, low_t, act, act, du, du],
        in_specs=[left_spec] * 2 + right_specs((1, 3)),
        out_specs=[partner_spec] * 2,
        grid=(tiles,),
        flops=ffn,
        name="grad_for_partner",
        vmem=VM_PART,
    )
    dctx, delta, out_grad = call(
        heads_back_start,
        [shape_of((seq, lanes), BF16), shape_of((blocks, 8, BLOCK), F32), shape_of((width, lanes), F32)],
        [meta, da, other_da, ctx_own, ctx_send, wo],
        in_specs=[SMEM] + [VMEM] * 5,
        scratch=[pltpu.VMEM((width, rows), BF16)],
        flops=4 * seq * width * lanes,
        name="heads_back_start",
        vmem=VM_START,
    )
    received = [g.swap(a, "c") for a in after(for_partner, other_da)]
    leaving = Scatter.shapes(g, shard, hidden, weights=2)
    ffn_grad = Scatter(
        g,
        shard,
        call(
            partial(grad_for_chip, g.nz),
            leaving,
            [meta, after(df_t, dctx), low_t, act, act, du, du, *received],
            in_specs=[SMEM] + [left_spec] * 2 + right_specs((0, 2)) + [partner_spec] * 2,
            out_specs=[
                pl.BlockSpec((*a.shape[:-1], BLOCK), lambda i, n=len(a.shape) - 1: (0,) * n + (i,)) for a in leaving
            ],
            scratch=[pltpu.VMEM((2, 2, leaving[0].shape[-2], BLOCK), BF16)],
            grid=(tiles,),
            flops=ffn,
            name="grad_for_chip",
            vmem=VM_GRAD,
        ),
    )

    def attend_back(first, last, dctx, *dq):
        return call(
            partial(attention_backward, first, last, len(dq)),
            [shape_of((heads, PAIR, seq), F32), shape_of(((last - first) * BLOCK, 2 * lanes), BF16)],
            [meta, lows, highs, q, k, v, dctx, lse, delta, seg_row, *dq],
            in_specs=[SMEM] * 3 + [VMEM] * (7 + len(dq)),
            scratch=[pltpu.VMEM((2 * heads, BLOCK, PAIR), F32)] * 2 + [pltpu.VMEM((2 * heads, BLOCK, BLOCK), BF16)] * 2,
            flops=5 * seq * seq * lanes,
            name="attention_backward",
            vmem=VM_BACK,
        )

    dq_t, dkv_one = attend_back(0, blocks // 2, after(dctx, ffn_grad.arrays))
    ffn_away = ffn_grad.first(dkv_one)
    dq_t, dkv_two = attend_back(blocks // 2, blocks, after(dctx, ffn_away), dq_t)
    ffn_second = ffn_grad.second(dkv_two)

    *arrays, vector, dqkv = call(
        partial(projection_grad, g.nz),
        Scatter.shapes(g, shard, 2 * lanes, SPARE) + [shape_of((2, 8, width), F32), shape_of((seq, 3 * lanes), BF16)],
        [meta, token_t, out_grad, after(dq_t, ffn_second), dkv_one, dkv_two, sums, g.swap(sums, "c")],
        in_specs=[SMEM] + [VMEM] * 7,
        scratch=[pltpu.VMEM((2, width // 2, 2 * lanes), BF16)],
        flops=2 * seq * width * 3 * lanes,
        name="projection_grad",
        vmem=VM_PROJ,
    )
    head_grad = Scatter(g, shard, arrays, (vector[0], vector[1]))
    ffn_parts = ffn_grad.third(arrays)
    ffn_share = ffn_parts[0] + sum(part.astype(F32) for part in ffn_parts[1:])
    (ig_other,) = call(
        input_grad_other,
        [shape_of((rows, width), BF16)],
        [meta, dqkv, w],
        in_specs=[SMEM] + [VMEM] * 2,
        flops=seq * width * 3 * lanes,
        name="input_grad_other",
        vmem=VM_PROJ,
    )
    head_away = head_grad.first((ffn_share, ig_other))
    ig_arrived = g.swap(after(ig_other, head_away), "c")
    (input_grad,) = call(
        input_grad_own,
        [shape_of((rows, width), F32)],
        [meta, dqkv, w, dr1, ig_arrived],
        in_specs=[SMEM] + [VMEM] * 4,
        flops=seq * width * 3 * lanes,
        name="input_grad_own",
        vmem=VM_PROJ,
    )
    head_grad.second(input_grad)
    down_share, up_share = ffn_share[0], ffn_share[1]
    parts = head_grad.third()
    if regular:
        qkv_share, out_share, vectors_grad, up_bias_share, qv_share = call(
            partial(finish_heads, len(parts) - 2),
            [shape_of((3, shard, local_width), F32), shape_of((shard, local_width), F32), shape_of((6, width), F32)]
            + [shape_of((1, width), F32), shape_of((2, local_width), F32)],
            parts,
            name="finish_heads",
            vmem=SUM_VMEM,
        )
    else:
        shares, summed = parts
        shares = shares.reshape(shard, heads, 4, d).transpose(2, 0, 1, 3).reshape(4, shard, local_width)
        qkv_share, out_share = shares[:3], shares[3]
        vectors_grad, up_bias_share = summed[:6], summed[6:7]
        qv_share = summed[7, : 2 * local_width].reshape(2, local_width)
    qkv_share = qkv_share.transpose(1, 0, 2)
    up_bias_share = up_bias_share.reshape(-1)
    return (output, input_grad, qkv_share, qv_share, out_share, up_share, up_bias_share, down_share, vectors_grad)


def solution(mesh):
    g = Grid(mesh)
    dp, tensor = ("z", "y"), ("x", "c")
    rows = P(dp + tensor, None)
    in_specs = (
        rows,
        P(dp, None),
        P(dp, None, tensor),
        P(None, tensor),
        P(dp, tensor),
        P(),
        P(),
        P(),
        P(dp, tensor),
        P(tensor),
        P(dp, tensor),
        P(),
        P(),
        P(),
        rows,
    )
    out_specs = (
        rows,
        rows,
        P(dp, None, tensor),
        P(None, tensor),
        P(dp, tensor),
        P(dp, tensor),
        P(tensor),
        P(dp, tensor),
        P(),
    )
    return jax.shard_map(partial(local, g), mesh=g.mesh, in_specs=in_specs, out_specs=out_specs, check_vma=False)
```
